128 devices in a mesh: row: 8 (over y, core), col: 16 (over x, z).
Axes of the slice: x: 4, y: 4, z: 4, core: 2. Of those that a mesh axis runs over, the one named last changes fastest.
Arguments:
- object_field: float32 [2, 1024, 2048], P(None, 'row', 'col'), may hold values from -4 to 4
- probe_modes: float32 [8, 2, 128, 128], replicated, may hold values from -1.5 to 1.5
- coefficients: float32 [8, 16, 32, 8], P('row', 'col'), may hold values from -4 to 4
- offsets: int32 [8, 16, 32, 2], P('row', 'col'), may hold values from 0 to 128
- counts: int32 [8, 16], P('row', 'col'), may hold values from 16 to 32
- measured: int32 [8, 16, 32, 128, 128], P('row', 'col'), may hold values from 0 to 4095
Outputs:
- object_out: float32 [2, 1024, 2048], P(None, 'row', 'col')
- modes_out: float32 [8, 2, 128, 128], replicated
- coefficients_out: float32 [8, 16, 32, 8], P('row', 'col')
The draws below stay inside these ranges and needn't reach their ends.
All inputs are finite; a program needn't handle non-finite values.
Results may differ from the reference program's by a relative error of at most 0.0003.
Values sent between devices are 32-bit elements; how exact they have to be, the bound alone decides.
No kernel may reach another device: no remote copies, remote signals or barrier semaphores. Data moves between devices by JAX's collectives and lax.ppermute only.
A program may use at most 128 MiB of HBM per device.

```python
import jax
import jax.numpy as jnp
from jax import lax

PS = 128
MODES = 8
TILE = 128
PMAX = 32
ITERS = 2
OBJ_ROWS = 1024
OBJ_COLS = 2048
N_ROW = 8
N_COL = 16


def draw_measured(key, part):
    ceilings = jax.random.randint(jax.random.fold_in(key, 11), (N_ROW, N_COL, 1, 1, 1), 512, 4097)
    return jax.random.randint(jax.random.fold_in(key, 12), (N_ROW, N_COL, PMAX, PS, PS), 0, ceilings).astype(jnp.int32)


def place_ends(drawn, own_key, least, largest):
    shape = drawn.shape
    spot = [jax.random.randint(jax.random.fold_in(own_key, axis), (), 0, shape[axis]) for axis in range(len(shape))]
    drawn = drawn.at[tuple(spot)].set(least)
    longest = shape.index(max(shape))
    spot[longest] = (spot[longest] + 1) % shape[longest]
    return drawn.at[tuple(spot)].set(largest)


def levels(key, dims, cuts, smallest, largest):
    level = 1.0
    for position, parts in cuts:
        draws = jax.random.uniform(jax.random.fold_in(jax.random.fold_in(key, 6), position), (parts,), jnp.float32, smallest / len(cuts), largest / len(cuts))
        level = level * jnp.repeat(jnp.exp(draws), dims[position] // parts).reshape((-1,) + (1,) * (len(dims) - 1 - position))
    return level


def gaussian(key, dims, spread, most, shards=(), kind=jnp.bfloat16):
    loudness = levels(key, dims, shards, -0.22, 0.18) if shards else 1.0
    result = jax.random.normal(key, dims, jnp.float32) * spread * loudness
    return jnp.minimum(jnp.maximum(result, -most), most).astype(kind)


def setup_inputs(seed: int = 0) -> dict:
    splits = jax.random.split(jax.random.key(seed), 7)
    return {
        "object_field": gaussian(splits[0], (2, OBJ_ROWS, OBJ_COLS), 0.7, 4.0, ((1, 8), (2, 16)), jnp.float32),
        "probe_modes": gaussian(splits[1], (MODES, 2, PS, PS), 0.25, 1.5, (), jnp.float32),
        "coefficients": gaussian(splits[2], (N_ROW, N_COL, PMAX, MODES), 1.0, 4.0, ((0, 8), (1, 16)), jnp.float32),
        "offsets": place_ends(jax.random.randint(splits[3], (N_ROW, N_COL, PMAX, 2), 0, TILE + 1), jax.random.fold_in(splits[3], 1), 0, TILE).astype(jnp.int32),
        "counts": place_ends(jax.random.randint(splits[4], (N_ROW, N_COL), PMAX // 2, PMAX + 1), jax.random.fold_in(splits[4], 1), PMAX // 2, PMAX).astype(jnp.int32),
        "measured": draw_measured(jax.random.fold_in(splits[6], 71), 0),
    }


amp_floor = 0.5
count_scale = 0.03125
highest = lax.Precision.HIGHEST

def position_update(patches, coef_rows, in_use, photons, probe_modes):
    obj_real = patches[:, 0]
    obj_imag = patches[:, 1]
    probes = jnp.einsum('pk,kcxy->pcxy', coef_rows, probe_modes, precision=highest)
    prb_real = probes[:, 0]
    prb_imag = probes[:, 1]
    psi_real = prb_real * obj_real - prb_imag * obj_imag
    psi_imag = prb_real * obj_imag + prb_imag * obj_real
    far_field = jnp.fft.fft2(psi_real + 1j * psi_imag, norm='ortho')
    amplitude = jnp.sqrt(far_field.real * far_field.real + far_field.imag * far_field.imag)
    target = jnp.sqrt(photons.astype(jnp.float32)) * count_scale
    corrected = far_field * (target / jnp.maximum(amplitude, amp_floor))
    back_field = jnp.fft.ifft2(corrected, norm='ortho')
    gate_grid = in_use[:, None, None]
    diff_real = (back_field.real - psi_real) * gate_grid
    diff_imag = (back_field.imag - psi_imag) * gate_grid
    grad_real = prb_real * diff_real + prb_imag * diff_imag
    grad_imag = prb_real * diff_imag - prb_imag * diff_real
    weight_grid = (prb_real * prb_real + prb_imag * prb_imag) * gate_grid
    cross_real = obj_real * diff_real + obj_imag * diff_imag
    cross_imag = obj_real * diff_imag - obj_imag * diff_real
    obj_power = (obj_real * obj_real + obj_imag * obj_imag) * gate_grid
    used_coef = coef_rows * in_use[:, None]
    moment_real = jnp.einsum('pk,pxy->kxy', used_coef, cross_real, precision=highest)
    moment_imag = jnp.einsum('pk,pxy->kxy', used_coef, cross_imag, precision=highest)
    moment_power = jnp.einsum('pk,pxy->kxy', used_coef * coef_rows, obj_power, precision=highest)
    mode_real = probe_modes[:, 0]
    mode_imag = probe_modes[:, 1]
    numerator = jnp.einsum('pxy,kxy->pk', cross_real, mode_real, precision=highest) + jnp.einsum('pxy,kxy->pk', cross_imag, mode_imag, precision=highest)
    denominator = jnp.einsum('pxy,kxy->pk', obj_power, mode_real * mode_real + mode_imag * mode_imag, precision=highest)
    coef_new = coef_rows + numerator / (denominator + 1.0)
    pieces = jnp.stack([grad_real, grad_imag, weight_grid], axis=1)
    moments = jnp.stack([moment_real, moment_imag, moment_power], axis=0)
    return (pieces, moments, coef_new)

def reference(object_field, probe_modes, coefficients, offsets, counts, measured):
    margin = PS // 2
    tile_count = N_ROW * N_COL
    coef_flat = coefficients.reshape(tile_count, PMAX, MODES)
    anchor_flat = offsets.reshape(tile_count, PMAX, 2)
    count_flat = counts.reshape(tile_count)
    photon_flat = measured.reshape(tile_count, PMAX, PS, PS)
    tile_ids = jnp.arange(tile_count, dtype=jnp.int32)
    for iteration in range(ITERS):
        padded = jnp.pad(object_field, ((0, 0), (margin, margin), (margin, margin)))
        empty_sums = jnp.zeros((3,) + padded.shape[1:], jnp.float32)
        empty_moments = jnp.zeros((3, MODES, PS, PS), jnp.float32)

        def per_tile(running, inputs):
            accumulated, moment_sum = running
            tile_id, coef_rows, anchors, count_here, photons = inputs
            row_anchor = tile_id // N_COL * TILE
            col_anchor = tile_id % N_COL * TILE
            row_index = (anchors[:, 0] + row_anchor).astype(jnp.int32)
            col_index = (anchors[:, 1] + col_anchor).astype(jnp.int32)
            patches = jax.vmap(lambda top_row, left_col: lax.dynamic_slice(padded, (jnp.int32(0), top_row, left_col), (2, PS, PS)))(row_index, col_index)
            in_use = (jnp.arange(PMAX, dtype=jnp.int32) < count_here).astype(jnp.float32)
            pieces, moments, coef_new = position_update(patches, coef_rows, in_use, photons, probe_modes)

            def add_piece(slot_index, totals):
                corner = (jnp.int32(0), row_index[slot_index], col_index[slot_index])
                current = lax.dynamic_slice(totals, corner, (3, PS, PS))
                return lax.dynamic_update_slice(totals, current + pieces[slot_index], corner)
            accumulated = lax.fori_loop(0, PMAX, add_piece, accumulated)
            return ((accumulated, moment_sum + moments), coef_new)
        (accumulated, moment_sum), coef_flat = lax.scan(per_tile, (empty_sums, empty_moments), (tile_ids, coef_flat, anchor_flat, count_flat, photon_flat))
        interior = accumulated[:, margin:margin + OBJ_ROWS, margin:margin + OBJ_COLS]
        object_field = object_field + interior[0:2] / (interior[2:3] + 1.0)
        probe_modes = probe_modes + jnp.stack([moment_sum[0], moment_sum[1]], axis=1) / (moment_sum[2][:, None] + 1.0)
    return (object_field, probe_modes, coef_flat.reshape(coefficients.shape))
```

```python
import functools
import math

import jax
import jax.numpy as jnp
import numpy as np
from jax import lax
from jax.experimental import pallas as pl
from jax.experimental.pallas import tpu as pltpu
from jax.sharding import PartitionSpec as P

PS = 128
MODES = 8
TILE = 128
PMAX = 32
ITERS = 2
EXT = TILE + PS
F32 = jnp.float32
BF16 = jnp.bfloat16
DEVICES = 128


def split(x):
    hi = x.astype(BF16)
    lo = (x - hi.astype(F32)).astype(BF16)
    return hi, lo


def triple(x, axis):
    hi, lo = split(x)
    return jnp.concatenate([hi, lo, hi], axis=axis)


def dft_constants():
    ramp = np.arange(PS)
    angles = (ramp[:, None] * ramp[None, :] % PS) * (2.0 * math.pi / PS)
    cos = np.cos(angles) / math.sqrt(PS)
    sin = -np.sin(angles) / math.sqrt(PS)
    ahead = np.block([[cos, sin], [-sin, cos]])
    back = np.block([[cos, -sin], [sin, cos]])

    def parts(table):
        table = table.astype(np.float32)
        hi = table.astype(jnp.bfloat16)
        lo = (table - hi.astype(np.float32)).astype(jnp.bfloat16)
        return hi, lo

    def tall(table):
        hi, lo = parts(table)
        return np.concatenate([hi, hi, lo], axis=0)

    def wide(table):
        hi, lo = parts(table)
        return np.concatenate([hi, hi, lo], axis=1)

    return tall(ahead), wide(back), wide(ahead), tall(back)


def dot(a, b):
    return jnp.dot(a, b, preferred_element_type=F32)


def patch_kernel(offs, ext, coef, patches, powers, moment, pw):
    lane = lax.broadcasted_iota(jnp.int32, (PS, PS), 1)

    def cut(p, _):
        top = offs[p, 0]
        left = offs[p, 1]
        turn = (PS - left) & (PS - 1)
        inside = lane < PS - left
        total = None
        for c in range(2):
            a = pltpu.roll(ext[c, 0, pl.ds(top, PS), :], turn, 1)
            b = pltpu.roll(ext[c, 1, pl.ds(top, PS), :], turn, 1)
            patch = jnp.where(inside, a, b)
            patches[p, c] = patch
            total = patch * patch if total is None else total + patch * patch
        pw[pl.ds(p, PS, stride=PMAX), :] = total
        return 0

    lax.fori_loop(0, PMAX, cut, 0)
    powers[...] = pw[...]
    square = coef[...] * coef[...]
    hi, lo = split(square.T)
    zero = jnp.zeros_like(hi)
    left = jnp.concatenate(
        [jnp.concatenate([hi, hi], axis=1), jnp.concatenate([lo, zero], axis=1)], axis=0
    )

    def rows(y, _):
        pair = jnp.concatenate(
            [pw[pl.ds(2 * y * PMAX, PMAX), :], pw[pl.ds((2 * y + 1) * PMAX, PMAX), :]], axis=1
        )
        h, l = split(pair)
        out = dot(left, jnp.concatenate([h, l], axis=0))
        out = out[:MODES] + out[MODES:]
        moment[2 * y] = out[:, :PS]
        moment[2 * y + 1] = out[:, PS:]
        return 0

    lax.fori_loop(0, PS // 2, rows, 0, unroll=4)


def wave_kernel(
    offs, patches, photons, modes, coef, ahead_t, back_w, ahead_w, back_t,
    acc, cross_r, cross_i, moment, probe_r, probe_i, field, wave,
):
    step = pl.program_id(0)
    lane = lax.broadcasted_iota(jnp.int32, (PS, PS), 1)

    @pl.when(step == 0)
    def _():
        acc[...] = jnp.zeros_like(acc)
        left = triple(coef[...], 1)

        def rows(y, _):
            m = modes[y]
            h = m.astype(BF16).astype(F32)
            right = jnp.concatenate([h, h, m - h], axis=0).astype(BF16)
            out = dot(left, right)
            start = pl.multiple_of(y * PMAX, PMAX)
            probe_r[pl.ds(start, PMAX), :] = out[:, :PS]
            probe_i[pl.ds(start, PMAX), :] = out[:, PS:]
            return 0

        lax.fori_loop(0, PS, rows, 0, unroll=8)

    for q in range(2):
        p = 2 * step + q
        pr = probe_r[pl.ds(p, PS, stride=PMAX), :]
        pi = probe_i[pl.ds(p, PS, stride=PMAX), :]
        obj_r = patches[q, 0]
        obj_i = patches[q, 1]
        rows = slice(q * PS, (q + 1) * PS)
        wave[rows, :PS] = pr * obj_r - pi * obj_i
        wave[rows, PS:] = pr * obj_i + pi * obj_r

    def regroup(x):
        top = jnp.concatenate([x[:PS, :PS], x[PS:, :PS]], axis=1)
        low = jnp.concatenate([x[:PS, PS:], x[PS:, PS:]], axis=1)
        return jnp.concatenate([top, low], axis=0)

    out = dot(triple(wave[...], 1), ahead_t[...])
    far = dot(back_w[...], triple(regroup(out), 0))
    count = jnp.concatenate([photons[0], photons[1]], axis=1).astype(F32)
    far_r = far[:PS]
    far_i = far[PS:]
    size = jnp.maximum(far_r * far_r + far_i * far_i, 0.25)
    scale = count * lax.rsqrt(jnp.maximum(count * size, 0.0625)) * 0.03125
    fixed = jnp.concatenate([far_r * scale, far_i * scale], axis=0)
    out = dot(ahead_w[...], triple(fixed, 0))
    field[...] = dot(triple(regroup(out), 1), back_t[...]) - wave[...]

    for q in range(2):
        p = 2 * step + q
        top = offs[p, 0]
        left = offs[p, 1]
        turn = left & (PS - 1)
        inside = lane >= left
        rows = slice(q * PS, (q + 1) * PS)
        diff_r = field[rows, :PS]
        diff_i = field[rows, PS:]
        obj_r = patches[q, 0]
        obj_i = patches[q, 1]
        cross_r[pl.ds(p, PS, stride=PMAX), :] = obj_r * diff_r + obj_i * diff_i
        cross_i[pl.ds(p, PS, stride=PMAX), :] = obj_r * diff_i - obj_i * diff_r
        pr = probe_r[pl.ds(p, PS, stride=PMAX), :]
        pi = probe_i[pl.ds(p, PS, stride=PMAX), :]
        pieces = (
            pr * diff_r + pi * diff_i,
            pr * diff_i - pi * diff_r,
            pr * pr + pi * pi,
        )
        for c in range(3):
            turned = pltpu.roll(pieces[c], turn, 1)
            near = jnp.where(inside, turned, 0.0)
            acc[c, 0, pl.ds(top, PS), :] += near
            acc[c, 1, pl.ds(top, PS), :] += turned - near

    @pl.when(step == PMAX // 2 - 1)
    def _():
        hi, lo = split(coef[...].T)
        zero = jnp.zeros_like(hi)
        left = jnp.concatenate(
            [jnp.concatenate([hi, hi], axis=1), jnp.concatenate([lo, zero], axis=1)], axis=0
        )

        def rows(y, _):
            start = pl.multiple_of(y * PMAX, PMAX)
            pair = jnp.concatenate(
                [cross_r[pl.ds(start, PMAX), :], cross_i[pl.ds(start, PMAX), :]], axis=1
            )
            h, l = split(pair)
            out = dot(left, jnp.concatenate([h, l], axis=0))
            moment[y] = out[:MODES] + out[MODES:]
            return 0

        lax.fori_loop(0, PS, rows, 0, unroll=8)


CHUNK = 16


def coef_kernel(cross_r, cross_i, powers, modes, coef, out, num, den):
    step = pl.program_id(0)

    @pl.when(step == 0)
    def _():
        num[...] = jnp.zeros_like(num)
        den[...] = jnp.zeros_like(den)

    dims = (((1,), (1,)), ((), ()))

    def wide_dot(a, b):
        return lax.dot_general(a, b, dims, preferred_element_type=F32)

    top = jnp.zeros((PMAX, MODES), F32)
    low = jnp.zeros((PMAX, MODES), F32)
    for y in range(CHUNK):
        rows = slice(y * PMAX, (y + 1) * PMAX)
        cross = jnp.concatenate([cross_r[rows, :], cross_i[rows, :]], axis=1)
        m = modes[y]
        power = m[:, :PS] * m[:, :PS] + m[:, PS:] * m[:, PS:]
        h, l = split(m)
        top += wide_dot(triple(cross, 1), jnp.concatenate([h, h, l], axis=1))
        h, l = split(power)
        low += wide_dot(triple(powers[rows, :], 1), jnp.concatenate([h, h, l], axis=1))
    num[...] += top
    den[...] += low

    @pl.when(step == PS // CHUNK - 1)
    def _():
        out[...] = coef[...] + num[...] / (den[...] + 1.0)


SMEM = pl.BlockSpec(memory_space=pltpu.SMEM)
VMEM = pl.BlockSpec(memory_space=pltpu.VMEM)


def cut_patches(offs, ext, coef):
    return pl.pallas_call(
        patch_kernel,
        out_shape=(
            jax.ShapeDtypeStruct((PMAX, 2, PS, PS), F32),
            jax.ShapeDtypeStruct((PS * PMAX, PS), F32),
            jax.ShapeDtypeStruct((PS, MODES, PS), F32),
        ),
        in_specs=[SMEM, VMEM, VMEM],
        out_specs=(VMEM, VMEM, VMEM),
        scratch_shapes=[pltpu.VMEM((PS * PMAX, PS), F32)],
        compiler_params=pltpu.CompilerParams(vmem_limit_bytes=24 << 20),
        name="cut",
    )(offs, ext, coef)


def waves(offs, patches, photons, modes, coef, tables):
    whole = lambda *shape: pl.BlockSpec(shape, lambda i: (0,) * len(shape))
    table_specs = [whole(*t.shape) for t in tables]
    return pl.pallas_call(
        wave_kernel,
        grid=(PMAX // 2,),
        out_shape=(
            jax.ShapeDtypeStruct((3, 2, EXT, PS), F32),
            jax.ShapeDtypeStruct((PS * PMAX, PS), F32),
            jax.ShapeDtypeStruct((PS * PMAX, PS), F32),
            jax.ShapeDtypeStruct((PS, MODES, 2 * PS), F32),
        ),
        in_specs=[
            SMEM,
            pl.BlockSpec((2, 2, PS, PS), lambda i: (i, 0, 0, 0)),
            pl.BlockSpec((2, PS, PS), lambda i: (i, 0, 0)),
            whole(PS, MODES, 2 * PS),
            whole(PMAX, MODES),
            *table_specs,
        ],
        out_specs=(
            whole(3, 2, EXT, PS),
            whole(PS * PMAX, PS),
            whole(PS * PMAX, PS),
            whole(PS, MODES, 2 * PS),
        ),
        scratch_shapes=[
            pltpu.VMEM((PS * PMAX, PS), F32),
            pltpu.VMEM((PS * PMAX, PS), F32),
            pltpu.VMEM((2 * PS, 2 * PS), F32),
            pltpu.VMEM((2 * PS, 2 * PS), F32),
        ],
        compiler_params=pltpu.CompilerParams(
            dimension_semantics=("arbitrary",), vmem_limit_bytes=40 << 20
        ),
        name="waves",
    )(offs, patches, photons, modes, coef, *tables)


def new_coefficients(cross_r, cross_i, powers, modes, coef):
    rows = pl.BlockSpec((CHUNK * PMAX, PS), lambda i: (i, 0))
    whole = pl.BlockSpec((PMAX, MODES), lambda i: (0, 0))
    return pl.pallas_call(
        coef_kernel,
        grid=(PS // CHUNK,),
        out_shape=jax.ShapeDtypeStruct((PMAX, MODES), F32),
        in_specs=[
            rows,
            rows,
            rows,
            pl.BlockSpec((CHUNK, MODES, 2 * PS), lambda i: (i, 0, 0)),
            whole,
        ],
        out_specs=whole,
        scratch_shapes=[pltpu.VMEM((PMAX, MODES), F32)] * 2,
        compiler_params=pltpu.CompilerParams(
            dimension_semantics=("arbitrary",), vmem_limit_bytes=16 << 20
        ),
        name="coefs",
    )(cross_r, cross_i, powers, modes, coef)


def swap_sides(low_part, high_part, axis):
    count = lax.axis_size(axis)
    up = [(i, i + 1) for i in range(count - 1)]
    down = [(i + 1, i) for i in range(count - 1)]
    from_below = lax.ppermute(high_part, axis, up)
    from_above = lax.ppermute(low_part, axis, down)
    return from_below, from_above


def extend(block):
    margin = PS // 2
    low, high = swap_sides(block[:, :margin], block[:, -margin:], "row")
    block = jnp.concatenate([low, block, high], axis=1)
    low, high = swap_sides(block[:, :, :margin], block[:, :, -margin:], "col")
    return jnp.concatenate([low, block, high], axis=2)


def fold(acc):
    margin = PS // 2
    full = jnp.concatenate([acc[:, 0], acc[:, 1]], axis=2)
    low, high = swap_sides(full[:, :margin], full[:, -margin:], "row")
    mid = full[:, margin:-margin]
    mid = jnp.concatenate([mid[:, :margin] + low, mid[:, margin:] + high], axis=1)
    low, high = swap_sides(mid[:, :, :margin], mid[:, :, -margin:], "col")
    mid = mid[:, :, margin:-margin]
    return jnp.concatenate([mid[:, :, :margin] + low, mid[:, :, margin:] + high], axis=2)


def shards(object_field, probe_modes, coefficients, offsets, counts, measured):
    tables = tuple(jnp.asarray(t) for t in dft_constants())
    offs = offsets[0, 0]
    photons = measured[0, 0]
    coef = coefficients[0, 0]
    live = (lax.iota(jnp.int32, PMAX) < counts[0, 0]).astype(F32)[:, None]
    me = lax.axis_index("row") * lax.axis_size("col") + lax.axis_index("col")
    modes = probe_modes.transpose(2, 0, 1, 3).reshape(PS, MODES, 2 * PS)
    for iteration in range(ITERS):
        ext = extend(object_field)
        ext = jnp.stack([ext[:, :, :PS], ext[:, :, PS:]], axis=1)
        used = coef * live
        patches, powers, power_moment = cut_patches(offs, ext, used)
        acc, cross_r, cross_i, moment = waves(offs, patches, photons, modes, used, tables)
        sent = jnp.concatenate([moment, power_moment], axis=2)
        got = lax.all_to_all(sent, ("row", "col"), 0, 0, tiled=True)
        total = jnp.sum(got, axis=0)
        power = total[:, 2 * PS:] + 1.0
        mine = lax.dynamic_index_in_dim(modes, me, 0, keepdims=False)
        mine = mine + total[:, : 2 * PS] / jnp.concatenate([power, power], axis=1)
        coef = new_coefficients(cross_r, cross_i, powers, modes, coef)
        copies = jnp.broadcast_to(mine[None], (DEVICES, MODES, 2 * PS))
        modes = lax.all_to_all(copies, ("row", "col"), 0, 0, tiled=True)
        interior = fold(acc)
        object_field = object_field + interior[0:2] / (interior[2:3] + 1.0)
    probe_modes = modes.reshape(PS, MODES, 2, PS).transpose(1, 2, 0, 3)
    return (object_field, probe_modes, coef[None, None])


def solution(mesh):
    placed = (
        P(None, "row", "col"),
        P(),
        P("row", "col", None, None),
        P("row", "col", None, None),
        P("row", "col"),
        P("row", "col", None, None, None),
    )
    return jax.shard_map(
        shards,
        mesh=mesh,
        in_specs=placed,
        out_specs=(P(None, "row", "col"), P(), P("row", "col", None, None)),
        check_vma=False,
    )
```

```python
import functools
import math

import jax
import jax.numpy as jnp
import numpy as np
from jax import lax
from jax.experimental import pallas as pl
from jax.experimental.pallas import tpu as pltpu
from jax.sharding import PartitionSpec as P

PS = 128
MODES = 8
TILE = 128
PMAX = 32
ITERS = 2
EXT = TILE + PS
F32 = jnp.float32
BF16 = jnp.bfloat16
DEVICES = 128
PAIRS = 4
LEAD = 33


def split(x):
    hi = x.astype(BF16)
    lo = (x - hi.astype(F32)).astype(BF16)
    return hi, lo


def triple(x, axis):
    hi, lo = split(x)
    return jnp.concatenate([hi, lo, hi], axis=axis)


def dft_constants():
    ramp = np.arange(PS)
    angles = (ramp[:, None] * ramp[None, :] % PS) * (2.0 * math.pi / PS)
    cos = np.cos(angles) / math.sqrt(PS)
    sin = -np.sin(angles) / math.sqrt(PS)
    ahead = np.block([[cos, sin], [-sin, cos]])
    back = np.block([[cos, -sin], [sin, cos]])

    def parts(table):
        table = table.astype(np.float32)
        hi = table.astype(jnp.bfloat16)
        lo = (table - hi.astype(np.float32)).astype(jnp.bfloat16)
        return hi, lo

    def tall(table):
        hi, lo = parts(table)
        return np.concatenate([hi, hi, lo], axis=0)

    def wide(table):
        hi, lo = parts(table)
        return np.concatenate([hi, hi, lo], axis=1)

    return tall(ahead), wide(back), wide(ahead), tall(back)


def dot(a, b):
    return jnp.dot(a, b, preferred_element_type=F32)


def patch_kernel(offs, ext, coef, patches, pw, moment):
    lane = lax.broadcasted_iota(jnp.int32, (PS, PS), 1)

    def cut(p, _):
        top = offs[p, 0]
        left = offs[p, 1]
        turn = (PS - left) & (PS - 1)
        inside = lane < PS - left
        total = None
        for c in range(2):
            a = pltpu.roll(ext[c, 0, pl.ds(top, PS), :], turn, 1)
            b = pltpu.roll(ext[c, 1, pl.ds(top, PS), :], turn, 1)
            patch = jnp.where(inside, a, b)
            patches[p, c] = patch
            total = patch * patch if total is None else total + patch * patch
        pw[pl.ds(p, PS, stride=LEAD), :] = total
        return 0

    lax.fori_loop(0, PMAX, cut, 0, unroll=4)
    square = coef[...] * coef[...]
    hi, lo = split(square.T)
    zero = jnp.zeros_like(hi)
    left = jnp.concatenate(
        [jnp.concatenate([hi, hi], axis=1), jnp.concatenate([lo, zero], axis=1)], axis=0
    )

    def rows(y, _):
        pair = jnp.concatenate(
            [pw[pl.ds(2 * y * LEAD, PMAX), :], pw[pl.ds((2 * y + 1) * LEAD, PMAX), :]], axis=1
        )
        h, l = split(pair)
        out = dot(left, jnp.concatenate([h, l], axis=0))
        out = out[:MODES] + out[MODES:]
        moment[2 * y] = out[:, :PS]
        moment[2 * y + 1] = out[:, PS:]
        return 0

    lax.fori_loop(0, PS // 2, rows, 0, unroll=8)


def probe_kernel(modes, coef, probe_r, probe_i):
    left = triple(coef[...], 1)

    def rows(y, _):
        m = modes[y]
        h = m.astype(BF16).astype(F32)
        right = jnp.concatenate([h, h, m - h], axis=0).astype(BF16)
        out = dot(left, right)
        start = y * LEAD
        probe_r[pl.ds(start, PMAX), :] = out[:, :PS]
        probe_i[pl.ds(start, PMAX), :] = out[:, PS:]
        return 0

    lax.fori_loop(0, PS, rows, 0, unroll=8)


def wave_kernel(
    offs, patches, photons, probe_r, probe_i, coef, ahead_t, back_w, ahead_w, back_t,
    acc_rl, acc_rh, acc_il, acc_ih, acc_pl, acc_ph, cross_r, cross_i, moment,
    wave, field,
):
    step = pl.program_id(0)
    lane = lax.broadcasted_iota(jnp.int32, (PS, PS), 1)
    sums = ((acc_rl, acc_rh), (acc_il, acc_ih), (acc_pl, acc_ph))

    @pl.when(step == 0)
    def _():
        for low, high in sums:
            low[...] = jnp.zeros_like(low)
            high[...] = jnp.zeros_like(high)

    def regroup(x):
        top = jnp.concatenate([x[:PS, :PS], x[PS:, :PS]], axis=1)
        low = jnp.concatenate([x[:PS, PS:], x[PS:, PS:]], axis=1)
        return jnp.concatenate([top, low], axis=0)

    def take(j, q):
        p = 2 * PAIRS * step + 2 * j + q
        return (
            probe_r[pl.ds(p, PS, stride=LEAD), :],
            probe_i[pl.ds(p, PS, stride=LEAD), :],
            patches[2 * j + q, 0],
            patches[2 * j + q, 1],
        )

    def start(j):
        for q in range(2):
            pr, pi, obj_r, obj_i = take(j, q)
            rows = slice(q * PS, (q + 1) * PS)
            wave[j, rows, :PS] = pr * obj_r - pi * obj_i
            wave[j, rows, PS:] = pr * obj_i + pi * obj_r

    def correct(j, far):
        count = jnp.concatenate([photons[2 * j], photons[2 * j + 1]], axis=1).astype(F32)
        far_r = far[:PS]
        far_i = far[PS:]
        size = jnp.maximum(far_r * far_r + far_i * far_i, 0.25)
        scale = count * lax.rsqrt(jnp.maximum(count * size, 0.0625)) * 0.03125
        return jnp.concatenate([far_r * scale, far_i * scale], axis=0)

    def finish(j):
        for q in range(2):
            p = 2 * PAIRS * step + 2 * j + q
            top = offs[p, 0]
            left = offs[p, 1]
            turn = left & (PS - 1)
            inside = lane >= left
            rows = slice(q * PS, (q + 1) * PS)
            diff_r = field[j, rows, :PS]
            diff_i = field[j, rows, PS:]
            pr, pi, obj_r, obj_i = take(j, q)
            cross_r[pl.ds(p, PS, stride=LEAD), :] = obj_r * diff_r + obj_i * diff_i
            cross_i[pl.ds(p, PS, stride=LEAD), :] = obj_r * diff_i - obj_i * diff_r
            pieces = (
                pr * diff_r + pi * diff_i,
                pr * diff_i - pi * diff_r,
                pr * pr + pi * pi,
            )
            for (low, high), piece in zip(sums, pieces):
                turned = pltpu.roll(piece, turn, 1)
                near = jnp.where(inside, turned, 0.0)
                low[pl.ds(top, PS), :] += near
                high[pl.ds(top, PS), :] += turned - near

    pairs = range(PAIRS)
    for j in pairs:
        start(j)
    x = [dot(triple(wave[j], 1), ahead_t[...]) for j in pairs]
    x = [dot(back_w[...], triple(regroup(x[j]), 0)) for j in pairs]
    x = [correct(j, x[j]) for j in pairs]
    x = [dot(ahead_w[...], triple(x[j], 0)) for j in pairs]
    for j in pairs:
        field[j] = dot(triple(regroup(x[j]), 1), back_t[...]) - wave[j]
    for j in pairs:
        finish(j)

    @pl.when(step == PMAX // (2 * PAIRS) - 1)
    def _():
        hi, lo = split(coef[...].T)
        zero = jnp.zeros_like(hi)
        left = jnp.concatenate(
            [jnp.concatenate([hi, hi], axis=1), jnp.concatenate([lo, zero], axis=1)], axis=0
        )

        def rows(y, _):
            start = y * LEAD
            pair = jnp.concatenate(
                [cross_r[pl.ds(start, PMAX), :], cross_i[pl.ds(start, PMAX), :]], axis=1
            )
            h, l = split(pair)
            out = dot(left, jnp.concatenate([h, l], axis=0))
            moment[y] = out[:MODES] + out[MODES:]
            return 0

        lax.fori_loop(0, PS, rows, 0, unroll=8)


CHUNK = 16


def coef_kernel(cross_r, cross_i, powers, modes, coef, out, num, den):
    step = pl.program_id(0)

    @pl.when(step == 0)
    def _():
        num[...] = jnp.zeros_like(num)
        den[...] = jnp.zeros_like(den)

    dims = (((1,), (1,)), ((), ()))

    def wide_dot(a, b):
        return lax.dot_general(a, b, dims, preferred_element_type=F32)

    top = jnp.zeros((PMAX, MODES), F32)
    low = jnp.zeros((PMAX, MODES), F32)
    for y in range(CHUNK):
        rows = slice(y * LEAD, y * LEAD + PMAX)
        cross = jnp.concatenate([cross_r[rows, :], cross_i[rows, :]], axis=1)
        m = modes[y]
        power = m[:, :PS] * m[:, :PS] + m[:, PS:] * m[:, PS:]
        h, l = split(m)
        top += wide_dot(triple(cross, 1), jnp.concatenate([h, h, l], axis=1))
        h, l = split(power)
        low += wide_dot(triple(powers[rows, :], 1), jnp.concatenate([h, h, l], axis=1))
    num[...] += top
    den[...] += low

    @pl.when(step == PS // CHUNK - 1)
    def _():
        out[...] = coef[...] + num[...] / (den[...] + 1.0)


SMEM = pl.BlockSpec(memory_space=pltpu.SMEM)
VMEM = pl.BlockSpec(memory_space=pltpu.VMEM)


def cut_patches(offs, ext, coef):
    return pl.pallas_call(
        patch_kernel,
        out_shape=(
            jax.ShapeDtypeStruct((PMAX, 2, PS, PS), F32),
            jax.ShapeDtypeStruct((PS * LEAD, PS), F32),
            jax.ShapeDtypeStruct((PS, MODES, PS), F32),
        ),
        in_specs=[SMEM, VMEM, VMEM],
        out_specs=(VMEM, VMEM, VMEM),
        compiler_params=pltpu.CompilerParams(vmem_limit_bytes=4 << 20),
        name="cut",
    )(offs, ext, coef)


def mix_probes(modes, coef):
    grid = jax.ShapeDtypeStruct((PS * LEAD, PS), F32)
    return pl.pallas_call(
        probe_kernel,
        out_shape=(grid, grid),
        in_specs=[VMEM, VMEM],
        out_specs=(VMEM, VMEM),
        compiler_params=pltpu.CompilerParams(vmem_limit_bytes=2 << 20),
        name="probes",
    )(modes, coef)


def waves(offs, patches, photons, probe_r, probe_i, coef, tables):
    half = jax.ShapeDtypeStruct((EXT, PS), F32)
    grid = jax.ShapeDtypeStruct((PS * LEAD, PS), F32)
    return pl.pallas_call(
        wave_kernel,
        grid=(PMAX // (2 * PAIRS),),
        out_shape=(*[half] * 6, grid, grid, jax.ShapeDtypeStruct((PS, MODES, 2 * PS), F32)),
        in_specs=[
            SMEM,
            pl.BlockSpec((2 * PAIRS, 2, PS, PS), lambda i: (i, 0, 0, 0)),
            pl.BlockSpec((2 * PAIRS, PS, PS), lambda i: (i, 0, 0)),
            VMEM,
            VMEM,
            VMEM,
            *[VMEM] * len(tables),
        ],
        out_specs=(VMEM,) * 9,
        scratch_shapes=[
            pltpu.VMEM((PAIRS, 2 * PS, 2 * PS), F32),
            pltpu.VMEM((PAIRS, 2 * PS, 2 * PS), F32),
        ],
        compiler_params=pltpu.CompilerParams(
            dimension_semantics=("arbitrary",), vmem_limit_bytes=20 << 20
        ),
        name="waves",
    )(offs, patches, photons, probe_r, probe_i, coef, *tables)


def new_coefficients(cross_r, cross_i, powers, modes, coef):
    rows = pl.BlockSpec((CHUNK * LEAD, PS), lambda i: (i, 0))
    whole = pl.BlockSpec((PMAX, MODES), lambda i: (0, 0))
    return pl.pallas_call(
        coef_kernel,
        grid=(PS // CHUNK,),
        out_shape=jax.ShapeDtypeStruct((PMAX, MODES), F32),
        in_specs=[
            rows,
            rows,
            rows,
            pl.BlockSpec((CHUNK, MODES, 2 * PS), lambda i: (i, 0, 0)),
            whole,
        ],
        out_specs=whole,
        scratch_shapes=[pltpu.VMEM((PMAX, MODES), F32)] * 2,
        compiler_params=pltpu.CompilerParams(
            dimension_semantics=("arbitrary",), vmem_limit_bytes=6 << 20
        ),
        name="coefs",
    )(cross_r, cross_i, powers, modes, coef)


def swap_sides(low_part, high_part, axis):
    count = lax.axis_size(axis)
    up = [(i, i + 1) for i in range(count - 1)]
    down = [(i + 1, i) for i in range(count - 1)]
    from_below = lax.ppermute(high_part, axis, up)
    from_above = lax.ppermute(low_part, axis, down)
    return from_below, from_above


def extend(block):
    margin = PS // 2
    low, high = swap_sides(block[:, :margin], block[:, -margin:], "row")
    block = jnp.concatenate([low, block, high], axis=1)
    low, high = swap_sides(block[:, :, :margin], block[:, :, -margin:], "col")
    return jnp.concatenate([low, block, high], axis=2)


def fold(acc):
    margin = PS // 2
    full = jnp.concatenate([jnp.stack(acc[::2]), jnp.stack(acc[1::2])], axis=2)
    low, high = swap_sides(full[:, :margin], full[:, -margin:], "row")
    mid = full[:, margin:-margin]
    mid = jnp.concatenate([mid[:, :margin] + low, mid[:, margin:] + high], axis=1)
    low, high = swap_sides(mid[:, :, :margin], mid[:, :, -margin:], "col")
    mid = mid[:, :, margin:-margin]
    return jnp.concatenate([mid[:, :, :margin] + low, mid[:, :, margin:] + high], axis=2)


def shards(object_field, probe_modes, coefficients, offsets, counts, measured):
    tables = tuple(jnp.asarray(t) for t in dft_constants())
    offs = offsets[0, 0]
    photons = measured[0, 0]
    coef = coefficients[0, 0]
    live = (lax.iota(jnp.int32, PMAX) < counts[0, 0]).astype(F32)[:, None]
    me = lax.axis_index("row") * lax.axis_size("col") + lax.axis_index("col")
    modes = probe_modes.transpose(2, 0, 1, 3).reshape(PS, MODES, 2 * PS)
    for iteration in range(ITERS):
        ext = extend(object_field)
        ext = jnp.stack([ext[:, :, :PS], ext[:, :, PS:]], axis=1)
        used = coef * live
        patches, powers, power_moment = cut_patches(offs, ext, used)
        probe_r, probe_i = mix_probes(modes, used)
        *acc, cross_r, cross_i, moment = waves(
            offs, patches, photons, probe_r, probe_i, used, tables
        )
        sent = jnp.concatenate([moment, power_moment], axis=2)
        got = lax.all_to_all(sent, ("row", "col"), 0, 0, tiled=True)
        total = jnp.sum(got, axis=0)
        power = total[:, 2 * PS:] + 1.0
        mine = lax.dynamic_index_in_dim(modes, me, 0, keepdims=False)
        mine = mine + total[:, : 2 * PS] / jnp.concatenate([power, power], axis=1)
        coef = new_coefficients(cross_r, cross_i, powers, modes, coef)
        copies = jnp.broadcast_to(mine[None], (DEVICES, MODES, 2 * PS))
        modes = lax.all_to_all(copies, ("row", "col"), 0, 0, tiled=True)
        interior = fold(acc)
        object_field = object_field + interior[0:2] / (interior[2:3] + 1.0)
    probe_modes = modes.reshape(PS, MODES, 2, PS).transpose(1, 2, 0, 3)
    return (object_field, probe_modes, coef[None, None])


def solution(mesh):
    placed = (
        P(None, "row", "col"),
        P(),
        P("row", "col", None, None),
        P("row", "col", None, None),
        P("row", "col"),
        P("row", "col", None, None, None),
    )
    return jax.shard_map(
        shards,
        mesh=mesh,
        in_specs=placed,
        out_specs=(P(None, "row", "col"), P(), P("row", "col", None, None)),
        check_vma=False,
    )
```

```python
import functools
import math

import jax
import jax.numpy as jnp
import numpy as np
from jax import lax
from jax.experimental import pallas as pl
from jax.experimental.pallas import tpu as pltpu
from jax.sharding import PartitionSpec as P

PS = 128
MODES = 8
TILE = 128
PMAX = 32
ITERS = 2
EXT = TILE + PS
F32 = jnp.float32
BF16 = jnp.bfloat16
PAIRS = 4
LEAD = 33
ROWS = PS // 2


def split(x):
    hi = x.astype(BF16)
    lo = (x - hi.astype(F32)).astype(BF16)
    return hi, lo


def triple(x, axis):
    hi, lo = split(x)
    return jnp.concatenate([hi, lo, hi], axis=axis)


def dft_constants():
    ramp = np.arange(PS)
    angles = (ramp[:, None] * ramp[None, :] % PS) * (2.0 * math.pi / PS)
    cos = np.cos(angles) / math.sqrt(PS)
    sin = -np.sin(angles) / math.sqrt(PS)
    ahead = np.block([[cos, sin], [-sin, cos]])
    back = np.block([[cos, -sin], [sin, cos]])

    def parts(table):
        table = table.astype(np.float32)
        hi = table.astype(jnp.bfloat16)
        lo = (table - hi.astype(np.float32)).astype(jnp.bfloat16)
        return hi, lo

    def tall(table):
        hi, lo = parts(table)
        return np.concatenate([hi, hi, lo], axis=0)

    def wide(table):
        hi, lo = parts(table)
        return np.concatenate([hi, hi, lo], axis=1)

    return tall(ahead), wide(back), wide(ahead), tall(back)


def dot(a, b):
    return jnp.dot(a, b, preferred_element_type=F32)


def probe_kernel(half, near, far, coef, probe_r, probe_i):
    left = triple(coef[...], 1)
    for source, base in ((near, half[0] * ROWS), (far, (1 - half[0]) * ROWS)):

        def rows(y, _):
            m = source[y]
            h = m.astype(BF16).astype(F32)
            right = jnp.concatenate([h, h, m - h], axis=0).astype(BF16)
            out = dot(left, right)
            start = (base + y) * LEAD
            probe_r[pl.ds(start, PMAX), :] = out[:, :PS]
            probe_i[pl.ds(start, PMAX), :] = out[:, PS:]
            return 0

        lax.fori_loop(0, ROWS, rows, 0, unroll=8)


def wave_kernel(
    half, offs, ext, photons, probe_r, probe_i, coef, ahead_t, back_w, ahead_w, back_t,
    acc_rl, acc_rh, acc_il, acc_ih, acc_pl, acc_ph, out_r, out_i, out_p, near, far,
    patches, wave, field, cross_r, cross_i, power, sems,
):
    step = pl.program_id(0)
    lane = lax.broadcasted_iota(jnp.int32, (PS, PS), 1)
    sums = ((acc_rl, acc_rh), (acc_il, acc_ih), (acc_pl, acc_ph))

    @pl.when(step == 0)
    def _():
        for low, high in sums:
            low[...] = jnp.zeros_like(low)
            high[...] = jnp.zeros_like(high)

    def regroup(x):
        top = jnp.concatenate([x[:PS, :PS], x[PS:, :PS]], axis=1)
        low = jnp.concatenate([x[:PS, PS:], x[PS:, PS:]], axis=1)
        return jnp.concatenate([top, low], axis=0)

    def take(j, q):
        p = 2 * PAIRS * step + 2 * j + q
        return (
            probe_r[pl.ds(p, PS, stride=LEAD), :],
            probe_i[pl.ds(p, PS, stride=LEAD), :],
            patches[2 * j + q, 0],
            patches[2 * j + q, 1],
        )

    def cut(j, q):
        p = 2 * PAIRS * step + 2 * j + q
        top = offs[p, 0]
        left = offs[p, 1]
        turn = (PS - left) & (PS - 1)
        inside = lane < PS - left
        total = None
        for c in range(2):
            a = pltpu.roll(ext[c, 0, pl.ds(top, PS), :], turn, 1)
            b = pltpu.roll(ext[c, 1, pl.ds(top, PS), :], turn, 1)
            patch = jnp.where(inside, a, b)
            patches[2 * j + q, c] = patch
            total = patch * patch if total is None else total + patch * patch
        power[pl.ds(p, PS, stride=LEAD), :] = total

    def start(j):
        for q in range(2):
            cut(j, q)
            pr, pi, obj_r, obj_i = take(j, q)
            rows = slice(q * PS, (q + 1) * PS)
            wave[j, rows, :PS] = pr * obj_r - pi * obj_i
            wave[j, rows, PS:] = pr * obj_i + pi * obj_r

    def correct(j, there):
        count = jnp.concatenate([photons[2 * j], photons[2 * j + 1]], axis=1).astype(F32)
        far_r = there[:PS]
        far_i = there[PS:]
        size = jnp.maximum(far_r * far_r + far_i * far_i, 0.25)
        scale = count * lax.rsqrt(jnp.maximum(count * size, 0.0625)) * 0.03125
        return jnp.concatenate([far_r * scale, far_i * scale], axis=0)

    def finish(j):
        for q in range(2):
            p = 2 * PAIRS * step + 2 * j + q
            top = offs[p, 0]
            left = offs[p, 1]
            turn = left & (PS - 1)
            inside = lane >= left
            rows = slice(q * PS, (q + 1) * PS)
            diff_r = field[j, rows, :PS]
            diff_i = field[j, rows, PS:]
            pr, pi, obj_r, obj_i = take(j, q)
            cross_r[pl.ds(p, PS, stride=LEAD), :] = obj_r * diff_r + obj_i * diff_i
            cross_i[pl.ds(p, PS, stride=LEAD), :] = obj_r * diff_i - obj_i * diff_r
            pieces = (
                pr * diff_r + pi * diff_i,
                pr * diff_i - pi * diff_r,
                pr * pr + pi * pi,
            )
            for (low, high), piece in zip(sums, pieces):
                turned = pltpu.roll(piece, turn, 1)
                near = jnp.where(inside, turned, 0.0)
                low[pl.ds(top, PS), :] += near
                high[pl.ds(top, PS), :] += turned - near

    pairs = range(PAIRS)
    for j in pairs:
        start(j)
    x = [dot(triple(wave[j], 1), ahead_t[...]) for j in pairs]
    x = [dot(back_w[...], triple(regroup(x[j]), 0)) for j in pairs]
    x = [correct(j, x[j]) for j in pairs]
    x = [dot(ahead_w[...], triple(x[j], 0)) for j in pairs]
    for j in pairs:
        field[j] = dot(triple(regroup(x[j]), 1), back_t[...]) - wave[j]
    for j in pairs:
        finish(j)

    @pl.when(step == PMAX // (2 * PAIRS) - 1)
    def _():
        copies = [
            pltpu.make_async_copy(source, target, sems.at[i])
            for i, (source, target) in enumerate(
                ((cross_r, out_r), (cross_i, out_i), (power, out_p))
            )
        ]
        for copy in copies:
            copy.start()

        def stacked(x):
            hi, lo = split(x.T)
            zero = jnp.zeros_like(hi)
            return jnp.concatenate(
                [jnp.concatenate([hi, hi], axis=1), jnp.concatenate([lo, zero], axis=1)], axis=0
            )

        left = stacked(coef[...])
        left_square = stacked(coef[...] * coef[...])
        for target, base in ((near, half[0] * ROWS), (far, (1 - half[0]) * ROWS)):

            def rows(y, _):
                begin = (base + y) * LEAD
                pair = jnp.concatenate(
                    [cross_r[pl.ds(begin, PMAX), :], cross_i[pl.ds(begin, PMAX), :]], axis=1
                )
                h, l = split(pair)
                out = dot(left, jnp.concatenate([h, l], axis=0))
                target[y, :, : 2 * PS] = out[:MODES] + out[MODES:]
                h, l = split(power[pl.ds(begin, PMAX), :])
                out = dot(left_square, jnp.concatenate([h, l], axis=0))
                target[y, :, 2 * PS:] = out[:MODES] + out[MODES:]
                return 0

            lax.fori_loop(0, ROWS, rows, 0, unroll=8)
        for copy in copies:
            copy.wait()


CHUNK = 16


def coef_kernel(cross_r, cross_i, powers, modes, coef, out, num, den):
    step = pl.program_id(0)

    @pl.when(step == 0)
    def _():
        num[...] = jnp.zeros_like(num)
        den[...] = jnp.zeros_like(den)

    dims = (((1,), (1,)), ((), ()))

    def wide_dot(a, b):
        return lax.dot_general(a, b, dims, preferred_element_type=F32)

    top = jnp.zeros((PMAX, MODES), F32)
    low = jnp.zeros((PMAX, MODES), F32)
    for y in range(CHUNK):
        rows = slice(y * LEAD, y * LEAD + PMAX)
        cross = jnp.concatenate([cross_r[rows, :], cross_i[rows, :]], axis=1)
        m = modes[y]
        power = m[:, :PS] * m[:, :PS] + m[:, PS:] * m[:, PS:]
        h, l = split(m)
        top += wide_dot(triple(cross, 1), jnp.concatenate([h, h, l], axis=1))
        h, l = split(power)
        low += wide_dot(triple(powers[rows, :], 1), jnp.concatenate([h, h, l], axis=1))
    num[...] += top
    den[...] += low

    @pl.when(step == PS // CHUNK - 1)
    def _():
        out[...] = coef[...] + num[...] / (den[...] + 1.0)


SMEM = pl.BlockSpec(memory_space=pltpu.SMEM)
VMEM = pl.BlockSpec(memory_space=pltpu.VMEM)


def mix_probes(half, near, far, coef):
    grid = jax.ShapeDtypeStruct((PS * LEAD, PS), F32)
    return pl.pallas_call(
        probe_kernel,
        out_shape=(grid, grid),
        in_specs=[SMEM, VMEM, VMEM, VMEM],
        out_specs=(VMEM, VMEM),
        compiler_params=pltpu.CompilerParams(vmem_limit_bytes=2 << 20),
        name="probes",
    )(half, near, far, coef)


def waves(half, offs, ext, photons, probe_r, probe_i, coef, tables):
    part = jax.ShapeDtypeStruct((EXT, PS), F32)
    grid = jax.ShapeDtypeStruct((PS * LEAD, PS), F32)
    rows = jax.ShapeDtypeStruct((ROWS, MODES, 3 * PS), F32)
    square = pltpu.VMEM((PAIRS, 2 * PS, 2 * PS), F32)
    return pl.pallas_call(
        wave_kernel,
        grid=(PMAX // (2 * PAIRS),),
        out_shape=(*[part] * 6, *[grid] * 3, rows, rows),
        in_specs=[
            SMEM,
            SMEM,
            VMEM,
            pl.BlockSpec((2 * PAIRS, PS, PS), lambda i: (i, 0, 0)),
            VMEM,
            VMEM,
            VMEM,
            *[VMEM] * len(tables),
        ],
        out_specs=(*[VMEM] * 6, *[pl.BlockSpec(memory_space=pl.ANY)] * 3, VMEM, VMEM),
        scratch_shapes=[
            pltpu.VMEM((2 * PAIRS, 2, PS, PS), F32),
            square,
            square,
            *[pltpu.VMEM((PS * LEAD, PS), F32)] * 3,
            pltpu.SemaphoreType.DMA((3,)),
        ],
        compiler_params=pltpu.CompilerParams(
            dimension_semantics=("arbitrary",), vmem_limit_bytes=24 << 20
        ),
        name="waves",
    )(half, offs, ext, photons, probe_r, probe_i, coef, *tables)


def new_coefficients(cross_r, cross_i, powers, modes, coef):
    rows = pl.BlockSpec((CHUNK * LEAD, PS), lambda i: (i, 0))
    whole = pl.BlockSpec((PMAX, MODES), lambda i: (0, 0))
    return pl.pallas_call(
        coef_kernel,
        grid=(PS // CHUNK,),
        out_shape=jax.ShapeDtypeStruct((PMAX, MODES), F32),
        in_specs=[
            rows,
            rows,
            rows,
            pl.BlockSpec((CHUNK, MODES, 2 * PS), lambda i: (i, 0, 0)),
            whole,
        ],
        out_specs=whole,
        scratch_shapes=[pltpu.VMEM((PMAX, MODES), F32)] * 2,
        compiler_params=pltpu.CompilerParams(
            dimension_semantics=("arbitrary",), vmem_limit_bytes=6 << 20
        ),
        name="coefs",
    )(cross_r, cross_i, powers, modes, coef)


def shifted(x, move):
    rows, cols = lax.axis_size("row"), lax.axis_size("col")
    pairs = []
    for a in range(rows):
        for b in range(cols):
            c, d = a + move[0], b + move[1]
            if 0 <= c < rows and 0 <= d < cols:
                pairs.append((c * cols + d, a * cols + b))
    return lax.ppermute(x, ("row", "col"), pairs)


def extend(block):
    margin = PS // 2
    ends = {-1: slice(PS - margin, PS), 0: slice(0, PS), 1: slice(0, margin)}
    rows = []
    for a in (-1, 0, 1):
        row = [
            block if (a, b) == (0, 0) else shifted(block[:, ends[a], ends[b]], (a, b))
            for b in (-1, 0, 1)
        ]
        rows.append(jnp.concatenate(row, axis=2))
    full = jnp.concatenate(rows, axis=1)
    return jnp.stack([full[:, :, :PS], full[:, :, PS:]], axis=1)


def sum_extended(acc):
    low = shifted(jnp.stack([x[PS:] for x in acc]), (-1, 0))
    high = shifted(jnp.stack([x[:PS] for x in acc]), (1, 0))
    left = jnp.concatenate([jnp.stack(acc[::2])[:, :PS] + low[::2], jnp.stack(acc[::2])[:, PS:] + high[::2]], axis=1)
    right = jnp.concatenate([jnp.stack(acc[1::2])[:, :PS] + low[1::2], jnp.stack(acc[1::2])[:, PS:] + high[1::2]], axis=1)
    return jnp.stack([left + shifted(right, (0, -1)), right + shifted(left, (0, 1))], axis=1)


def inside_object():
    margin = PS // 2

    def axis(name, count):
        place = lax.axis_index(name) * TILE - margin + lax.iota(jnp.int32, EXT)
        return (place >= 0) & (place < count * TILE)

    rows = axis("row", lax.axis_size("row"))
    cols = axis("col", lax.axis_size("col")).reshape(2, 1, PS)
    return rows[None, :, None] & cols


def fold(acc):
    margin = PS // 2
    full = jnp.concatenate([jnp.stack(acc[::2]), jnp.stack(acc[1::2])], axis=2)
    low = shifted(full[:, -margin:], (-1, 0))
    high = shifted(full[:, :margin], (1, 0))
    mid = full[:, margin:-margin]
    mid = jnp.concatenate([mid[:, :margin] + low, mid[:, margin:] + high], axis=1)
    low = shifted(mid[:, :, -margin:], (0, -1))
    high = shifted(mid[:, :, :margin], (0, 1))
    mid = mid[:, :, margin:-margin]
    return jnp.concatenate([mid[:, :, :margin] + low, mid[:, :, margin:] + high], axis=2)


def shards(object_field, probe_modes, coefficients, offsets, counts, measured):
    tables = tuple(jnp.asarray(t) for t in dft_constants())
    offs = offsets[0, 0]
    photons = measured[0, 0]
    coef = coefficients[0, 0]
    live = (lax.iota(jnp.int32, PMAX) < counts[0, 0]).astype(F32)[:, None]
    rows, cols = lax.axis_size("row"), lax.axis_size("col")
    core = lax.axis_index("row") % 2
    half = core.reshape(1)
    groups = [[a * cols + b for a in range(k, rows, 2) for b in range(cols)] for k in range(2)]
    mates = [(a, a ^ 1) for a in range(rows)]
    place = lax.axis_index("row") // 2 * cols + lax.axis_index("col")

    def exchange(x):
        return lax.all_to_all(x, ("row", "col"), 0, 0, axis_index_groups=groups, tiled=True)

    modes = probe_modes.transpose(2, 0, 1, 3).reshape(PS, MODES, 2 * PS)
    near = lax.dynamic_slice_in_dim(modes, core * ROWS, ROWS, 0)
    far = lax.dynamic_slice_in_dim(modes, (1 - core) * ROWS, ROWS, 0)
    mine = lax.dynamic_index_in_dim(near, place, 0, keepdims=False)
    ext = extend(object_field)
    for iteration in range(ITERS):
        used = coef * live
        probe_r, probe_i = mix_probes(half, near, far, used)
        *acc, cross_r, cross_i, powers, kept, given = waves(
            half, offs, ext, photons, probe_r, probe_i, used, tables
        )
        sent = kept + lax.ppermute(given, "row", mates)
        total = jnp.sum(exchange(sent), axis=0)
        power = total[:, 2 * PS:] + 1.0
        mine = mine + total[:, : 2 * PS] / jnp.concatenate([power, power], axis=1)
        near = exchange(jnp.broadcast_to(mine[None], (ROWS, MODES, 2 * PS)))
        far = lax.ppermute(near, "row", mates)
        coef = new_coefficients(cross_r, cross_i, powers, modes, coef)
        modes = jnp.where(
            core == 0, jnp.concatenate([near, far]), jnp.concatenate([far, near])
        )
        if iteration < ITERS - 1:
            total = sum_extended(acc)
            step = total[0:2] / (total[2:3] + 1.0)
            ext = ext + jnp.where(inside_object()[None], step, 0.0)
        else:
            margin = PS // 2
            field = jnp.concatenate(
                [ext[:, 0, margin:-margin, margin:], ext[:, 1, margin:-margin, :margin]], axis=2
            )
            total = fold(acc)
            object_field = field + total[0:2] / (total[2:3] + 1.0)
    probe_modes = modes.reshape(PS, MODES, 2, PS).transpose(1, 2, 0, 3)
    return (object_field, probe_modes, coef[None, None])


def solution(mesh):
    placed = (
        P(None, "row", "col"),
        P(),
        P("row", "col", None, None),
        P("row", "col", None, None),
        P("row", "col"),
        P("row", "col", None, None, None),
    )
    return jax.shard_map(
        shards,
        mesh=mesh,
        in_specs=placed,
        out_specs=(P(None, "row", "col"), P(), P("row", "col", None, None)),
        check_vma=False,
    )
```

```python
import functools
import math

import jax
import jax.numpy as jnp
import numpy as np
from jax import lax
from jax.experimental import pallas as pl
from jax.experimental.pallas import tpu as pltpu
from jax.sharding import PartitionSpec as P

PS = 128
MODES = 8
TILE = 128
PMAX = 32
ITERS = 2
EXT = TILE + PS
F32 = jnp.float32
BF16 = jnp.bfloat16
PAIRS = 4
LEAD = 33
ROWS = PS // 2
MARGIN = PS // 2


def split(x):
    hi = x.astype(BF16)
    lo = (x - hi.astype(F32)).astype(BF16)
    return hi, lo


def triple(x, axis):
    hi, lo = split(x)
    return jnp.concatenate([hi, lo, hi], axis=axis)


def dft_constants():
    ramp = np.arange(PS)
    angles = (ramp[:, None] * ramp[None, :] % PS) * (2.0 * math.pi / PS)
    cos = np.cos(angles) / math.sqrt(PS)
    sin = -np.sin(angles) / math.sqrt(PS)
    ahead = np.block([[cos, sin], [-sin, cos]])
    back = np.block([[cos, -sin], [sin, cos]])

    def parts(table):
        table = table.astype(np.float32)
        hi = table.astype(jnp.bfloat16)
        lo = (table - hi.astype(np.float32)).astype(jnp.bfloat16)
        return hi, lo

    def tall(table):
        hi, lo = parts(table)
        return np.concatenate([hi, hi, lo], axis=0)

    def wide(table):
        hi, lo = parts(table)
        return np.concatenate([hi, hi, lo], axis=1)

    return tall(ahead), wide(back), wide(ahead), tall(back)


def dot(a, b):
    return jnp.dot(a, b, preferred_element_type=F32)


def probe_kernel(half, near, far, coef, probe_r, probe_i):
    left = triple(coef[...], 1)
    skip = far.shape[0] - ROWS
    for source, base, skip in ((near, half[0] * ROWS, 0), (far, (1 - half[0]) * ROWS, skip)):

        def rows(y, _):
            m = source[skip + y]
            h = m.astype(BF16).astype(F32)
            right = jnp.concatenate([h, h, m - h], axis=0).astype(BF16)
            out = dot(left, right)
            start = (base + y) * LEAD
            probe_r[pl.ds(start, PMAX), :] = out[:, :PS]
            probe_i[pl.ds(start, PMAX), :] = out[:, PS:]
            return 0

        lax.fori_loop(0, ROWS, rows, 0, unroll=8)


def wave_kernel(
    half, offs, ext, photons, probe_r, probe_i, coef, ahead_t, back_w, ahead_w, back_t,
    up, mid, down, out_r, out_i, out_p, near, far,
    acc_rl, acc_rh, acc_il, acc_ih, acc_pl, acc_ph,
    patches, wave, field, cross_r, cross_i, power, sems,
):
    step = pl.program_id(0)
    lane = lax.broadcasted_iota(jnp.int32, (PS, PS), 1)
    sums = ((acc_rl, acc_rh), (acc_il, acc_ih), (acc_pl, acc_ph))

    @pl.when(step == 0)
    def _():
        for low, high in sums:
            low[...] = jnp.zeros_like(low)
            high[...] = jnp.zeros_like(high)

    def own_lanes(left):
        return (lane < left + MARGIN) & (lane >= left - MARGIN)

    def regroup(x):
        top = jnp.concatenate([x[:PS, :PS], x[PS:, :PS]], axis=1)
        low = jnp.concatenate([x[:PS, PS:], x[PS:, PS:]], axis=1)
        return jnp.concatenate([top, low], axis=0)

    def take(j, q):
        p = 2 * PAIRS * step + 2 * j + q
        return (
            probe_r[pl.ds(p, PS, stride=LEAD), :],
            probe_i[pl.ds(p, PS, stride=LEAD), :],
            patches[2 * j + q, 0],
            patches[2 * j + q, 1],
        )

    def cut(j, q):
        p = 2 * PAIRS * step + 2 * j + q
        top = offs[p, 0]
        left = offs[p, 1]
        turn = (PS + MARGIN - left) & (PS - 1)
        inside = own_lanes(left)
        total = None
        for c in range(2):
            patch = jnp.where(
                inside, ext[c, 0, pl.ds(top, PS), :], ext[c, 1, pl.ds(top, PS), :]
            )
            patch = pltpu.roll(patch, turn, 1)
            patches[2 * j + q, c] = patch
            total = patch * patch if total is None else total + patch * patch
        power[pl.ds(p, PS, stride=LEAD), :] = total

    def start(j):
        for q in range(2):
            cut(j, q)
            pr, pi, obj_r, obj_i = take(j, q)
            rows = slice(q * PS, (q + 1) * PS)
            wave[j, rows, :PS] = pr * obj_r - pi * obj_i
            wave[j, rows, PS:] = pr * obj_i + pi * obj_r

    def correct(j, there):
        count = jnp.concatenate([photons[2 * j], photons[2 * j + 1]], axis=1).astype(F32)
        far_r = there[:PS]
        far_i = there[PS:]
        size = jnp.maximum(far_r * far_r + far_i * far_i, 0.25)
        scale = count * lax.rsqrt(jnp.maximum(count * size, 0.0625)) * 0.03125
        return jnp.concatenate([far_r * scale, far_i * scale], axis=0)

    def finish(j):
        for q in range(2):
            p = 2 * PAIRS * step + 2 * j + q
            top = offs[p, 0]
            left = offs[p, 1]
            turn = (left + MARGIN) & (PS - 1)
            inside = own_lanes(left)
            rows = slice(q * PS, (q + 1) * PS)
            diff_r = field[j, rows, :PS]
            diff_i = field[j, rows, PS:]
            pr, pi, obj_r, obj_i = take(j, q)
            cross_r[pl.ds(p, PS, stride=LEAD), :] = obj_r * diff_r + obj_i * diff_i
            cross_i[pl.ds(p, PS, stride=LEAD), :] = obj_r * diff_i - obj_i * diff_r
            pieces = (
                pr * diff_r + pi * diff_i,
                pr * diff_i - pi * diff_r,
                pr * pr + pi * pi,
            )
            for (low, high), piece in zip(sums, pieces):
                turned = pltpu.roll(piece, turn, 1)
                near = jnp.where(inside, turned, 0.0)
                low[pl.ds(top, PS), :] += near
                high[pl.ds(top, PS), :] += turned - near

    pairs = range(PAIRS)
    for j in pairs:
        start(j)
    x = [dot(triple(wave[j], 1), ahead_t[...]) for j in pairs]
    x = [dot(back_w[...], triple(regroup(x[j]), 0)) for j in pairs]
    x = [correct(j, x[j]) for j in pairs]
    x = [dot(ahead_w[...], triple(x[j], 0)) for j in pairs]
    for j in pairs:
        field[j] = dot(triple(regroup(x[j]), 1), back_t[...]) - wave[j]
    for j in pairs:
        finish(j)

    @pl.when(step == PMAX // (2 * PAIRS) - 1)
    def _():
        width = up.shape[1]
        for i, piece in enumerate((acc_rl, acc_il, acc_pl, acc_rh, acc_ih, acc_ph)):
            down[i] = piece[:width]
            up[i] = piece[EXT - width:]
            if width < PS:
                mid[i] = piece[width : EXT - width]
        copies = [
            pltpu.make_async_copy(source, target, sems.at[i])
            for i, (source, target) in enumerate(
                ((cross_r, out_r), (cross_i, out_i), (power, out_p))
            )
        ]
        for copy in copies:
            copy.start()

        def stacked(x):
            hi, lo = split(x.T)
            zero = jnp.zeros_like(hi)
            return jnp.concatenate(
                [jnp.concatenate([hi, hi], axis=1), jnp.concatenate([lo, zero], axis=1)], axis=0
            )

        left = stacked(coef[...])
        left_square = stacked(coef[...] * coef[...])
        for target, base in ((near, half[0] * ROWS), (far, (1 - half[0]) * ROWS)):

            def rows(y, _):
                begin = (base + y) * LEAD
                pair = jnp.concatenate(
                    [cross_r[pl.ds(begin, PMAX), :], cross_i[pl.ds(begin, PMAX), :]], axis=1
                )
                h, l = split(pair)
                out = dot(left, jnp.concatenate([h, l], axis=0))
                target[y, :, : 2 * PS] = out[:MODES] + out[MODES:]
                h, l = split(power[pl.ds(begin, PMAX), :])
                out = dot(left_square, jnp.concatenate([h, l], axis=0))
                target[y, :, 2 * PS:] = out[:MODES] + out[MODES:]
                return 0

            lax.fori_loop(0, ROWS, rows, 0, unroll=8)
        for copy in copies:
            copy.wait()


CHUNK = 16


def coef_kernel(cross_r, cross_i, powers, modes, coef, out, num, den):
    step = pl.program_id(0)

    @pl.when(step == 0)
    def _():
        num[...] = jnp.zeros_like(num)
        den[...] = jnp.zeros_like(den)

    dims = (((1,), (1,)), ((), ()))

    def wide_dot(a, b):
        return lax.dot_general(a, b, dims, preferred_element_type=F32)

    top = jnp.zeros((PMAX, MODES), F32)
    low = jnp.zeros((PMAX, MODES), F32)
    for y in range(CHUNK):
        rows = slice(y * LEAD, y * LEAD + PMAX)
        cross = jnp.concatenate([cross_r[rows, :], cross_i[rows, :]], axis=1)
        m = modes[y]
        power = m[:, :PS] * m[:, :PS] + m[:, PS:] * m[:, PS:]
        h, l = split(m)
        top += wide_dot(triple(cross, 1), jnp.concatenate([h, h, l], axis=1))
        h, l = split(power)
        low += wide_dot(triple(powers[rows, :], 1), jnp.concatenate([h, h, l], axis=1))
    num[...] += top
    den[...] += low

    @pl.when(step == PS // CHUNK - 1)
    def _():
        out[...] = coef[...] + num[...] / (den[...] + 1.0)


SMEM = pl.BlockSpec(memory_space=pltpu.SMEM)
VMEM = pl.BlockSpec(memory_space=pltpu.VMEM)


def mix_probes(half, near, far, coef):
    grid = jax.ShapeDtypeStruct((PS * LEAD, PS), F32)
    return pl.pallas_call(
        probe_kernel,
        out_shape=(grid, grid),
        in_specs=[SMEM, VMEM, VMEM, VMEM],
        out_specs=(VMEM, VMEM),
        compiler_params=pltpu.CompilerParams(vmem_limit_bytes=2 << 20),
        name="probes",
    )(half, near, far, coef)


def waves(half, offs, ext, photons, probe_r, probe_i, coef, tables, width):
    edge = jax.ShapeDtypeStruct((6, width, PS), F32)
    inner = jax.ShapeDtypeStruct((6, max(EXT - 2 * width, 8), PS), F32)
    grid = jax.ShapeDtypeStruct((PS * LEAD, PS), F32)
    rows = jax.ShapeDtypeStruct((ROWS, MODES, 3 * PS), F32)
    square = pltpu.VMEM((PAIRS, 2 * PS, 2 * PS), F32)
    return pl.pallas_call(
        wave_kernel,
        grid=(PMAX // (2 * PAIRS),),
        out_shape=(edge, inner, edge, *[grid] * 3, rows, rows),
        in_specs=[
            SMEM,
            SMEM,
            VMEM,
            pl.BlockSpec((2 * PAIRS, PS, PS), lambda i: (i, 0, 0)),
            VMEM,
            VMEM,
            VMEM,
            *[VMEM] * len(tables),
        ],
        out_specs=(*[VMEM] * 3, *[pl.BlockSpec(memory_space=pltpu.HBM)] * 3, VMEM, VMEM),
        scratch_shapes=[
            *[pltpu.VMEM((EXT, PS), F32)] * 6,
            pltpu.VMEM((2 * PAIRS, 2, PS, PS), F32),
            square,
            square,
            *[pltpu.VMEM((PS * LEAD, PS), F32)] * 3,
            pltpu.SemaphoreType.DMA((3,)),
        ],
        compiler_params=pltpu.CompilerParams(
            dimension_semantics=("arbitrary",), vmem_limit_bytes=24 << 20
        ),
        name="waves",
    )(half, offs, ext, photons, probe_r, probe_i, coef, *tables)


def new_coefficients(cross_r, cross_i, powers, modes, coef):
    rows = pl.BlockSpec((CHUNK * LEAD, PS), lambda i: (i, 0))
    whole = pl.BlockSpec((PMAX, MODES), lambda i: (0, 0))
    return pl.pallas_call(
        coef_kernel,
        grid=(PS // CHUNK,),
        out_shape=jax.ShapeDtypeStruct((PMAX, MODES), F32),
        in_specs=[
            rows,
            rows,
            rows,
            pl.BlockSpec((CHUNK, MODES, 2 * PS), lambda i: (i, 0, 0)),
            whole,
        ],
        out_specs=whole,
        scratch_shapes=[pltpu.VMEM((PMAX, MODES), F32)] * 2,
        compiler_params=pltpu.CompilerParams(
            dimension_semantics=("arbitrary",), vmem_limit_bytes=56 << 20
        ),
        name="coefs",
    )(cross_r, cross_i, powers, modes, coef)


def shifted(x, move):
    rows, cols = lax.axis_size("row"), lax.axis_size("col")
    pairs = []
    for a in range(rows):
        for b in range(cols):
            c, d = a + move[0], b + move[1]
            if 0 <= c < rows and 0 <= d < cols:
                pairs.append((c * cols + d, a * cols + b))
    return lax.ppermute(x, ("row", "col"), pairs)


def by_side(low, high):
    lane = lax.broadcasted_iota(jnp.int32, low.shape, low.ndim - 1)
    return jnp.where(lane < MARGIN, low, high)


def extend(block):
    beside = by_side(shifted(block, (0, 1)), shifted(block, (0, -1)))
    both = jnp.stack([block, beside], axis=1)
    above = shifted(both[:, :, -MARGIN:], (-1, 0))
    below = shifted(both[:, :, :MARGIN], (1, 0))
    return jnp.concatenate([above, both, below], axis=2)


def sum_extended(up, down):
    low = down + shifted(up, (-1, 0))
    high = up + shifted(down, (1, 0))
    full = jnp.concatenate([low, high], axis=1)
    own, beside = full[:3], full[3:]
    from_left = shifted(by_side(beside, own), (0, -1))
    from_right = shifted(by_side(own, beside), (0, 1))
    own = own + by_side(from_left, from_right)
    beside = beside + by_side(from_right, from_left)
    return jnp.stack([own, beside], axis=1)


def inside_object():
    a, b = lax.axis_index("row"), lax.axis_index("col")
    place = a * TILE - MARGIN + lax.iota(jnp.int32, EXT)
    rows = (place >= 0) & (place < lax.axis_size("row") * TILE)
    lane = lax.iota(jnp.int32, PS)
    beside = ((lane < MARGIN) & (b < lax.axis_size("col") - 1)) | ((lane >= MARGIN) & (b > 0))
    cols = jnp.stack([jnp.ones_like(beside), beside])
    return rows[None, :, None] & cols[:, None, :]


def fold(up, mid, down):
    edges = jnp.concatenate([shifted(up, (-1, 0)), shifted(down, (1, 0))], axis=1)
    mid = mid + edges
    beside = mid[3:]
    return mid[:3] + by_side(shifted(beside, (0, -1)), shifted(beside, (0, 1)))


def shards(object_field, probe_modes, coefficients, offsets, counts, measured):
    tables = tuple(jnp.asarray(t) for t in dft_constants())
    offs = offsets[0, 0]
    photons = measured[0, 0]
    coef = coefficients[0, 0]
    live = (lax.iota(jnp.int32, PMAX) < counts[0, 0]).astype(F32)[:, None]
    rows, cols = lax.axis_size("row"), lax.axis_size("col")
    core = lax.axis_index("row") % 2
    half = core.reshape(1)
    groups = [[a * cols + b for a in range(k, rows, 2) for b in range(cols)] for k in range(2)]
    mates = [(a, a ^ 1) for a in range(rows)]
    place = lax.axis_index("row") // 2 * cols + lax.axis_index("col")

    def exchange(x):
        return lax.all_to_all(x, ("row", "col"), 0, 0, axis_index_groups=groups, tiled=True)

    modes = probe_modes.transpose(2, 0, 1, 3).reshape(PS, MODES, 2 * PS)
    mine = lax.dynamic_index_in_dim(modes, core * ROWS + place, 0, keepdims=False)
    ext = extend(object_field)
    for iteration in range(ITERS):
        final = iteration == ITERS - 1
        used = coef * live
        if iteration == 0:
            probe_r, probe_i = mix_probes(jnp.zeros_like(half), modes, modes, used)
        else:
            probe_r, probe_i = mix_probes(half, near, far, used)
        up, mid, down, cross_r, cross_i, powers, kept, given = waves(
            half, offs, ext, photons, probe_r, probe_i, used, tables, MARGIN if final else PS
        )
        sent = kept + lax.ppermute(given, "row", mates)
        total = jnp.sum(exchange(sent), axis=0)
        power = total[:, 2 * PS:] + 1.0
        mine = mine + total[:, : 2 * PS] / jnp.concatenate([power, power], axis=1)
        near = exchange(jnp.broadcast_to(mine[None], (ROWS, MODES, 2 * PS)))
        far = lax.ppermute(near, "row", mates)
        coef = new_coefficients(cross_r, cross_i, powers, modes, coef)
        modes = jnp.where(
            core == 0, jnp.concatenate([near, far]), jnp.concatenate([far, near])
        )
        if final:
            total = fold(up, mid, down)
            object_field = ext[:, 0, MARGIN:-MARGIN] + total[0:2] / (total[2:3] + 1.0)
        else:
            total = sum_extended(up, down)
            step = total[0:2] / (total[2:3] + 1.0)
            ext = ext + jnp.where(inside_object()[None], step, 0.0)
    probe_modes = modes.reshape(PS, MODES, 2, PS).transpose(1, 2, 0, 3)
    return (object_field, probe_modes, coef[None, None])


def solution(mesh):
    placed = (
        P(None, "row", "col"),
        P(),
        P("row", "col", None, None),
        P("row", "col", None, None),
        P("row", "col"),
        P("row", "col", None, None, None),
    )
    return jax.shard_map(
        shards,
        mesh=mesh,
        in_specs=placed,
        out_specs=(P(None, "row", "col"), P(), P("row", "col", None, None)),
        check_vma=False,
    )
```

```python
import functools
import math

import jax
import jax.numpy as jnp
import numpy as np
from jax import lax
from jax.experimental import pallas as pl
from jax.experimental.pallas import tpu as pltpu
from jax.sharding import PartitionSpec as P

PS = 128
MODES = 8
TILE = 128
PMAX = 32
ITERS = 2
EXT = TILE + PS
F32 = jnp.float32
BF16 = jnp.bfloat16
PAIRS = 4
LEAD = 33
ROWS = PS // 2
MARGIN = PS // 2


def split(x):
    hi = x.astype(BF16)
    lo = (x - hi.astype(F32)).astype(BF16)
    return hi, lo


def triple(x, axis):
    hi, lo = split(x)
    return jnp.concatenate([hi, lo, hi], axis=axis)


def dft_constants():
    ramp = np.arange(PS)
    angles = (ramp[:, None] * ramp[None, :] % PS) * (2.0 * math.pi / PS)
    cos = np.cos(angles) / math.sqrt(PS)
    sin = -np.sin(angles) / math.sqrt(PS)
    ahead = np.block([[cos, sin], [-sin, cos]])
    back = np.block([[cos, -sin], [sin, cos]])

    def parts(table):
        table = table.astype(np.float32)
        hi = table.astype(jnp.bfloat16)
        lo = (table - hi.astype(np.float32)).astype(jnp.bfloat16)
        return hi, lo

    def tall(table):
        hi, lo = parts(table)
        return np.concatenate([hi, hi, lo], axis=0)

    def wide(table):
        hi, lo = parts(table)
        return np.concatenate([hi, hi, lo], axis=1)

    return tall(ahead), wide(back), wide(ahead), tall(back)


def dot(a, b):
    return jnp.dot(a, b, preferred_element_type=F32)


def probe_kernel(half, near, far, coef, probe_r, probe_i):
    left = triple(coef[...], 1)
    skip = far.shape[0] - ROWS
    for source, base, skip in ((near, half[0] * ROWS, 0), (far, (1 - half[0]) * ROWS, skip)):

        def rows(y, _):
            m = source[skip + y]
            h = m.astype(BF16).astype(F32)
            right = jnp.concatenate([h, h, m - h], axis=0).astype(BF16)
            out = dot(left, right)
            start = (base + y) * LEAD
            probe_r[pl.ds(start, PMAX), :] = out[:, :PS]
            probe_i[pl.ds(start, PMAX), :] = out[:, PS:]
            return 0

        lax.fori_loop(0, ROWS, rows, 0, unroll=8)


def wave_kernel(
    half, offs, ext, photons, probe_r, probe_i, coef, ahead_t, back_w, ahead_w, back_t,
    up, mid, down, out_r, out_i, out_p, near, far,
    acc_rl, acc_rh, acc_il, acc_ih, acc_pl, acc_ph,
    patches, wave, field, cross_r, cross_i, power, sems,
):
    step = pl.program_id(0)
    lane = lax.broadcasted_iota(jnp.int32, (PS, PS), 1)
    sums = ((acc_rl, acc_rh), (acc_il, acc_ih), (acc_pl, acc_ph))

    @pl.when(step == 0)
    def _():
        for low, high in sums:
            low[...] = jnp.zeros_like(low)
            high[...] = jnp.zeros_like(high)

    def own_lanes(left):
        return (lane < left + MARGIN) & (lane >= left - MARGIN)

    def regroup(x):
        top = jnp.concatenate([x[:PS, :PS], x[PS:, :PS]], axis=1)
        low = jnp.concatenate([x[:PS, PS:], x[PS:, PS:]], axis=1)
        return jnp.concatenate([top, low], axis=0)

    def take(j, q):
        p = 2 * PAIRS * step + 2 * j + q
        return (
            probe_r[pl.ds(p, PS, stride=LEAD), :],
            probe_i[pl.ds(p, PS, stride=LEAD), :],
            patches[2 * j + q, 0],
            patches[2 * j + q, 1],
        )

    def cut(j, q):
        p = 2 * PAIRS * step + 2 * j + q
        top = offs[p, 0]
        left = offs[p, 1]
        turn = (PS + MARGIN - left) & (PS - 1)
        inside = own_lanes(left)
        total = None
        for c in range(2):
            patch = jnp.where(
                inside, ext[c, 0, pl.ds(top, PS), :], ext[c, 1, pl.ds(top, PS), :]
            )
            patch = pltpu.roll(patch, turn, 1)
            patches[2 * j + q, c] = patch
            total = patch * patch if total is None else total + patch * patch
        power[pl.ds(p, PS, stride=LEAD), :] = total

    def start(j):
        for q in range(2):
            cut(j, q)
            pr, pi, obj_r, obj_i = take(j, q)
            rows = slice(q * PS, (q + 1) * PS)
            wave[j, rows, :PS] = pr * obj_r - pi * obj_i
            wave[j, rows, PS:] = pr * obj_i + pi * obj_r

    def correct(j, there):
        count = jnp.concatenate([photons[2 * j], photons[2 * j + 1]], axis=1).astype(F32)
        far_r = there[:PS]
        far_i = there[PS:]
        size = jnp.maximum(far_r * far_r + far_i * far_i, 0.25)
        scale = count * lax.rsqrt(jnp.maximum(count * size, 0.0625)) * 0.03125
        return jnp.concatenate([far_r * scale, far_i * scale], axis=0)

    def finish(j):
        for q in range(2):
            p = 2 * PAIRS * step + 2 * j + q
            top = offs[p, 0]
            left = offs[p, 1]
            turn = (left + MARGIN) & (PS - 1)
            inside = own_lanes(left)
            rows = slice(q * PS, (q + 1) * PS)
            diff_r = field[j, rows, :PS]
            diff_i = field[j, rows, PS:]
            pr, pi, obj_r, obj_i = take(j, q)
            cross_r[pl.ds(p, PS, stride=LEAD), :] = obj_r * diff_r + obj_i * diff_i
            cross_i[pl.ds(p, PS, stride=LEAD), :] = obj_r * diff_i - obj_i * diff_r
            pieces = (
                pr * diff_r + pi * diff_i,
                pr * diff_i - pi * diff_r,
                pr * pr + pi * pi,
            )
            for (low, high), piece in zip(sums, pieces):
                turned = pltpu.roll(piece, turn, 1)
                near = jnp.where(inside, turned, 0.0)
                low[pl.ds(top, PS), :] += near
                high[pl.ds(top, PS), :] += turned - near

    pairs = range(PAIRS)
    for j in pairs:
        start(j)
    x = [dot(triple(wave[j], 1), ahead_t[...]) for j in pairs]
    x = [dot(back_w[...], triple(regroup(x[j]), 0)) for j in pairs]
    x = [correct(j, x[j]) for j in pairs]
    x = [dot(ahead_w[...], triple(x[j], 0)) for j in pairs]
    for j in pairs:
        field[j] = dot(triple(regroup(x[j]), 1), back_t[...]) - wave[j]
    for j in pairs:
        finish(j)

    @pl.when(step == PMAX // (2 * PAIRS) - 1)
    def _():
        width = up.shape[1]
        moves = [(cross_r, out_r), (cross_i, out_i), (power, out_p)]
        for i, piece in enumerate((acc_rl, acc_il, acc_pl, acc_rh, acc_ih, acc_ph)):
            moves.append((piece.at[:width], down.at[i]))
            moves.append((piece.at[EXT - width:], up.at[i]))
            if width < PS:
                moves.append((piece.at[width : EXT - width], mid.at[i]))
        copies = [
            pltpu.make_async_copy(source, target, sems.at[i])
            for i, (source, target) in enumerate(moves)
        ]
        for copy in copies:
            copy.start()

        def stacked(x):
            hi, lo = split(x.T)
            zero = jnp.zeros_like(hi)
            return jnp.concatenate(
                [jnp.concatenate([hi, hi], axis=1), jnp.concatenate([lo, zero], axis=1)], axis=0
            )

        left = stacked(coef[...])
        left_square = stacked(coef[...] * coef[...])
        for target, base in ((near, half[0] * ROWS), (far, (1 - half[0]) * ROWS)):

            def rows(y, _):
                begin = (base + y) * LEAD
                pair = jnp.concatenate(
                    [cross_r[pl.ds(begin, PMAX), :], cross_i[pl.ds(begin, PMAX), :]], axis=1
                )
                h, l = split(pair)
                out = dot(left, jnp.concatenate([h, l], axis=0))
                target[y, :, : 2 * PS] = out[:MODES] + out[MODES:]
                h, l = split(power[pl.ds(begin, PMAX), :])
                out = dot(left_square, jnp.concatenate([h, l], axis=0))
                target[y, :, 2 * PS:] = out[:MODES] + out[MODES:]
                return 0

            lax.fori_loop(0, ROWS, rows, 0, unroll=8)
        for copy in copies:
            copy.wait()


CHUNK = 16


def coef_kernel(cross_r, cross_i, powers, modes, coef, out, num, den):
    step = pl.program_id(0)

    @pl.when(step == 0)
    def _():
        num[...] = jnp.zeros_like(num)
        den[...] = jnp.zeros_like(den)

    dims = (((1,), (1,)), ((), ()))

    def wide_dot(a, b):
        return lax.dot_general(a, b, dims, preferred_element_type=F32)

    top = jnp.zeros((PMAX, MODES), F32)
    low = jnp.zeros((PMAX, MODES), F32)
    for y in range(CHUNK):
        rows = slice(y * LEAD, y * LEAD + PMAX)
        cross = jnp.concatenate([cross_r[rows, :], cross_i[rows, :]], axis=1)
        m = modes[y]
        power = m[:, :PS] * m[:, :PS] + m[:, PS:] * m[:, PS:]
        h, l = split(m)
        top += wide_dot(triple(cross, 1), jnp.concatenate([h, h, l], axis=1))
        h, l = split(power)
        low += wide_dot(triple(powers[rows, :], 1), jnp.concatenate([h, h, l], axis=1))
    num[...] += top
    den[...] += low

    @pl.when(step == PS // CHUNK - 1)
    def _():
        out[...] = coef[...] + num[...] / (den[...] + 1.0)


def update_kernel(got, mine, new, copies):
    total = jnp.sum(got[...], axis=0)
    power = total[:, 2 * PS:] + 1.0
    row = mine[...] + total[:, : 2 * PS] / jnp.concatenate([power, power], axis=1)
    new[...] = row
    copies[...] = jnp.broadcast_to(row[None], copies.shape)


SMEM = pl.BlockSpec(memory_space=pltpu.SMEM)
VMEM = pl.BlockSpec(memory_space=pltpu.VMEM)


def mix_probes(half, near, far, coef):
    grid = jax.ShapeDtypeStruct((PS * LEAD, PS), F32)
    return pl.pallas_call(
        probe_kernel,
        out_shape=(grid, grid),
        in_specs=[SMEM, VMEM, VMEM, VMEM],
        out_specs=(VMEM, VMEM),
        compiler_params=pltpu.CompilerParams(vmem_limit_bytes=2 << 20),
        name="probes",
    )(half, near, far, coef)


def waves(half, offs, ext, photons, probe_r, probe_i, coef, tables, width):
    edge = pltpu.HBM((6, width, PS), F32)
    inner = pltpu.HBM((6, max(EXT - 2 * width, 8), PS), F32)
    grid = pltpu.HBM((PS * LEAD, PS), F32)
    rows = jax.ShapeDtypeStruct((ROWS, MODES, 3 * PS), F32)
    square = pltpu.VMEM((PAIRS, 2 * PS, 2 * PS), F32)
    return pl.pallas_call(
        wave_kernel,
        grid=(PMAX // (2 * PAIRS),),
        out_shape=(edge, inner, edge, *[grid] * 3, rows, rows),
        in_specs=[
            SMEM,
            SMEM,
            VMEM,
            pl.BlockSpec((2 * PAIRS, PS, PS), lambda i: (i, 0, 0)),
            VMEM,
            VMEM,
            VMEM,
            *[VMEM] * len(tables),
        ],
        out_specs=(*[pl.BlockSpec(memory_space=pltpu.HBM)] * 6, VMEM, VMEM),
        scratch_shapes=[
            *[pltpu.VMEM((EXT, PS), F32)] * 6,
            pltpu.VMEM((2 * PAIRS, 2, PS, PS), F32),
            square,
            square,
            *[pltpu.VMEM((PS * LEAD, PS), F32)] * 3,
            pltpu.SemaphoreType.DMA((21,)),
        ],
        compiler_params=pltpu.CompilerParams(
            dimension_semantics=("arbitrary",), vmem_limit_bytes=24 << 20
        ),
        name="waves",
    )(half, offs, ext, photons, probe_r, probe_i, coef, *tables)


def new_coefficients(cross_r, cross_i, powers, modes, coef):
    rows = pl.BlockSpec((CHUNK * LEAD, PS), lambda i: (i, 0))
    whole = pl.BlockSpec((PMAX, MODES), lambda i: (0, 0))
    return pl.pallas_call(
        coef_kernel,
        grid=(PS // CHUNK,),
        out_shape=jax.ShapeDtypeStruct((PMAX, MODES), F32),
        in_specs=[
            rows,
            rows,
            rows,
            pl.BlockSpec((CHUNK, MODES, 2 * PS), lambda i: (i, 0, 0)),
            whole,
        ],
        out_specs=whole,
        scratch_shapes=[pltpu.VMEM((PMAX, MODES), F32)] * 2,
        compiler_params=pltpu.CompilerParams(
            dimension_semantics=("arbitrary",), vmem_limit_bytes=56 << 20
        ),
        name="coefs",
    )(cross_r, cross_i, powers, modes, coef)


def update_row(got, mine):
    return pl.pallas_call(
        update_kernel,
        out_shape=(
            jax.ShapeDtypeStruct((MODES, 2 * PS), F32),
            jax.ShapeDtypeStruct((ROWS, MODES, 2 * PS), F32),
        ),
        in_specs=[VMEM, VMEM],
        out_specs=(VMEM, VMEM),
        compiler_params=pltpu.CompilerParams(vmem_limit_bytes=2 << 20),
        name="update",
    )(got, mine)


def shifted(x, move):
    rows, cols = lax.axis_size("row"), lax.axis_size("col")
    pairs = []
    for a in range(rows):
        for b in range(cols):
            c, d = a + move[0], b + move[1]
            if 0 <= c < rows and 0 <= d < cols:
                pairs.append((c * cols + d, a * cols + b))
    return lax.ppermute(x, ("row", "col"), pairs)


def by_side(low, high):
    lane = lax.broadcasted_iota(jnp.int32, low.shape, low.ndim - 1)
    return jnp.where(lane < MARGIN, low, high)


def extend(block):
    beside = by_side(shifted(block, (0, 1)), shifted(block, (0, -1)))
    both = jnp.stack([block, beside], axis=1)
    above = shifted(both[:, :, -MARGIN:], (-1, 0))
    below = shifted(both[:, :, :MARGIN], (1, 0))
    return jnp.concatenate([above, both, below], axis=2)


def sum_rows(up, down):
    low = down + shifted(up, (-1, 0))
    high = up + shifted(down, (1, 0))
    return jnp.concatenate([low, high], axis=1)


def sum_columns(full):
    own, beside = full[:3], full[3:]
    from_left = shifted(by_side(beside, own), (0, -1))
    from_right = shifted(by_side(own, beside), (0, 1))
    own = own + by_side(from_left, from_right)
    beside = beside + by_side(from_right, from_left)
    return jnp.stack([own, beside], axis=1)


def inside_object():
    a, b = lax.axis_index("row"), lax.axis_index("col")
    place = a * TILE - MARGIN + lax.iota(jnp.int32, EXT)
    rows = (place >= 0) & (place < lax.axis_size("row") * TILE)
    lane = lax.iota(jnp.int32, PS)
    beside = ((lane < MARGIN) & (b < lax.axis_size("col") - 1)) | ((lane >= MARGIN) & (b > 0))
    cols = jnp.stack([jnp.ones_like(beside), beside])
    return rows[None, :, None] & cols[:, None, :]


def fold(up, mid, down):
    edges = jnp.concatenate([shifted(up, (-1, 0)), shifted(down, (1, 0))], axis=1)
    mid = mid + edges
    beside = mid[3:]
    return mid[:3] + by_side(shifted(beside, (0, -1)), shifted(beside, (0, 1)))


def shards(object_field, probe_modes, coefficients, offsets, counts, measured):
    tables = tuple(jnp.asarray(t) for t in dft_constants())
    offs = offsets[0, 0]
    photons = measured[0, 0]
    coef = coefficients[0, 0]
    live = (lax.iota(jnp.int32, PMAX) < counts[0, 0]).astype(F32)[:, None]
    rows, cols = lax.axis_size("row"), lax.axis_size("col")
    core = lax.axis_index("row") % 2
    half = core.reshape(1)
    groups = [[a * cols + b for a in range(k, rows, 2) for b in range(cols)] for k in range(2)]
    mates = [(a, a ^ 1) for a in range(rows)]
    place = lax.axis_index("row") // 2 * cols + lax.axis_index("col")

    def exchange(x):
        return lax.all_to_all(x, ("row", "col"), 0, 0, axis_index_groups=groups, tiled=True)

    modes = probe_modes.transpose(2, 0, 1, 3).reshape(PS, MODES, 2 * PS)
    mine = lax.dynamic_index_in_dim(modes, core * ROWS + place, 0, keepdims=False)
    ext = extend(object_field)
    for iteration in range(ITERS):
        final = iteration == ITERS - 1
        used = coef * live
        if iteration == 0:
            probe_r, probe_i = mix_probes(jnp.zeros_like(half), modes, modes, used)
        else:
            probe_r, probe_i = mix_probes(half, near, far, used)
        up, mid, down, cross_r, cross_i, powers, kept, given = waves(
            half, offs, ext, photons, probe_r, probe_i, used, tables, MARGIN if final else PS
        )
        sent = kept + lax.ppermute(given, "row", mates)
        got = exchange(sent)
        coef = new_coefficients(cross_r, cross_i, powers, modes, coef)
        got, coef = lax.optimization_barrier((got, coef))
        mine, copies = update_row(got, mine)
        if not final:
            full, copies = lax.optimization_barrier((sum_rows(up, down), copies))
        near = exchange(copies)
        far = lax.ppermute(near, "row", mates)
        modes = jnp.where(
            core == 0, jnp.concatenate([near, far]), jnp.concatenate([far, near])
        )
        if final:
            total = fold(up, mid, down)
            object_field = ext[:, 0, MARGIN:-MARGIN] + total[0:2] / (total[2:3] + 1.0)
        else:
            total = sum_columns(full)
            step = total[0:2] / (total[2:3] + 1.0)
            ext = ext + jnp.where(inside_object()[None], step, 0.0)
    probe_modes = modes.reshape(PS, MODES, 2, PS).transpose(1, 2, 0, 3)
    return (object_field, probe_modes, coef[None, None])


def solution(mesh):
    placed = (
        P(None, "row", "col"),
        P(),
        P("row", "col", None, None),
        P("row", "col", None, None),
        P("row", "col"),
        P("row", "col", None, None, None),
    )
    return jax.shard_map(
        shards,
        mesh=mesh,
        in_specs=placed,
        out_specs=(P(None, "row", "col"), P(), P("row", "col", None, None)),
        check_vma=False,
    )
```

```python
import functools
import math

import jax
import jax.numpy as jnp
import numpy as np
from jax import lax
from jax.experimental import pallas as pl
from jax.experimental.pallas import tpu as pltpu
from jax.sharding import PartitionSpec as P

PS = 128
MODES = 8
TILE = 128
PMAX = 32
ITERS = 2
EXT = TILE + PS
F32 = jnp.float32
BF16 = jnp.bfloat16
PAIRS = 4
LEAD = 33
ROWS = PS // 2
MARGIN = PS // 2


def split(x):
    hi = x.astype(BF16)
    lo = (x - hi.astype(F32)).astype(BF16)
    return hi, lo


def triple(x, axis):
    hi, lo = split(x)
    return jnp.concatenate([hi, lo, hi], axis=axis)


def dft_constants():
    ramp = np.arange(PS)
    angles = (ramp[:, None] * ramp[None, :] % PS) * (2.0 * math.pi / PS)
    cos = np.cos(angles) / math.sqrt(PS)
    sin = -np.sin(angles) / math.sqrt(PS)
    ahead = np.block([[cos, sin], [-sin, cos]])
    back = np.block([[cos, -sin], [sin, cos]])

    def parts(table):
        table = table.astype(np.float32)
        hi = table.astype(jnp.bfloat16)
        lo = (table - hi.astype(np.float32)).astype(jnp.bfloat16)
        return hi, lo

    def tall(table):
        hi, lo = parts(table)
        return np.concatenate([hi, hi, lo], axis=0)

    def wide(table):
        hi, lo = parts(table)
        return np.concatenate([hi, hi, lo], axis=1)

    return tall(ahead), wide(back), wide(ahead), tall(back)


def dot(a, b):
    return jnp.dot(a, b, preferred_element_type=F32)


def live_only(coef, counts):
    slot = lax.broadcasted_iota(jnp.int32, coef.shape, 1)
    return jnp.where(slot < counts[0, 0], coef[...], 0.0)


def probe_kernel(base, counts, modes, coef, *refs):
    probe_r, probe_i = refs[-2:]
    left = triple(live_only(coef, counts).T, 1)

    def rows(y, _):
        m = modes[y]
        h = m.astype(BF16).astype(F32)
        right = jnp.concatenate([h, h, m - h], axis=0).astype(BF16)
        out = dot(left, right)
        start = (base[0] + y) * LEAD
        probe_r[pl.ds(start, PMAX), :] = out[:, :PS]
        probe_i[pl.ds(start, PMAX), :] = out[:, PS:]
        return 0

    lax.fori_loop(0, modes.shape[0], rows, 0, unroll=8)


def wave_kernel(half, counts, offs, *refs):
    (
        photons, probe_r, probe_i, coef, ahead_t, back_w, ahead_w, back_t,
        up, mid, down, out_r, out_i, out_p, near, far,
        acc_rl, acc_rh, acc_il, acc_ih, acc_pl, acc_ph,
        patches, wave, field, cross_r, cross_i, power, sems, ext,
    ) = refs[-30:]
    pieces = refs[:-30]
    step = pl.program_id(0)
    lane = lax.broadcasted_iota(jnp.int32, (PS, PS), 1)
    if len(pieces) == 1:
        ext = pieces[0]
    sums = ((acc_rl, acc_rh), (acc_il, acc_ih), (acc_pl, acc_ph))

    @pl.when(step == 0)
    def _():
        if len(pieces) == 3:
            row = 0
            for piece in pieces:
                ext[:, :, row : row + piece.shape[2]] = piece[...]
                row += piece.shape[2]
        for low, high in sums:
            low[...] = jnp.zeros_like(low)
            high[...] = jnp.zeros_like(high)

    def own_lanes(left):
        return (lane < left + MARGIN) & (lane >= left - MARGIN)

    def regroup(x):
        top = jnp.concatenate([x[:PS, :PS], x[PS:, :PS]], axis=1)
        low = jnp.concatenate([x[:PS, PS:], x[PS:, PS:]], axis=1)
        return jnp.concatenate([top, low], axis=0)

    def take(j, q):
        p = 2 * PAIRS * step + 2 * j + q
        return (
            probe_r[pl.ds(p, PS, stride=LEAD), :],
            probe_i[pl.ds(p, PS, stride=LEAD), :],
            patches[2 * j + q, 0],
            patches[2 * j + q, 1],
        )

    def cut(j, q):
        p = 2 * PAIRS * step + 2 * j + q
        top = offs[0, p]
        left = offs[1, p]
        turn = (PS + MARGIN - left) & (PS - 1)
        inside = own_lanes(left)
        total = None
        for c in range(2):
            patch = jnp.where(
                inside, ext[c, 0, pl.ds(top, PS), :], ext[c, 1, pl.ds(top, PS), :]
            )
            patch = pltpu.roll(patch, turn, 1)
            patches[2 * j + q, c] = patch
            total = patch * patch if total is None else total + patch * patch
        power[pl.ds(p, PS, stride=LEAD), :] = total

    def start(j):
        for q in range(2):
            cut(j, q)
            pr, pi, obj_r, obj_i = take(j, q)
            rows = slice(q * PS, (q + 1) * PS)
            wave[j, rows, :PS] = pr * obj_r - pi * obj_i
            wave[j, rows, PS:] = pr * obj_i + pi * obj_r

    def correct(j, there):
        count = jnp.concatenate([photons[2 * j], photons[2 * j + 1]], axis=1).astype(F32)
        far_r = there[:PS]
        far_i = there[PS:]
        size = jnp.maximum(far_r * far_r + far_i * far_i, 0.25)
        scale = count * lax.rsqrt(jnp.maximum(count * size, 0.0625)) * 0.03125
        return jnp.concatenate([far_r * scale, far_i * scale], axis=0)

    def finish(j):
        for q in range(2):
            p = 2 * PAIRS * step + 2 * j + q
            top = offs[0, p]
            left = offs[1, p]
            turn = (left + MARGIN) & (PS - 1)
            inside = own_lanes(left)
            rows = slice(q * PS, (q + 1) * PS)
            diff_r = field[j, rows, :PS]
            diff_i = field[j, rows, PS:]
            pr, pi, obj_r, obj_i = take(j, q)
            cross_r[pl.ds(p, PS, stride=LEAD), :] = obj_r * diff_r + obj_i * diff_i
            cross_i[pl.ds(p, PS, stride=LEAD), :] = obj_r * diff_i - obj_i * diff_r
            pieces = (
                pr * diff_r + pi * diff_i,
                pr * diff_i - pi * diff_r,
                pr * pr + pi * pi,
            )
            for (low, high), piece in zip(sums, pieces):
                turned = pltpu.roll(piece, turn, 1)
                near = jnp.where(inside, turned, 0.0)
                low[pl.ds(top, PS), :] += near
                high[pl.ds(top, PS), :] += turned - near

    pairs = range(PAIRS)
    for j in pairs:
        start(j)
    x = [dot(triple(wave[j], 1), ahead_t[...]) for j in pairs]
    x = [dot(back_w[...], triple(regroup(x[j]), 0)) for j in pairs]
    x = [correct(j, x[j]) for j in pairs]
    x = [dot(ahead_w[...], triple(x[j], 0)) for j in pairs]
    for j in pairs:
        field[j] = dot(triple(regroup(x[j]), 1), back_t[...]) - wave[j]
    for j in pairs:
        finish(j)

    @pl.when(step == PMAX // (2 * PAIRS) - 1)
    def _():
        width = up.shape[1]
        moves = [(cross_r, out_r), (cross_i, out_i), (power, out_p)]
        for i, piece in enumerate((acc_rl, acc_il, acc_pl, acc_rh, acc_ih, acc_ph)):
            moves.append((piece.at[:width], down.at[i]))
            moves.append((piece.at[EXT - width:], up.at[i]))
            if width < PS:
                moves.append((piece.at[width : EXT - width], mid.at[i]))
        copies = [
            pltpu.make_async_copy(source, target, sems.at[i])
            for i, (source, target) in enumerate(moves)
        ]
        for copy in copies:
            copy.start()

        def stacked(x):
            hi, lo = split(x)
            zero = jnp.zeros_like(hi)
            return jnp.concatenate(
                [jnp.concatenate([hi, hi], axis=1), jnp.concatenate([lo, zero], axis=1)], axis=0
            )

        used = live_only(coef, counts)
        left = stacked(used)
        left_square = stacked(used * used)
        for target, base in ((near, half[0] * ROWS), (far, (1 - half[0]) * ROWS)):

            def rows(y, _):
                begin = (base + y) * LEAD
                pair = jnp.concatenate(
                    [cross_r[pl.ds(begin, PMAX), :], cross_i[pl.ds(begin, PMAX), :]], axis=1
                )
                h, l = split(pair)
                out = dot(left, jnp.concatenate([h, l], axis=0))
                target[y, :, : 2 * PS] = out[:MODES] + out[MODES:]
                h, l = split(power[pl.ds(begin, PMAX), :])
                out = dot(left_square, jnp.concatenate([h, l], axis=0))
                target[y, :, 2 * PS:] = out[:MODES] + out[MODES:]
                return 0

            lax.fori_loop(0, ROWS, rows, 0, unroll=8)
        for copy in copies:
            copy.wait()


CHUNK = 16


def coef_kernel(cross_r, cross_i, powers, modes, coef, out, num, den):
    step = pl.program_id(0)

    @pl.when(step == 0)
    def _():
        num[...] = jnp.zeros_like(num)
        den[...] = jnp.zeros_like(den)

    dims = (((1,), (1,)), ((), ()))

    def wide_dot(a, b):
        return lax.dot_general(a, b, dims, preferred_element_type=F32)

    top = jnp.zeros((PMAX, MODES), F32)
    low = jnp.zeros((PMAX, MODES), F32)
    for y in range(CHUNK):
        rows = slice(y * LEAD, y * LEAD + PMAX)
        cross = jnp.concatenate([cross_r[rows, :], cross_i[rows, :]], axis=1)
        m = modes[y]
        power = m[:, :PS] * m[:, :PS] + m[:, PS:] * m[:, PS:]
        h, l = split(m)
        top += wide_dot(triple(cross, 1), jnp.concatenate([h, h, l], axis=1))
        h, l = split(power)
        low += wide_dot(triple(powers[rows, :], 1), jnp.concatenate([h, h, l], axis=1))
    num[...] += top
    den[...] += low

    @pl.when(step == PS // CHUNK - 1)
    def _():
        out[...] = coef[...] + (num[...] / (den[...] + 1.0)).T


def update_kernel(got, mine, new, copies):
    total = jnp.sum(got[...], axis=0)
    power = total[:, 2 * PS:] + 1.0
    row = mine[...] + total[:, : 2 * PS] / jnp.concatenate([power, power], axis=1)
    new[...] = row
    copies[...] = jnp.broadcast_to(row[None], copies.shape)


def beside_kernel(block, right, left, both, first, last):
    lane = lax.broadcasted_iota(jnp.int32, (PS, PS), 1)
    for c in range(2):
        beside = jnp.where(lane < MARGIN, right[c], left[c])
        for i, plane in ((0, block[c]), (1, beside)):
            both[c, i] = plane
            first[c, i] = plane[:MARGIN]
            last[c, i] = plane[MARGIN:]


def rows_kernel(up, down, from_above, from_below, full, to_right, to_left):
    lane = lax.broadcasted_iota(jnp.int32, (PS, PS), 1)
    for c in range(3):
        for rows, own, other in ((slice(0, PS), down, from_above), (slice(PS, EXT), up, from_below)):
            centre = own[c] + other[c]
            beside = own[3 + c] + other[3 + c]
            full[c, rows] = centre
            full[3 + c, rows] = beside
            to_right[c, rows] = jnp.where(lane < MARGIN, beside, centre)
            to_left[c, rows] = jnp.where(lane < MARGIN, centre, beside)


SMEM = pl.BlockSpec(memory_space=pltpu.SMEM)
VMEM = pl.BlockSpec(memory_space=pltpu.VMEM)


def mix_probes(base, counts, modes, coef, *before):
    grid = jax.ShapeDtypeStruct((PS * LEAD, PS), F32)
    return pl.pallas_call(
        probe_kernel,
        out_shape=(grid, grid),
        in_specs=[SMEM, SMEM, VMEM, VMEM, *[VMEM] * len(before)],
        out_specs=(VMEM, VMEM),
        input_output_aliases={4: 0, 5: 1} if before else {},
        compiler_params=pltpu.CompilerParams(vmem_limit_bytes=2 << 20),
        name="probes",
    )(base, counts, modes, coef, *before)


def sum_rows(up, down):
    side = jax.ShapeDtypeStruct((3, EXT, PS), F32)
    return pl.pallas_call(
        rows_kernel,
        out_shape=(jax.ShapeDtypeStruct((6, EXT, PS), F32), side, side),
        in_specs=[VMEM] * 4,
        out_specs=(VMEM,) * 3,
        compiler_params=pltpu.CompilerParams(vmem_limit_bytes=2 << 20),
        name="rows",
    )(up, down, shifted(up, (-1, 0)), shifted(down, (1, 0)))


def waves(half, counts, offs, pieces, photons, probe_r, probe_i, coef, tables, width):
    edge = pltpu.HBM((6, width, PS), F32)
    inner = pltpu.HBM((6, max(EXT - 2 * width, 8), PS), F32)
    grid = pltpu.HBM((PS * LEAD, PS), F32)
    rows = jax.ShapeDtypeStruct((ROWS, MODES, 3 * PS), F32)
    square = pltpu.VMEM((PAIRS, 2 * PS, 2 * PS), F32)
    return pl.pallas_call(
        wave_kernel,
        grid=(PMAX // (2 * PAIRS),),
        out_shape=(edge, inner, edge, *[grid] * 3, rows, rows),
        in_specs=[
            SMEM,
            SMEM,
            SMEM,
            *[VMEM] * len(pieces),
            pl.BlockSpec((2 * PAIRS, PS, PS), lambda i: (i, 0, 0)),
            VMEM,
            VMEM,
            VMEM,
            *[VMEM] * len(tables),
        ],
        out_specs=(*[pl.BlockSpec(memory_space=pltpu.HBM)] * 6, VMEM, VMEM),
        scratch_shapes=[
            *[pltpu.VMEM((EXT, PS), F32)] * 6,
            pltpu.VMEM((2 * PAIRS, 2, PS, PS), F32),
            square,
            square,
            *[pltpu.VMEM((PS * LEAD, PS), F32)] * 3,
            pltpu.SemaphoreType.DMA((21,)),
            pltpu.VMEM((2, 2, EXT, PS), F32),
        ],
        compiler_params=pltpu.CompilerParams(
            dimension_semantics=("arbitrary",), vmem_limit_bytes=24 << 20
        ),
        name="waves",
    )(half, counts, offs, *pieces, photons, probe_r, probe_i, coef, *tables)


def new_coefficients(cross_r, cross_i, powers, modes, coef):
    rows = pl.BlockSpec((CHUNK * LEAD, PS), lambda i: (i, 0))
    whole = pl.BlockSpec((MODES, PMAX), lambda i: (0, 0))
    return pl.pallas_call(
        coef_kernel,
        grid=(PS // CHUNK,),
        out_shape=jax.ShapeDtypeStruct((MODES, PMAX), F32),
        in_specs=[
            rows,
            rows,
            rows,
            pl.BlockSpec((CHUNK, MODES, 2 * PS), lambda i: (i, 0, 0)),
            whole,
        ],
        out_specs=whole,
        scratch_shapes=[pltpu.VMEM((PMAX, MODES), F32)] * 2,
        compiler_params=pltpu.CompilerParams(
            dimension_semantics=("arbitrary",), vmem_limit_bytes=56 << 20
        ),
        name="coefs",
    )(cross_r, cross_i, powers, modes, coef)


def update_row(got, mine):
    return pl.pallas_call(
        update_kernel,
        out_shape=(
            jax.ShapeDtypeStruct((MODES, 2 * PS), F32),
            jax.ShapeDtypeStruct((ROWS, MODES, 2 * PS), F32),
        ),
        in_specs=[VMEM, VMEM],
        out_specs=(VMEM, VMEM),
        compiler_params=pltpu.CompilerParams(vmem_limit_bytes=2 << 20),
        name="update",
    )(got, mine)


def shifted(x, move):
    rows, cols = lax.axis_size("row"), lax.axis_size("col")
    pairs = []
    for a in range(rows):
        for b in range(cols):
            c, d = a + move[0], b + move[1]
            if 0 <= c < rows and 0 <= d < cols:
                pairs.append((c * cols + d, a * cols + b))
    return lax.ppermute(x, ("row", "col"), pairs)


def by_side(low, high):
    lane = lax.broadcasted_iota(jnp.int32, low.shape, low.ndim - 1)
    return jnp.where(lane < MARGIN, low, high)


def extend(block):
    strip = jax.ShapeDtypeStruct((2, 2, MARGIN, PS), F32)
    both, first, last = pl.pallas_call(
        beside_kernel,
        out_shape=(jax.ShapeDtypeStruct((2, 2, PS, PS), F32), strip, strip),
        in_specs=[VMEM] * 3,
        out_specs=(VMEM,) * 3,
        compiler_params=pltpu.CompilerParams(vmem_limit_bytes=2 << 20),
        name="beside",
    )(block, shifted(block, (0, 1)), shifted(block, (0, -1)))
    return shifted(last, (-1, 0)), both, shifted(first, (1, 0))


def sum_columns(full, from_left, from_right):
    own = full[:3] + by_side(from_left, from_right)
    beside = full[3:] + by_side(from_right, from_left)
    return jnp.stack([own, beside], axis=1)


def inside_object():
    a, b = lax.axis_index("row"), lax.axis_index("col")
    place = a * TILE - MARGIN + lax.iota(jnp.int32, EXT)
    rows = (place >= 0) & (place < lax.axis_size("row") * TILE)
    lane = lax.iota(jnp.int32, PS)
    beside = ((lane < MARGIN) & (b < lax.axis_size("col") - 1)) | ((lane >= MARGIN) & (b > 0))
    cols = jnp.stack([jnp.ones_like(beside), beside])
    return rows[None, :, None] & cols[:, None, :]


def fold(up, mid, down):
    edges = jnp.concatenate([shifted(up, (-1, 0)), shifted(down, (1, 0))], axis=1)
    mid = mid + edges
    beside = mid[3:]
    return mid[:3] + by_side(shifted(beside, (0, -1)), shifted(beside, (0, 1)))


def shards(object_field, probe_modes, coefficients, offsets, counts, measured):
    tables = tuple(jnp.asarray(t) for t in dft_constants())
    offs = offsets[0, 0].T
    photons = measured[0, 0]
    coef = coefficients[0, 0].T
    rows, cols = lax.axis_size("row"), lax.axis_size("col")
    core = lax.axis_index("row") % 2
    half = core.reshape(1)
    groups = [[a * cols + b for a in range(k, rows, 2) for b in range(cols)] for k in range(2)]
    mates = [(a, a ^ 1) for a in range(rows)]
    place = lax.axis_index("row") // 2 * cols + lax.axis_index("col")

    def exchange(x):
        return lax.all_to_all(x, ("row", "col"), 0, 0, axis_index_groups=groups, tiled=True)

    modes = probe_modes.transpose(2, 0, 1, 3).reshape(PS, MODES, 2 * PS)
    mine = lax.dynamic_index_in_dim(modes, core * ROWS + place, 0, keepdims=False)
    pieces = extend(object_field)
    ext = jnp.concatenate(pieces, axis=2)
    for iteration in range(ITERS):
        final = iteration == ITERS - 1
        if iteration == 0:
            probe_r, probe_i = mix_probes(jnp.zeros_like(half), counts, modes, coef)
        else:
            probe_r, probe_i = mix_probes(half * ROWS, counts, near, coef)
            probe_r, probe_i = mix_probes((1 - half) * ROWS, counts, far, coef, probe_r, probe_i)
        up, mid, down, cross_r, cross_i, powers, kept, given = waves(
            half, counts, offs, pieces, photons, probe_r, probe_i, coef, tables, MARGIN if final else PS
        )
        sent = kept + lax.ppermute(given, "row", mates)
        got = exchange(sent)
        if final:
            coef = new_coefficients(cross_r, cross_i, powers, modes, coef)
            got, coef = lax.optimization_barrier((got, coef))
            mine, copies = update_row(got, mine)
        else:
            full, to_right, to_left = sum_rows(up, down)
            from_left = shifted(to_right, (0, -1))
            from_right = shifted(to_left, (0, 1))
            got, full = lax.optimization_barrier((got, full))
            mine, copies = update_row(got, mine)
            copies, cross_r = lax.optimization_barrier((copies, cross_r))
            coef = new_coefficients(cross_r, cross_i, powers, modes, coef)
        near = exchange(copies)
        far = lax.ppermute(near, "row", mates)
        modes = jnp.where(
            core == 0, jnp.concatenate([near, far]), jnp.concatenate([far, near])
        )
        if final:
            total = fold(up, mid, down)
            object_field = ext[:, 0, MARGIN:-MARGIN] + total[0:2] / (total[2:3] + 1.0)
        else:
            total = sum_columns(full, from_left, from_right)
            step = total[0:2] / (total[2:3] + 1.0)
            ext = ext + jnp.where(inside_object()[None], step, 0.0)
            pieces = (ext,)
    probe_modes = modes.reshape(PS, MODES, 2, PS).transpose(1, 2, 0, 3)
    return (object_field, probe_modes, coef.T[None, None])


def solution(mesh):
    placed = (
        P(None, "row", "col"),
        P(),
        P("row", "col", None, None),
        P("row", "col", None, None),
        P("row", "col"),
        P("row", "col", None, None, None),
    )
    return jax.shard_map(
        shards,
        mesh=mesh,
        in_specs=placed,
        out_specs=(P(None, "row", "col"), P(), P("row", "col", None, None)),
        check_vma=False,
    )
```

```python
import math

import jax
import jax.numpy as jnp
import numpy as np
from jax import lax
from jax.experimental import pallas as pl
from jax.experimental.pallas import tpu as pltpu
from jax.sharding import PartitionSpec as P

PS = 128
MODES = 8
TILE = 128
PMAX = 32
ITERS = 2
EXT = TILE + PS
F32 = jnp.float32
BF16 = jnp.bfloat16
PAIRS = 4
LEAD = 33
ROWS = PS // 2
MARGIN = PS // 2


def split(x):
    hi = x.astype(BF16)
    lo = (x - hi.astype(F32)).astype(BF16)
    return hi, lo


def triple(x, axis):
    hi, lo = split(x)
    return jnp.concatenate([hi, lo, hi], axis=axis)


def dft_constants():
    ramp = np.arange(PS)
    angles = (ramp[:, None] * ramp[None, :] % PS) * (2.0 * math.pi / PS)
    cos = np.cos(angles) / math.sqrt(PS)
    sin = -np.sin(angles) / math.sqrt(PS)
    parts = []
    for table in (np.block([[cos, sin], [-sin, cos]]), np.block([[cos, -sin], [sin, cos]])):
        table = table.astype(np.float32)
        hi = table.astype(jnp.bfloat16)
        parts += [hi, (table - hi.astype(np.float32)).astype(jnp.bfloat16)]
    return np.stack(parts)


def dot(a, b):
    return jnp.dot(a, b, preferred_element_type=F32)


def live_only(coef, counts):
    slot = lax.broadcasted_iota(jnp.int32, coef.shape, 1)
    return jnp.where(slot < counts[0, 0], coef[...], 0.0)


def probe_kernel(base, counts, modes, coef, *refs):
    probe_r, probe_i = refs[-2:]
    left = triple(live_only(coef, counts).T, 1)

    def rows(y, _):
        m = modes[y]
        h = m.astype(BF16).astype(F32)
        right = jnp.concatenate([h, h, m - h], axis=0).astype(BF16)
        out = dot(left, right)
        start = (base[0] + y) * LEAD
        probe_r[pl.ds(start, PMAX), :] = out[:, :PS]
        probe_i[pl.ds(start, PMAX), :] = out[:, PS:]
        return 0

    lax.fori_loop(0, modes.shape[0], rows, 0, unroll=8)


def wave_kernel(half, counts, offs, *refs):
    (
        photons, probe_r, probe_i, coef, tables,
        up, mid, down, out_r, out_i, out_p, near, far,
        acc_rl, acc_rh, acc_il, acc_ih, acc_pl, acc_ph,
        patches, wave, field, cross_r, cross_i, power, sems, ext,
    ) = refs[-27:]
    pieces = refs[:-27]
    step = pl.program_id(0)
    lane = lax.broadcasted_iota(jnp.int32, (PS, PS), 1)
    if len(pieces) == 1:
        ext = pieces[0]
    sums = ((acc_rl, acc_rh), (acc_il, acc_ih), (acc_pl, acc_ph))

    @pl.when(step == 0)
    def _():
        if len(pieces) == 3:
            row = 0
            for piece in pieces:
                ext[:, :, row : row + piece.shape[2]] = piece[...]
                row += piece.shape[2]
        for low, high in sums:
            low[...] = jnp.zeros_like(low)
            high[...] = jnp.zeros_like(high)

    def own_lanes(left):
        return (lane < left + MARGIN) & (lane >= left - MARGIN)

    def regroup(x):
        top = jnp.concatenate([x[:PS, :PS], x[PS:, :PS]], axis=1)
        low = jnp.concatenate([x[:PS, PS:], x[PS:, PS:]], axis=1)
        return jnp.concatenate([top, low], axis=0)

    def take(j, q):
        p = 2 * PAIRS * step + 2 * j + q
        return (
            probe_r[pl.ds(p, PS, stride=LEAD), :],
            probe_i[pl.ds(p, PS, stride=LEAD), :],
            patches[2 * j + q, 0],
            patches[2 * j + q, 1],
        )

    def cut(j, q):
        p = 2 * PAIRS * step + 2 * j + q
        top = offs[0, p]
        left = offs[1, p]
        turn = (PS + MARGIN - left) & (PS - 1)
        inside = own_lanes(left)
        total = None
        for c in range(2):
            patch = jnp.where(
                inside, ext[c, 0, pl.ds(top, PS), :], ext[c, 1, pl.ds(top, PS), :]
            )
            patch = pltpu.roll(patch, turn, 1)
            patches[2 * j + q, c] = patch
            total = patch * patch if total is None else total + patch * patch
        power[pl.ds(p, PS, stride=LEAD), :] = total

    def start(j):
        for q in range(2):
            cut(j, q)
            pr, pi, obj_r, obj_i = take(j, q)
            rows = slice(q * PS, (q + 1) * PS)
            wave[j, rows, :PS] = pr * obj_r - pi * obj_i
            wave[j, rows, PS:] = pr * obj_i + pi * obj_r

    def correct(j, there):
        count = jnp.concatenate([photons[2 * j], photons[2 * j + 1]], axis=1).astype(F32)
        far_r = there[:PS]
        far_i = there[PS:]
        size = jnp.maximum(far_r * far_r + far_i * far_i, 0.25)
        scale = count * lax.rsqrt(jnp.maximum(count * size, 0.0625)) * 0.03125
        return jnp.concatenate([far_r * scale, far_i * scale], axis=0)

    def finish(j):
        for q in range(2):
            p = 2 * PAIRS * step + 2 * j + q
            top = offs[0, p]
            left = offs[1, p]
            turn = (left + MARGIN) & (PS - 1)
            inside = own_lanes(left)
            rows = slice(q * PS, (q + 1) * PS)
            diff_r = field[j, rows, :PS]
            diff_i = field[j, rows, PS:]
            pr, pi, obj_r, obj_i = take(j, q)
            cross_r[pl.ds(p, PS, stride=LEAD), :] = obj_r * diff_r + obj_i * diff_i
            cross_i[pl.ds(p, PS, stride=LEAD), :] = obj_r * diff_i - obj_i * diff_r
            pieces = (
                pr * diff_r + pi * diff_i,
                pr * diff_i - pi * diff_r,
                pr * pr + pi * pi,
            )
            for (low, high), piece in zip(sums, pieces):
                turned = pltpu.roll(piece, turn, 1)
                near = jnp.where(inside, turned, 0.0)
                low[pl.ds(top, PS), :] += near
                high[pl.ds(top, PS), :] += turned - near

    def table(i, axis):
        hi = tables[2 * i]
        return jnp.concatenate([hi, hi, tables[2 * i + 1]], axis=axis)

    pairs = range(PAIRS)
    for j in pairs:
        start(j)
    x = [dot(triple(wave[j], 1), table(0, 0)) for j in pairs]
    x = [dot(table(1, 1), triple(regroup(x[j]), 0)) for j in pairs]
    x = [correct(j, x[j]) for j in pairs]
    x = [dot(table(0, 1), triple(x[j], 0)) for j in pairs]
    for j in pairs:
        field[j] = dot(triple(regroup(x[j]), 1), table(1, 0)) - wave[j]
    for j in pairs:
        finish(j)

    @pl.when(step == PMAX // (2 * PAIRS) - 1)
    def _():
        width = up.shape[1]
        moves = [(cross_r, out_r), (cross_i, out_i), (power, out_p)]
        for i, piece in enumerate((acc_rl, acc_il, acc_pl, acc_rh, acc_ih, acc_ph)):
            moves.append((piece.at[:width], down.at[i]))
            moves.append((piece.at[EXT - width:], up.at[i]))
            if width < PS:
                moves.append((piece.at[width : EXT - width], mid.at[i]))
        copies = [
            pltpu.make_async_copy(source, target, sems.at[i])
            for i, (source, target) in enumerate(moves)
        ]
        for copy in copies:
            copy.start()

        def stacked(x):
            hi, lo = split(x)
            zero = jnp.zeros_like(hi)
            return jnp.concatenate(
                [jnp.concatenate([hi, hi], axis=1), jnp.concatenate([lo, zero], axis=1)], axis=0
            )

        used = live_only(coef, counts)
        left = stacked(used)
        left_square = stacked(used * used)
        for target, base in ((near, half[0] * ROWS), (far, (1 - half[0]) * ROWS)):

            def rows(y, _):
                begin = (base + y) * LEAD
                pair = jnp.concatenate(
                    [cross_r[pl.ds(begin, PMAX), :], cross_i[pl.ds(begin, PMAX), :]], axis=1
                )
                h, l = split(pair)
                out = dot(left, jnp.concatenate([h, l], axis=0))
                target[y, :, : 2 * PS] = out[:MODES] + out[MODES:]
                h, l = split(power[pl.ds(begin, PMAX), :])
                out = dot(left_square, jnp.concatenate([h, l], axis=0))
                target[y, :, 2 * PS:] = out[:MODES] + out[MODES:]
                return 0

            lax.fori_loop(0, ROWS, rows, 0, unroll=8)
        for copy in copies:
            copy.wait()


CHUNK = 64


def coef_kernel(cross_r, cross_i, powers, modes, coef, out, num, den):
    step = pl.program_id(0)

    @pl.when(step == 0)
    def _():
        num[...] = jnp.zeros_like(num)
        den[...] = jnp.zeros_like(den)

    dims = (((1,), (1,)), ((), ()))

    def wide_dot(a, b):
        return lax.dot_general(a, b, dims, preferred_element_type=F32)

    top = jnp.zeros((PMAX, MODES), F32)
    low = jnp.zeros((PMAX, MODES), F32)
    for y in range(CHUNK):
        rows = slice(y * LEAD, y * LEAD + PMAX)
        cross = jnp.concatenate([cross_r[rows, :], cross_i[rows, :]], axis=1)
        m = modes[y]
        power = m[:, :PS] * m[:, :PS] + m[:, PS:] * m[:, PS:]
        h, l = split(m)
        top += wide_dot(triple(cross, 1), jnp.concatenate([h, h, l], axis=1))
        h, l = split(power)
        low += wide_dot(triple(powers[rows, :], 1), jnp.concatenate([h, h, l], axis=1))
    num[...] += top
    den[...] += low

    @pl.when(step == PS // CHUNK - 1)
    def _():
        out[...] = coef[...] + (num[...] / (den[...] + 1.0)).T


def update_kernel(got, mine, new, copies):
    total = jnp.sum(got[...], axis=0)
    power = total[:, 2 * PS:] + 1.0
    row = mine[...] + total[:, : 2 * PS] / jnp.concatenate([power, power], axis=1)
    new[...] = row
    copies[...] = jnp.broadcast_to(row[None], copies.shape)


def beside_kernel(block, right, left, both, first, last):
    lane = lax.broadcasted_iota(jnp.int32, (PS, PS), 1)
    for c in range(2):
        beside = jnp.where(lane < MARGIN, right[c], left[c])
        for i, plane in ((0, block[c]), (1, beside)):
            both[c, i] = plane
            first[c, i] = plane[:MARGIN]
            last[c, i] = plane[MARGIN:]


def rows_kernel(up, down, from_above, from_below, full, to_right, to_left):
    lane = lax.broadcasted_iota(jnp.int32, (PS, PS), 1)
    for c in range(3):
        for rows, own, other in ((slice(0, PS), down, from_above), (slice(PS, EXT), up, from_below)):
            centre = own[c] + other[c]
            beside = own[3 + c] + other[3 + c]
            full[c, rows] = centre
            full[3 + c, rows] = beside
            to_right[c, rows] = jnp.where(lane < MARGIN, beside, centre)
            to_left[c, rows] = jnp.where(lane < MARGIN, centre, beside)


def fold_kernel(mid, from_above, from_below, own, beside):
    for c in range(3):
        for target, plane in ((own, c), (beside, 3 + c)):
            target[c, :MARGIN] = mid[plane, :MARGIN] + from_above[plane]
            target[c, MARGIN:] = mid[plane, MARGIN:] + from_below[plane]


SMEM = pl.BlockSpec(memory_space=pltpu.SMEM)
VMEM = pl.BlockSpec(memory_space=pltpu.VMEM)


def mix_probes(base, counts, modes, coef, *before):
    grid = jax.ShapeDtypeStruct((PS * LEAD, PS), F32)
    return pl.pallas_call(
        probe_kernel,
        out_shape=(grid, grid),
        in_specs=[SMEM, SMEM, VMEM, VMEM, *[VMEM] * len(before)],
        out_specs=(VMEM, VMEM),
        input_output_aliases={4: 0, 5: 1} if before else {},
        compiler_params=pltpu.CompilerParams(vmem_limit_bytes=2 << 20),
        name="probes",
    )(base, counts, modes, coef, *before)


def sum_rows(up, down, from_above, from_below):
    side = jax.ShapeDtypeStruct((3, EXT, PS), F32)
    return pl.pallas_call(
        rows_kernel,
        out_shape=(jax.ShapeDtypeStruct((6, EXT, PS), F32), side, side),
        in_specs=[VMEM] * 4,
        out_specs=(VMEM,) * 3,
        compiler_params=pltpu.CompilerParams(vmem_limit_bytes=2 << 20),
        name="rows",
    )(up, down, from_above, from_below)


def waves(half, counts, offs, pieces, photons, probe_r, probe_i, coef, tables, width):
    edge = pltpu.HBM((6, width, PS), F32)
    inner = pltpu.HBM((6, max(EXT - 2 * width, 8), PS), F32)
    grid = pltpu.HBM((PS * LEAD, PS), F32)
    rows = jax.ShapeDtypeStruct((ROWS, MODES, 3 * PS), F32)
    square = pltpu.VMEM((PAIRS, 2 * PS, 2 * PS), F32)
    return pl.pallas_call(
        wave_kernel,
        grid=(PMAX // (2 * PAIRS),),
        out_shape=(edge, inner, edge, *[grid] * 3, rows, rows),
        in_specs=[
            SMEM,
            SMEM,
            SMEM,
            *[VMEM] * len(pieces),
            pl.BlockSpec((2 * PAIRS, PS, PS), lambda i: (i, 0, 0)),
            VMEM,
            VMEM,
            VMEM,
            VMEM,
        ],
        out_specs=(*[pl.BlockSpec(memory_space=pltpu.HBM)] * 6, VMEM, VMEM),
        scratch_shapes=[
            *[pltpu.VMEM((EXT, PS), F32)] * 6,
            pltpu.VMEM((2 * PAIRS, 2, PS, PS), F32),
            square,
            square,
            *[pltpu.VMEM((PS * LEAD, PS), F32)] * 3,
            pltpu.SemaphoreType.DMA((21,)),
            pltpu.VMEM((2, 2, EXT, PS), F32),
        ],
        compiler_params=pltpu.CompilerParams(
            dimension_semantics=("arbitrary",), vmem_limit_bytes=24 << 20
        ),
        name="waves",
    )(half, counts, offs, *pieces, photons, probe_r, probe_i, coef, tables)


def new_coefficients(cross_r, cross_i, powers, modes, coef):
    rows = pl.BlockSpec((CHUNK * LEAD, PS), lambda i: (i, 0))
    whole = pl.BlockSpec((MODES, PMAX), lambda i: (0, 0))
    return pl.pallas_call(
        coef_kernel,
        grid=(PS // CHUNK,),
        out_shape=jax.ShapeDtypeStruct((MODES, PMAX), F32),
        in_specs=[
            rows,
            rows,
            rows,
            pl.BlockSpec((CHUNK, MODES, 2 * PS), lambda i: (i, 0, 0)),
            whole,
        ],
        out_specs=whole,
        scratch_shapes=[pltpu.VMEM((PMAX, MODES), F32)] * 2,
        compiler_params=pltpu.CompilerParams(
            dimension_semantics=("arbitrary",), vmem_limit_bytes=56 << 20
        ),
        name="coefs",
    )(cross_r, cross_i, powers, modes, coef)


def update_row(got, mine):
    return pl.pallas_call(
        update_kernel,
        out_shape=(
            jax.ShapeDtypeStruct((MODES, 2 * PS), F32),
            jax.ShapeDtypeStruct((ROWS, MODES, 2 * PS), F32),
        ),
        in_specs=[VMEM, VMEM],
        out_specs=(VMEM, VMEM),
        compiler_params=pltpu.CompilerParams(vmem_limit_bytes=2 << 20),
        name="update",
    )(got, mine)


def shifted(x, move):
    rows, cols = lax.axis_size("row"), lax.axis_size("col")
    pairs = []
    for a in range(rows):
        for b in range(cols):
            c, d = a + move[0], b + move[1]
            if 0 <= c < rows and 0 <= d < cols:
                pairs.append((c * cols + d, a * cols + b))
    return lax.ppermute(x, ("row", "col"), pairs)


def by_side(low, high):
    lane = lax.broadcasted_iota(jnp.int32, low.shape, low.ndim - 1)
    return jnp.where(lane < MARGIN, low, high)


def extend(block, modes):
    right, left, modes = lax.optimization_barrier(
        (shifted(block, (0, 1)), shifted(block, (0, -1)), modes)
    )
    strip = jax.ShapeDtypeStruct((2, 2, MARGIN, PS), F32)
    both, first, last = pl.pallas_call(
        beside_kernel,
        out_shape=(jax.ShapeDtypeStruct((2, 2, PS, PS), F32), strip, strip),
        in_specs=[VMEM] * 3,
        out_specs=(VMEM,) * 3,
        compiler_params=pltpu.CompilerParams(vmem_limit_bytes=2 << 20),
        name="beside",
    )(block, right, left)
    return (shifted(last, (-1, 0)), both, shifted(first, (1, 0))), modes


def sum_columns(full, from_left, from_right):
    own = full[:3] + by_side(from_left, from_right)
    beside = full[3:] + by_side(from_right, from_left)
    return jnp.stack([own, beside], axis=1)


def inside_object():
    a, b = lax.axis_index("row"), lax.axis_index("col")
    place = a * TILE - MARGIN + lax.iota(jnp.int32, EXT)
    rows = (place >= 0) & (place < lax.axis_size("row") * TILE)
    lane = lax.iota(jnp.int32, PS)
    beside = ((lane < MARGIN) & (b < lax.axis_size("col") - 1)) | ((lane >= MARGIN) & (b > 0))
    cols = jnp.stack([jnp.ones_like(beside), beside])
    return rows[None, :, None] & cols[:, None, :]


def fold_rows(mid, from_above, from_below):
    plane = jax.ShapeDtypeStruct((3, PS, PS), F32)
    return pl.pallas_call(
        fold_kernel,
        out_shape=(plane, plane),
        in_specs=[VMEM] * 3,
        out_specs=(VMEM, VMEM),
        compiler_params=pltpu.CompilerParams(vmem_limit_bytes=2 << 20),
        name="fold",
    )(mid, from_above, from_below)


def shards(object_field, probe_modes, coefficients, offsets, counts, measured):
    tables = jnp.asarray(dft_constants())
    offs = offsets[0, 0].T
    photons = measured[0, 0]
    coef = coefficients[0, 0].T
    rows, cols = lax.axis_size("row"), lax.axis_size("col")
    core = lax.axis_index("row") % 2
    half = core.reshape(1)
    groups = [[a * cols + b for a in range(k, rows, 2) for b in range(cols)] for k in range(2)]
    mates = [(a, a ^ 1) for a in range(rows)]
    place = lax.axis_index("row") // 2 * cols + lax.axis_index("col")

    def exchange(x):
        return lax.all_to_all(x, ("row", "col"), 0, 0, axis_index_groups=groups, tiled=True)

    modes = probe_modes.transpose(2, 0, 1, 3).reshape(PS, MODES, 2 * PS)
    mine = lax.dynamic_index_in_dim(modes, core * ROWS + place, 0, keepdims=False)
    pieces, modes = extend(object_field, modes)
    ext = jnp.concatenate(pieces, axis=2)
    for iteration in range(ITERS):
        final = iteration == ITERS - 1
        if iteration == 0:
            probe_r, probe_i = mix_probes(jnp.zeros_like(half), counts, modes, coef)
        else:
            probe_r, probe_i = mix_probes(half * ROWS, counts, near, coef)
            probe_r, probe_i = mix_probes((1 - half) * ROWS, counts, far, coef, probe_r, probe_i)
        up, mid, down, cross_r, cross_i, powers, kept, given = waves(
            half, counts, offs, pieces, photons, probe_r, probe_i, coef, tables, MARGIN if final else PS
        )
        if not final:
            from_above = shifted(up, (-1, 0))
            from_below = shifted(down, (1, 0))
        sent = kept + lax.ppermute(given, "row", mates)
        got = exchange(sent)
        if final:
            above, below = shifted(up, (-1, 0)), shifted(down, (1, 0))
            full, beside = fold_rows(mid, above, below)
            to_right, to_left = beside, beside
        else:
            full, to_right, to_left = sum_rows(up, down, from_above, from_below)
        from_left = shifted(to_right, (0, -1))
        from_right = shifted(to_left, (0, 1))
        mine, copies = update_row(got, mine)
        copies, cross_r = lax.optimization_barrier((copies, cross_r))
        coef = new_coefficients(cross_r, cross_i, powers, modes, coef)
        near = exchange(copies)
        far = lax.ppermute(near, "row", mates)
        modes = jnp.where(
            core == 0, jnp.concatenate([near, far]), jnp.concatenate([far, near])
        )
        if final:
            total = full + by_side(from_left, from_right)
            object_field = ext[:, 0, MARGIN:-MARGIN] + total[0:2] / (total[2:3] + 1.0)
        else:
            total = sum_columns(full, from_left, from_right)
            step = total[0:2] / (total[2:3] + 1.0)
            ext = ext + jnp.where(inside_object()[None], step, 0.0)
            pieces = (ext,)
    probe_modes = modes.reshape(PS, MODES, 2, PS).transpose(1, 2, 0, 3)
    return (object_field, probe_modes, coef.T[None, None])


def solution(mesh):
    placed = (
        P(None, "row", "col"),
        P(),
        P("row", "col", None, None),
        P("row", "col", None, None),
        P("row", "col"),
        P("row", "col", None, None, None),
    )
    return jax.shard_map(
        shards,
        mesh=mesh,
        in_specs=placed,
        out_specs=(P(None, "row", "col"), P(), P("row", "col", None, None)),
        check_vma=False,
    )
```

```python
import math

import jax
import jax.numpy as jnp
import numpy as np
from jax import lax
from jax.experimental import pallas as pl
from jax.experimental.pallas import tpu as pltpu
from jax.sharding import PartitionSpec as P

PS = 128
MODES = 8
TILE = 128
PMAX = 32
ITERS = 2
EXT = TILE + PS
F32 = jnp.float32
BF16 = jnp.bfloat16
PAIRS = 4
LEAD = 33
ROWS = PS // 2
MARGIN = PS // 2


def split(x):
    hi = x.astype(BF16)
    lo = (x - hi.astype(F32)).astype(BF16)
    return hi, lo


def triple(x, axis):
    hi, lo = split(x)
    return jnp.concatenate([hi, lo, hi], axis=axis)


def dft_constants():
    ramp = np.arange(PS)
    angles = (ramp[:, None] * ramp[None, :] % PS) * (2.0 * math.pi / PS)
    cos = np.cos(angles) / math.sqrt(PS)
    sin = -np.sin(angles) / math.sqrt(PS)
    parts = []
    for table in (np.block([[cos, sin], [-sin, cos]]), np.block([[cos, -sin], [sin, cos]])):
        table = table.astype(np.float32)
        hi = table.astype(jnp.bfloat16)
        parts += [hi, (table - hi.astype(np.float32)).astype(jnp.bfloat16)]
    return np.stack(parts)


def dot(a, b):
    return jnp.dot(a, b, preferred_element_type=F32)


def live_only(coef, counts):
    slot = lax.broadcasted_iota(jnp.int32, coef.shape, 1)
    return jnp.where(slot < counts[0, 0], coef[...], 0.0)


def probe_kernel(base, counts, modes, coef, *refs):
    probe_r, probe_i = refs[-2:]
    left = triple(live_only(coef, counts).T, 1)

    def rows(y, _):
        m = modes[y]
        h = m.astype(BF16).astype(F32)
        right = jnp.concatenate([h, h, m - h], axis=0).astype(BF16)
        out = dot(left, right)
        start = (base[0] + y) * LEAD
        probe_r[pl.ds(start, PMAX), :] = out[:, :PS]
        probe_i[pl.ds(start, PMAX), :] = out[:, PS:]
        return 0

    lax.fori_loop(0, modes.shape[0], rows, 0, unroll=8)


def wave_kernel(half, counts, offs, *refs):
    (
        photons, probe_r, probe_i, coef, tables,
        up, mid, down, out_r, out_i, out_p, near, far,
        acc_rl, acc_rh, acc_il, acc_ih, acc_pl, acc_ph,
        patches, wave, field, cross_r, cross_i, power, sems, ext,
    ) = refs[-27:]
    pieces = refs[:-27]
    step = pl.program_id(0)
    lane = lax.broadcasted_iota(jnp.int32, (PS, PS), 1)
    if len(pieces) == 1:
        ext = pieces[0]
    sums = ((acc_rl, acc_rh), (acc_il, acc_ih), (acc_pl, acc_ph))

    @pl.when(step == 0)
    def _():
        if len(pieces) == 3:
            row = 0
            for piece in pieces:
                ext[:, :, row : row + piece.shape[2]] = piece[...]
                row += piece.shape[2]
        for low, high in sums:
            low[...] = jnp.zeros_like(low)
            high[...] = jnp.zeros_like(high)

    def own_lanes(left):
        return (lane < left + MARGIN) & (lane >= left - MARGIN)

    def regroup(x):
        top = jnp.concatenate([x[:PS, :PS], x[PS:, :PS]], axis=1)
        low = jnp.concatenate([x[:PS, PS:], x[PS:, PS:]], axis=1)
        return jnp.concatenate([top, low], axis=0)

    def take(j, q):
        p = 2 * PAIRS * step + 2 * j + q
        return (
            probe_r[pl.ds(p, PS, stride=LEAD), :],
            probe_i[pl.ds(p, PS, stride=LEAD), :],
            patches[2 * j + q, 0],
            patches[2 * j + q, 1],
        )

    def cut(j, q):
        p = 2 * PAIRS * step + 2 * j + q
        top = offs[0, p]
        left = offs[1, p]
        turn = (PS + MARGIN - left) & (PS - 1)
        inside = own_lanes(left)
        total = None
        for c in range(2):
            patch = jnp.where(
                inside, ext[c, 0, pl.ds(top, PS), :], ext[c, 1, pl.ds(top, PS), :]
            )
            patch = pltpu.roll(patch, turn, 1)
            patches[2 * j + q, c] = patch
            total = patch * patch if total is None else total + patch * patch
        power[pl.ds(p, PS, stride=LEAD), :] = total

    def start(j):
        for q in range(2):
            cut(j, q)
            pr, pi, obj_r, obj_i = take(j, q)
            rows = slice(q * PS, (q + 1) * PS)
            wave[j, rows, :PS] = pr * obj_r - pi * obj_i
            wave[j, rows, PS:] = pr * obj_i + pi * obj_r

    def correct(j, there):
        count = jnp.concatenate([photons[2 * j], photons[2 * j + 1]], axis=1).astype(F32)
        far_r = there[:PS]
        far_i = there[PS:]
        size = jnp.maximum(far_r * far_r + far_i * far_i, 0.25)
        scale = count * lax.rsqrt(jnp.maximum(count * size, 0.0625)) * 0.03125
        return jnp.concatenate([far_r * scale, far_i * scale], axis=0)

    def finish(j):
        for q in range(2):
            p = 2 * PAIRS * step + 2 * j + q
            top = offs[0, p]
            left = offs[1, p]
            turn = (left + MARGIN) & (PS - 1)
            inside = own_lanes(left)
            rows = slice(q * PS, (q + 1) * PS)
            diff_r = field[j, rows, :PS]
            diff_i = field[j, rows, PS:]
            pr, pi, obj_r, obj_i = take(j, q)
            cross_r[pl.ds(p, PS, stride=LEAD), :] = obj_r * diff_r + obj_i * diff_i
            cross_i[pl.ds(p, PS, stride=LEAD), :] = obj_r * diff_i - obj_i * diff_r
            pieces = (
                pr * diff_r + pi * diff_i,
                pr * diff_i - pi * diff_r,
                pr * pr + pi * pi,
            )
            for (low, high), piece in zip(sums, pieces):
                turned = pltpu.roll(piece, turn, 1)
                near = jnp.where(inside, turned, 0.0)
                low[pl.ds(top, PS), :] += near
                high[pl.ds(top, PS), :] += turned - near

    def table(i, axis):
        hi = tables[2 * i]
        return jnp.concatenate([hi, hi, tables[2 * i + 1]], axis=axis)

    pairs = range(PAIRS)
    for j in pairs:
        start(j)
    x = [dot(triple(wave[j], 1), table(0, 0)) for j in pairs]
    x = [dot(table(1, 1), triple(regroup(x[j]), 0)) for j in pairs]
    x = [correct(j, x[j]) for j in pairs]
    x = [dot(table(0, 1), triple(x[j], 0)) for j in pairs]
    for j in pairs:
        field[j] = dot(triple(regroup(x[j]), 1), table(1, 0)) - wave[j]
    for j in pairs:
        finish(j)

    @pl.when(step == PMAX // (2 * PAIRS) - 1)
    def _():
        width = up.shape[1]
        moves = [(cross_r, out_r), (cross_i, out_i), (power, out_p)]
        for i, piece in enumerate((acc_rl, acc_il, acc_pl, acc_rh, acc_ih, acc_ph)):
            moves.append((piece.at[:width], down.at[i]))
            moves.append((piece.at[EXT - width:], up.at[i]))
            if width < PS:
                moves.append((piece.at[width : EXT - width], mid.at[i]))
        copies = [
            pltpu.make_async_copy(source, target, sems.at[i])
            for i, (source, target) in enumerate(moves)
        ]
        for copy in copies:
            copy.start()

        def stacked(x):
            hi, lo = split(x)
            zero = jnp.zeros_like(hi)
            return jnp.concatenate(
                [jnp.concatenate([hi, hi], axis=1), jnp.concatenate([lo, zero], axis=1)], axis=0
            )

        used = live_only(coef, counts)
        left = stacked(used)
        left_square = stacked(used * used)
        for target, base in ((near, half[0] * ROWS), (far, (1 - half[0]) * ROWS)):

            def rows(y, _):
                begin = (base + y) * LEAD
                pair = jnp.concatenate(
                    [cross_r[pl.ds(begin, PMAX), :], cross_i[pl.ds(begin, PMAX), :]], axis=1
                )
                h, l = split(pair)
                out = dot(left, jnp.concatenate([h, l], axis=0))
                target[y, :, : 2 * PS] = out[:MODES] + out[MODES:]
                h, l = split(power[pl.ds(begin, PMAX), :])
                out = dot(left_square, jnp.concatenate([h, l], axis=0))
                target[y, :, 2 * PS:] = out[:MODES] + out[MODES:]
                return 0

            lax.fori_loop(0, ROWS, rows, 0, unroll=8)
        for copy in copies:
            copy.wait()


CHUNK = 64


def coef_kernel(cross_r, cross_i, powers, modes, coef, out, num, den):
    step = pl.program_id(0)

    @pl.when(step == 0)
    def _():
        num[...] = jnp.zeros_like(num)
        den[...] = jnp.zeros_like(den)

    dims = (((1,), (1,)), ((), ()))

    def wide_dot(a, b):
        return lax.dot_general(a, b, dims, preferred_element_type=F32)

    top = jnp.zeros((PMAX, MODES), F32)
    low = jnp.zeros((PMAX, MODES), F32)
    for y in range(CHUNK):
        rows = slice(y * LEAD, y * LEAD + PMAX)
        cross = jnp.concatenate([cross_r[rows, :], cross_i[rows, :]], axis=1)
        m = modes[y]
        power = m[:, :PS] * m[:, :PS] + m[:, PS:] * m[:, PS:]
        h, l = split(m)
        top += wide_dot(triple(cross, 1), jnp.concatenate([h, h, l], axis=1))
        h, l = split(power)
        low += wide_dot(triple(powers[rows, :], 1), jnp.concatenate([h, h, l], axis=1))
    num[...] += top
    den[...] += low

    @pl.when(step == PS // CHUNK - 1)
    def _():
        out[...] = coef[...] + (num[...] / (den[...] + 1.0)).T


def update_kernel(got, mine, new, copies):
    total = jnp.sum(got[...], axis=0)
    power = total[:, 2 * PS:] + 1.0
    row = mine[...] + total[:, : 2 * PS] / jnp.concatenate([power, power], axis=1)
    new[...] = row
    copies[...] = jnp.broadcast_to(row[None], copies.shape)


def beside_kernel(block, right, left, both, first, last):
    lane = lax.broadcasted_iota(jnp.int32, (PS, PS), 1)
    for c in range(2):
        beside = jnp.where(lane < MARGIN, right[c], left[c])
        for i, plane in ((0, block[c]), (1, beside)):
            both[c, i] = plane
            first[c, i] = plane[:MARGIN]
            last[c, i] = plane[MARGIN:]


def rows_kernel(up, down, from_above, from_below, full, to_right, to_left):
    lane = lax.broadcasted_iota(jnp.int32, (PS, PS), 1)
    for c in range(3):
        for rows, own, other in ((slice(0, PS), down, from_above), (slice(PS, EXT), up, from_below)):
            centre = own[c] + other[c]
            beside = own[3 + c] + other[3 + c]
            full[c, rows] = centre
            full[3 + c, rows] = beside
            to_right[c, rows] = jnp.where(lane < MARGIN, beside, centre)
            to_left[c, rows] = jnp.where(lane < MARGIN, centre, beside)


SMEM = pl.BlockSpec(memory_space=pltpu.SMEM)
VMEM = pl.BlockSpec(memory_space=pltpu.VMEM)


def mix_probes(base, counts, modes, coef, *before):
    grid = jax.ShapeDtypeStruct((PS * LEAD, PS), F32)
    return pl.pallas_call(
        probe_kernel,
        out_shape=(grid, grid),
        in_specs=[SMEM, SMEM, VMEM, VMEM, *[VMEM] * len(before)],
        out_specs=(VMEM, VMEM),
        input_output_aliases={4: 0, 5: 1} if before else {},
        compiler_params=pltpu.CompilerParams(vmem_limit_bytes=2 << 20),
        name="probes",
    )(base, counts, modes, coef, *before)


def sum_rows(up, down, from_above, from_below):
    side = jax.ShapeDtypeStruct((3, EXT, PS), F32)
    return pl.pallas_call(
        rows_kernel,
        out_shape=(jax.ShapeDtypeStruct((6, EXT, PS), F32), side, side),
        in_specs=[VMEM] * 4,
        out_specs=(VMEM,) * 3,
        compiler_params=pltpu.CompilerParams(vmem_limit_bytes=2 << 20),
        name="rows",
    )(up, down, from_above, from_below)


def waves(half, counts, offs, pieces, photons, probe_r, probe_i, coef, tables, width):
    edge = pltpu.HBM((6, width, PS), F32)
    inner = pltpu.HBM((6, max(EXT - 2 * width, 8), PS), F32)
    grid = pltpu.HBM((PS * LEAD, PS), F32)
    rows = jax.ShapeDtypeStruct((ROWS, MODES, 3 * PS), F32)
    square = pltpu.VMEM((PAIRS, 2 * PS, 2 * PS), F32)
    return pl.pallas_call(
        wave_kernel,
        grid=(PMAX // (2 * PAIRS),),
        out_shape=(edge, inner, edge, *[grid] * 3, rows, rows),
        in_specs=[
            SMEM,
            SMEM,
            SMEM,
            *[VMEM] * len(pieces),
            pl.BlockSpec((2 * PAIRS, PS, PS), lambda i: (i, 0, 0)),
            VMEM,
            VMEM,
            VMEM,
            VMEM,
        ],
        out_specs=(*[pl.BlockSpec(memory_space=pltpu.HBM)] * 6, VMEM, VMEM),
        scratch_shapes=[
            *[pltpu.VMEM((EXT, PS), F32)] * 6,
            pltpu.VMEM((2 * PAIRS, 2, PS, PS), F32),
            square,
            square,
            *[pltpu.VMEM((PS * LEAD, PS), F32)] * 3,
            pltpu.SemaphoreType.DMA((21,)),
            pltpu.VMEM((2, 2, EXT, PS), F32),
        ],
        compiler_params=pltpu.CompilerParams(
            dimension_semantics=("arbitrary",), vmem_limit_bytes=24 << 20
        ),
        name="waves",
    )(half, counts, offs, *pieces, photons, probe_r, probe_i, coef, tables)


def new_coefficients(cross_r, cross_i, powers, modes, coef):
    rows = pl.BlockSpec((CHUNK * LEAD, PS), lambda i: (i, 0))
    whole = pl.BlockSpec((MODES, PMAX), lambda i: (0, 0))
    return pl.pallas_call(
        coef_kernel,
        grid=(PS // CHUNK,),
        out_shape=jax.ShapeDtypeStruct((MODES, PMAX), F32),
        in_specs=[
            rows,
            rows,
            rows,
            pl.BlockSpec((CHUNK, MODES, 2 * PS), lambda i: (i, 0, 0)),
            whole,
        ],
        out_specs=whole,
        scratch_shapes=[pltpu.VMEM((PMAX, MODES), F32)] * 2,
        compiler_params=pltpu.CompilerParams(
            dimension_semantics=("arbitrary",), vmem_limit_bytes=56 << 20
        ),
        name="coefs",
    )(cross_r, cross_i, powers, modes, coef)


def update_row(got, mine):
    return pl.pallas_call(
        update_kernel,
        out_shape=(
            jax.ShapeDtypeStruct((MODES, 2 * PS), F32),
            jax.ShapeDtypeStruct((ROWS, MODES, 2 * PS), F32),
        ),
        in_specs=[VMEM, VMEM],
        out_specs=(VMEM, VMEM),
        compiler_params=pltpu.CompilerParams(vmem_limit_bytes=2 << 20),
        name="update",
    )(got, mine)


def shifted(x, move):
    rows, cols = lax.axis_size("row"), lax.axis_size("col")
    pairs = []
    for a in range(rows):
        for b in range(cols):
            c, d = a + move[0], b + move[1]
            if 0 <= c < rows and 0 <= d < cols:
                pairs.append((c * cols + d, a * cols + b))
    return lax.ppermute(x, ("row", "col"), pairs)


def by_side(low, high):
    lane = lax.broadcasted_iota(jnp.int32, low.shape, low.ndim - 1)
    return jnp.where(lane < MARGIN, low, high)


def extend(block, modes):
    right, left, modes = lax.optimization_barrier(
        (shifted(block, (0, 1)), shifted(block, (0, -1)), modes)
    )
    strip = jax.ShapeDtypeStruct((2, 2, MARGIN, PS), F32)
    both, first, last = pl.pallas_call(
        beside_kernel,
        out_shape=(jax.ShapeDtypeStruct((2, 2, PS, PS), F32), strip, strip),
        in_specs=[VMEM] * 3,
        out_specs=(VMEM,) * 3,
        compiler_params=pltpu.CompilerParams(vmem_limit_bytes=2 << 20),
        name="beside",
    )(block, right, left)
    return (shifted(last, (-1, 0)), both, shifted(first, (1, 0))), modes


def sum_columns(full, from_left, from_right):
    own = full[:3] + by_side(from_left, from_right)
    beside = full[3:] + by_side(from_right, from_left)
    return jnp.stack([own, beside], axis=1)


def inside_object():
    a, b = lax.axis_index("row"), lax.axis_index("col")
    place = a * TILE - MARGIN + lax.iota(jnp.int32, EXT)
    rows = (place >= 0) & (place < lax.axis_size("row") * TILE)
    lane = lax.iota(jnp.int32, PS)
    beside = ((lane < MARGIN) & (b < lax.axis_size("col") - 1)) | ((lane >= MARGIN) & (b > 0))
    cols = jnp.stack([jnp.ones_like(beside), beside])
    return rows[None, :, None] & cols[:, None, :]


def fold(up, mid, down):
    edges = jnp.concatenate([shifted(up, (-1, 0)), shifted(down, (1, 0))], axis=1)
    mid = mid + edges
    beside = mid[3:]
    return mid[:3] + by_side(shifted(beside, (0, -1)), shifted(beside, (0, 1)))


def shards(object_field, probe_modes, coefficients, offsets, counts, measured):
    tables = jnp.asarray(dft_constants())
    offs = offsets[0, 0].T
    photons = measured[0, 0]
    coef = coefficients[0, 0].T
    rows, cols = lax.axis_size("row"), lax.axis_size("col")
    core = lax.axis_index("row") % 2
    half = core.reshape(1)
    groups = [[a * cols + b for a in range(k, rows, 2) for b in range(cols)] for k in range(2)]
    mates = [(a, a ^ 1) for a in range(rows)]
    place = lax.axis_index("row") // 2 * cols + lax.axis_index("col")

    def exchange(x):
        return lax.all_to_all(x, ("row", "col"), 0, 0, axis_index_groups=groups, tiled=True)

    modes = probe_modes.transpose(2, 0, 1, 3).reshape(PS, MODES, 2 * PS)
    mine = lax.dynamic_index_in_dim(modes, core * ROWS + place, 0, keepdims=False)
    pieces, modes = extend(object_field, modes)
    ext = jnp.concatenate(pieces, axis=2)
    for iteration in range(ITERS):
        final = iteration == ITERS - 1
        if iteration == 0:
            probe_r, probe_i = mix_probes(jnp.zeros_like(half), counts, modes, coef)
        else:
            probe_r, probe_i = mix_probes(half * ROWS, counts, near, coef)
            probe_r, probe_i = mix_probes((1 - half) * ROWS, counts, far, coef, probe_r, probe_i)
        up, mid, down, cross_r, cross_i, powers, kept, given = waves(
            half, counts, offs, pieces, photons, probe_r, probe_i, coef, tables, MARGIN if final else PS
        )
        if final:
            sent = kept + lax.ppermute(given, "row", mates)
            got = exchange(sent)
            coef = new_coefficients(cross_r, cross_i, powers, modes, coef)
            got, coef = lax.optimization_barrier((got, coef))
            mine, copies = update_row(got, mine)
            near = exchange(copies)
        else:
            from_above = shifted(up, (-1, 0))
            from_below = shifted(down, (1, 0))
            sent = kept + lax.ppermute(given, "row", mates)
            got = exchange(sent)
            full, to_right, to_left = sum_rows(up, down, from_above, from_below)
            from_left = shifted(to_right, (0, -1))
            from_right = shifted(to_left, (0, 1))
            mine, copies = update_row(got, mine)
            copies, cross_r = lax.optimization_barrier((copies, cross_r))
            coef = new_coefficients(cross_r, cross_i, powers, modes, coef)
            near = exchange(copies)
        far = lax.ppermute(near, "row", mates)
        modes = jnp.where(
            core == 0, jnp.concatenate([near, far]), jnp.concatenate([far, near])
        )
        if final:
            total = fold(up, mid, down)
            object_field = ext[:, 0, MARGIN:-MARGIN] + total[0:2] / (total[2:3] + 1.0)
        else:
            total = sum_columns(full, from_left, from_right)
            step = total[0:2] / (total[2:3] + 1.0)
            ext = ext + jnp.where(inside_object()[None], step, 0.0)
            pieces = (ext,)
    probe_modes = modes.reshape(PS, MODES, 2, PS).transpose(1, 2, 0, 3)
    return (object_field, probe_modes, coef.T[None, None])


def solution(mesh):
    placed = (
        P(None, "row", "col"),
        P(),
        P("row", "col", None, None),
        P("row", "col", None, None),
        P("row", "col"),
        P("row", "col", None, None, None),
    )
    return jax.shard_map(
        shards,
        mesh=mesh,
        in_specs=placed,
        out_specs=(P(None, "row", "col"), P(), P("row", "col", None, None)),
        check_vma=False,
    )
```

```python
import math

import jax
import jax.numpy as jnp
import numpy as np
from jax import lax
from jax.experimental import pallas as pl
from jax.experimental.pallas import tpu as pltpu
from jax.sharding import PartitionSpec as P

PS = 128
MODES = 8
TILE = 128
PMAX = 32
ITERS = 2
EXT = TILE + PS
F32 = jnp.float32
BF16 = jnp.bfloat16
PAIRS = 4
LEAD = 33
ROWS = PS // 2
MARGIN = PS // 2


def split(x):
    hi = x.astype(BF16)
    lo = (x - hi.astype(F32)).astype(BF16)
    return hi, lo


def triple(x, axis):
    hi, lo = split(x)
    return jnp.concatenate([hi, lo, hi], axis=axis)


def dft_constants():
    ramp = np.arange(PS)
    angles = (ramp[:, None] * ramp[None, :] % PS) * (2.0 * math.pi / PS)
    cos = np.cos(angles) / math.sqrt(PS)
    sin = -np.sin(angles) / math.sqrt(PS)
    parts = []
    for table in (np.block([[cos, sin], [-sin, cos]]), np.block([[cos, -sin], [sin, cos]])):
        table = table.astype(np.float32)
        hi = table.astype(jnp.bfloat16)
        parts += [hi, (table - hi.astype(np.float32)).astype(jnp.bfloat16)]
    return np.stack(parts)


def dot(a, b):
    return jnp.dot(a, b, preferred_element_type=F32)


def live_only(coef, counts):
    slot = lax.broadcasted_iota(jnp.int32, coef.shape, 1)
    return jnp.where(slot < counts[0, 0], coef[...], 0.0)


def probe_kernel(base, counts, modes, coef, *refs):
    probe_r, probe_i = refs[-2:]
    left = triple(live_only(coef, counts).T, 1)

    def rows(y, _):
        m = modes[y]
        h = m.astype(BF16).astype(F32)
        right = jnp.concatenate([h, h, m - h], axis=0).astype(BF16)
        out = dot(left, right)
        start = (base[0] + y) * LEAD
        probe_r[pl.ds(start, PMAX), :] = out[:, :PS]
        probe_i[pl.ds(start, PMAX), :] = out[:, PS:]
        return 0

    lax.fori_loop(0, modes.shape[0], rows, 0, unroll=64)


def first_probe_kernel(base, counts, modes, coef, tables, probe_r, probe_i, kept, sem):
    copy = pltpu.make_async_copy(tables, kept, sem)
    copy.start()
    probe_kernel(base, counts, modes, coef, probe_r, probe_i)
    copy.wait()


def wave_kernel(half, counts, offs, *refs):
    (
        photons, probe_r, probe_i, coef, tables,
        up, mid, down, out_r, out_i, out_p, near, far,
        acc_rl, acc_rh, acc_il, acc_ih, acc_pl, acc_ph,
        patches, wave, field, cross_r, cross_i, power, sems, ext,
    ) = refs[-27:]
    pieces = refs[:-27]
    step = pl.program_id(0)
    lane = lax.broadcasted_iota(jnp.int32, (PS, PS), 1)
    if len(pieces) == 1:
        ext = pieces[0]
    sums = ((acc_rl, acc_rh), (acc_il, acc_ih), (acc_pl, acc_ph))

    @pl.when(step == 0)
    def _():
        if len(pieces) == 3:
            row = 0
            for piece in pieces:
                ext[:, :, row : row + piece.shape[2]] = piece[...]
                row += piece.shape[2]
        for low, high in sums:
            low[...] = jnp.zeros_like(low)
            high[...] = jnp.zeros_like(high)

    def own_lanes(left):
        return (lane < left + MARGIN) & (lane >= left - MARGIN)

    def regroup(x):
        top = jnp.concatenate([x[:PS, :PS], x[PS:, :PS]], axis=1)
        low = jnp.concatenate([x[:PS, PS:], x[PS:, PS:]], axis=1)
        return jnp.concatenate([top, low], axis=0)

    def take(j, q):
        p = 2 * PAIRS * step + 2 * j + q
        return (
            probe_r[pl.ds(p, PS, stride=LEAD), :],
            probe_i[pl.ds(p, PS, stride=LEAD), :],
            patches[2 * j + q, 0],
            patches[2 * j + q, 1],
        )

    def cut(j, q):
        p = 2 * PAIRS * step + 2 * j + q
        top = offs[0, p]
        left = offs[1, p]
        turn = (PS + MARGIN - left) & (PS - 1)
        inside = own_lanes(left)
        total = None
        for c in range(2):
            patch = jnp.where(
                inside, ext[c, 0, pl.ds(top, PS), :], ext[c, 1, pl.ds(top, PS), :]
            )
            patch = pltpu.roll(patch, turn, 1)
            patches[2 * j + q, c] = patch
            total = patch * patch if total is None else total + patch * patch
        power[pl.ds(p, PS, stride=LEAD), :] = total

    def start(j):
        for q in range(2):
            cut(j, q)
            pr, pi, obj_r, obj_i = take(j, q)
            rows = slice(q * PS, (q + 1) * PS)
            wave[j, rows, :PS] = pr * obj_r - pi * obj_i
            wave[j, rows, PS:] = pr * obj_i + pi * obj_r

    def correct(j, there):
        count = jnp.concatenate([photons[2 * j], photons[2 * j + 1]], axis=1).astype(F32)
        far_r = there[:PS]
        far_i = there[PS:]
        power_there = jnp.maximum(far_r * far_r + far_i * far_i, 0.25)
        scale = count * lax.rsqrt(jnp.maximum(count * power_there, 0.0625)) * 0.03125
        return jnp.concatenate([far_r * scale, far_i * scale], axis=0)

    def finish(j):
        for q in range(2):
            p = 2 * PAIRS * step + 2 * j + q
            top = offs[0, p]
            left = offs[1, p]
            turn = (left + MARGIN) & (PS - 1)
            inside = own_lanes(left)
            rows = slice(q * PS, (q + 1) * PS)
            diff_r = field[j, rows, :PS]
            diff_i = field[j, rows, PS:]
            pr, pi, obj_r, obj_i = take(j, q)
            cross_r[pl.ds(p, PS, stride=LEAD), :] = obj_r * diff_r + obj_i * diff_i
            cross_i[pl.ds(p, PS, stride=LEAD), :] = obj_r * diff_i - obj_i * diff_r
            pieces = (
                pr * diff_r + pi * diff_i,
                pr * diff_i - pi * diff_r,
                pr * pr + pi * pi,
            )
            for (low, high), piece in zip(sums, pieces):
                turned = pltpu.roll(piece, turn, 1)
                near = jnp.where(inside, turned, 0.0)
                low[pl.ds(top, PS), :] += near
                high[pl.ds(top, PS), :] += turned - near

    def table(i, axis):
        hi = tables[2 * i]
        return jnp.concatenate([hi, hi, tables[2 * i + 1]], axis=axis)

    pairs = range(PAIRS)
    for j in pairs:
        start(j)
    size = 2 * PS
    x = []
    for j in range(0, PAIRS, 2):
        out = dot(triple(wave[j : j + 2].reshape(2 * size, size), 1), table(0, 0))
        x += [out[:size], out[size:]]
    x = [dot(table(1, 1), triple(regroup(x[j]), 0)) for j in pairs]
    x = [correct(j, x[j]) for j in pairs]
    x = [dot(table(0, 1), triple(x[j], 0)) for j in pairs]
    for j in range(0, PAIRS, 2):
        both = jnp.concatenate([regroup(x[j]), regroup(x[j + 1])], axis=0)
        out = dot(triple(both, 1), table(1, 0))
        field[j] = out[:size] - wave[j]
        field[j + 1] = out[size:] - wave[j + 1]
    for j in pairs:
        finish(j)

    @pl.when(step == PMAX // (2 * PAIRS) - 1)
    def _():
        width = up.shape[1]
        moves = [(cross_r, out_r), (cross_i, out_i), (power, out_p)]
        for i, piece in enumerate((acc_rl, acc_il, acc_pl, acc_rh, acc_ih, acc_ph)):
            moves.append((piece.at[:width], down.at[i]))
            moves.append((piece.at[EXT - width:], up.at[i]))
            if width < PS:
                moves.append((piece.at[width : EXT - width], mid.at[i]))
        copies = [
            pltpu.make_async_copy(source, target, sems.at[i])
            for i, (source, target) in enumerate(moves)
        ]
        for copy in copies:
            copy.start()

        def stacked(x):
            hi, lo = split(x)
            zero = jnp.zeros_like(hi)
            return jnp.concatenate(
                [jnp.concatenate([hi, hi], axis=1), jnp.concatenate([lo, zero], axis=1)], axis=0
            )

        used = live_only(coef, counts)
        left = stacked(used)
        left_square = stacked(used * used)
        for target, base in ((near, half[0] * ROWS), (far, (1 - half[0]) * ROWS)):

            def rows(y, _):
                begin = (base + y) * LEAD
                pair = jnp.concatenate(
                    [cross_r[pl.ds(begin, PMAX), :], cross_i[pl.ds(begin, PMAX), :]], axis=1
                )
                h, l = split(pair)
                out = dot(left, jnp.concatenate([h, l], axis=0))
                target[y, :, : 2 * PS] = out[:MODES] + out[MODES:]
                h, l = split(power[pl.ds(begin, PMAX), :])
                out = dot(left_square, jnp.concatenate([h, l], axis=0))
                target[y, :, 2 * PS:] = out[:MODES] + out[MODES:]
                return 0

            lax.fori_loop(0, ROWS, rows, 0, unroll=16)
        for copy in copies:
            copy.wait()


CHUNK = 64


def coef_kernel(cross_r, cross_i, powers, modes, coef, out, num, den):
    step = pl.program_id(0)

    @pl.when(step == 0)
    def _():
        num[...] = jnp.zeros_like(num)
        den[...] = jnp.zeros_like(den)

    dims = (((1,), (1,)), ((), ()))

    def wide_dot(a, b):
        return lax.dot_general(a, b, dims, preferred_element_type=F32)

    top = jnp.zeros((PMAX, MODES), F32)
    low = jnp.zeros((PMAX, MODES), F32)
    for y in range(CHUNK):
        rows = slice(y * LEAD, y * LEAD + PMAX)
        cross = jnp.concatenate([cross_r[rows, :], cross_i[rows, :]], axis=1)
        m = modes[y]
        power = m[:, :PS] * m[:, :PS] + m[:, PS:] * m[:, PS:]
        h, l = split(m)
        top += wide_dot(triple(cross, 1), jnp.concatenate([h, h, l], axis=1))
        h, l = split(power)
        low += wide_dot(triple(powers[rows, :], 1), jnp.concatenate([h, h, l], axis=1))
    num[...] += top
    den[...] += low

    @pl.when(step == PS // CHUNK - 1)
    def _():
        out[...] = coef[...] + (num[...] / (den[...] + 1.0)).T


def update_kernel(got, mine, new, copies):
    total = jnp.sum(got[...], axis=0)
    power = total[:, 2 * PS:] + 1.0
    row = mine[...] + total[:, : 2 * PS] / jnp.concatenate([power, power], axis=1)
    new[...] = row
    copies[...] = jnp.broadcast_to(row[None], copies.shape)


def beside_kernel(block, right, left, both, first, last):
    lane = lax.broadcasted_iota(jnp.int32, (PS, PS), 1)
    for c in range(2):
        beside = jnp.where(lane < MARGIN, right[c], left[c])
        for i, plane in ((0, block[c]), (1, beside)):
            both[c, i] = plane
            first[c, i] = plane[:MARGIN]
            last[c, i] = plane[MARGIN:]


def rows_kernel(
    down_own, down_beside, above_own, above_beside, up_own, up_beside, below_own, below_beside,
    own, beside, to_right, to_left,
):
    lane = lax.broadcasted_iota(jnp.int32, (PS, PS), 1)
    for rows, parts in (
        (slice(0, PS), (down_own, above_own, down_beside, above_beside)),
        (slice(PS, EXT), (up_own, below_own, up_beside, below_beside)),
    ):
        centre = parts[0][0] + parts[1][0]
        side = parts[2][0] + parts[3][0]
        own[0, rows] = centre
        beside[0, rows] = side
        to_right[0, rows] = jnp.where(lane < MARGIN, side, centre)
        to_left[0, rows] = jnp.where(lane < MARGIN, centre, side)


SMEM = pl.BlockSpec(memory_space=pltpu.SMEM)
VMEM = pl.BlockSpec(memory_space=pltpu.VMEM)


def mix_probes(base, counts, modes, coef, *before):
    grid = jax.ShapeDtypeStruct((PS * LEAD, PS), F32)
    return pl.pallas_call(
        probe_kernel,
        out_shape=(grid, grid),
        in_specs=[SMEM, SMEM, VMEM, VMEM, *[VMEM] * len(before)],
        out_specs=(VMEM, VMEM),
        input_output_aliases={4: 0, 5: 1} if before else {},
        compiler_params=pltpu.CompilerParams(vmem_limit_bytes=2 << 20),
        name="probes",
    )(base, counts, modes, coef, *before)


def first_probes(base, counts, modes, coef, tables):
    grid = jax.ShapeDtypeStruct((PS * LEAD, PS), F32)
    return pl.pallas_call(
        first_probe_kernel,
        out_shape=(grid, grid, jax.ShapeDtypeStruct(tables.shape, tables.dtype)),
        in_specs=[SMEM, SMEM, VMEM, VMEM, pl.BlockSpec(memory_space=pltpu.HBM)],
        out_specs=(VMEM, VMEM, VMEM),
        scratch_shapes=[pltpu.SemaphoreType.DMA],
        compiler_params=pltpu.CompilerParams(vmem_limit_bytes=2 << 20),
        name="probes",
    )(base, counts, modes, coef, tables)


def sum_rows(up, down, from_above, from_below):
    whole = jax.ShapeDtypeStruct((3, EXT, PS), F32)
    near = pl.BlockSpec((1, PS, PS), lambda c: (c, 0, 0))
    side = pl.BlockSpec((1, PS, PS), lambda c: (3 + c, 0, 0))
    return pl.pallas_call(
        rows_kernel,
        grid=(3,),
        out_shape=(whole,) * 4,
        in_specs=[near, side] * 4,
        out_specs=(pl.BlockSpec((1, EXT, PS), lambda c: (c, 0, 0)),) * 4,
        compiler_params=pltpu.CompilerParams(
            dimension_semantics=("arbitrary",), vmem_limit_bytes=56 << 20
        ),
        name="rows",
    )(down, down, from_above, from_above, up, up, from_below, from_below)


def waves(half, counts, offs, pieces, photons, probe_r, probe_i, coef, tables, width):
    edge = pltpu.HBM((6, width, PS), F32)
    inner = pltpu.HBM((6, max(EXT - 2 * width, 8), PS), F32)
    grid = pltpu.HBM((PS * LEAD, PS), F32)
    rows = jax.ShapeDtypeStruct((ROWS, MODES, 3 * PS), F32)
    square = pltpu.VMEM((PAIRS, 2 * PS, 2 * PS), F32)
    return pl.pallas_call(
        wave_kernel,
        grid=(PMAX // (2 * PAIRS),),
        out_shape=(edge, inner, edge, *[grid] * 3, rows, rows),
        in_specs=[
            SMEM,
            SMEM,
            SMEM,
            *[VMEM] * len(pieces),
            pl.BlockSpec((2 * PAIRS, PS, PS), lambda i: (i, 0, 0)),
            VMEM,
            VMEM,
            VMEM,
            VMEM,
        ],
        out_specs=(*[pl.BlockSpec(memory_space=pltpu.HBM)] * 6, VMEM, VMEM),
        scratch_shapes=[
            *[pltpu.VMEM((EXT, PS), F32)] * 6,
            pltpu.VMEM((2 * PAIRS, 2, PS, PS), F32),
            square,
            square,
            *[pltpu.VMEM((PS * LEAD, PS), F32)] * 3,
            pltpu.SemaphoreType.DMA((21,)),
            pltpu.VMEM((2, 2, EXT, PS), F32),
        ],
        compiler_params=pltpu.CompilerParams(
            dimension_semantics=("arbitrary",), vmem_limit_bytes=24 << 20
        ),
        name="waves",
    )(half, counts, offs, *pieces, photons, probe_r, probe_i, coef, tables)


def new_coefficients(cross_r, cross_i, powers, modes, coef):
    rows = pl.BlockSpec((CHUNK * LEAD, PS), lambda i: (i, 0))
    whole = pl.BlockSpec((MODES, PMAX), lambda i: (0, 0))
    return pl.pallas_call(
        coef_kernel,
        grid=(PS // CHUNK,),
        out_shape=jax.ShapeDtypeStruct((MODES, PMAX), F32),
        in_specs=[
            rows,
            rows,
            rows,
            pl.BlockSpec((CHUNK, MODES, 2 * PS), lambda i: (i, 0, 0)),
            whole,
        ],
        out_specs=whole,
        scratch_shapes=[pltpu.VMEM((PMAX, MODES), F32)] * 2,
        compiler_params=pltpu.CompilerParams(
            dimension_semantics=("arbitrary",), vmem_limit_bytes=56 << 20
        ),
        name="coefs",
    )(cross_r, cross_i, powers, modes, coef)


def update_row(got, mine):
    return pl.pallas_call(
        update_kernel,
        out_shape=(
            jax.ShapeDtypeStruct((MODES, 2 * PS), F32),
            jax.ShapeDtypeStruct((ROWS, MODES, 2 * PS), F32),
        ),
        in_specs=[VMEM, VMEM],
        out_specs=(VMEM, VMEM),
        compiler_params=pltpu.CompilerParams(vmem_limit_bytes=2 << 20),
        name="update",
    )(got, mine)


def shifted(x, move):
    rows, cols = lax.axis_size("row"), lax.axis_size("col")
    pairs = []
    for a in range(rows):
        for b in range(cols):
            c, d = a + move[0], b + move[1]
            if 0 <= c < rows and 0 <= d < cols:
                pairs.append((c * cols + d, a * cols + b))
    return lax.ppermute(x, ("row", "col"), pairs)


def by_side(low, high):
    lane = lax.broadcasted_iota(jnp.int32, low.shape, low.ndim - 1)
    return jnp.where(lane < MARGIN, low, high)


def extend(block, modes):
    right, left, modes = lax.optimization_barrier(
        (shifted(block, (0, 1)), shifted(block, (0, -1)), modes)
    )
    strip = jax.ShapeDtypeStruct((2, 2, MARGIN, PS), F32)
    both, first, last = pl.pallas_call(
        beside_kernel,
        out_shape=(jax.ShapeDtypeStruct((2, 2, PS, PS), F32), strip, strip),
        in_specs=[VMEM] * 3,
        out_specs=(VMEM,) * 3,
        compiler_params=pltpu.CompilerParams(vmem_limit_bytes=2 << 20),
        name="beside",
    )(block, right, left)
    return (shifted(last, (-1, 0)), both, shifted(first, (1, 0))), modes


def sum_columns(own, beside, from_left, from_right):
    own = own + by_side(from_left, from_right)
    beside = beside + by_side(from_right, from_left)
    return jnp.stack([own, beside], axis=1)


def inside_object():
    a, b = lax.axis_index("row"), lax.axis_index("col")
    place = a * TILE - MARGIN + lax.iota(jnp.int32, EXT)
    rows = (place >= 0) & (place < lax.axis_size("row") * TILE)
    lane = lax.iota(jnp.int32, PS)
    beside = ((lane < MARGIN) & (b < lax.axis_size("col") - 1)) | ((lane >= MARGIN) & (b > 0))
    cols = jnp.stack([jnp.ones_like(beside), beside])
    return rows[None, :, None] & cols[:, None, :]


def fold(up, mid, down):
    edges = jnp.concatenate([shifted(up, (-1, 0)), shifted(down, (1, 0))], axis=1)
    mid = mid + edges
    beside = mid[3:]
    return mid[:3] + by_side(shifted(beside, (0, -1)), shifted(beside, (0, 1)))


def shards(object_field, probe_modes, coefficients, offsets, counts, measured):
    tables = jnp.asarray(dft_constants())
    offs = offsets[0, 0].T
    photons = measured[0, 0]
    coef = coefficients[0, 0].T
    rows, cols = lax.axis_size("row"), lax.axis_size("col")
    core = lax.axis_index("row") % 2
    half = core.reshape(1)
    groups = [[a * cols + b for a in range(k, rows, 2) for b in range(cols)] for k in range(2)]
    mates = [(a, a ^ 1) for a in range(rows)]
    place = lax.axis_index("row") // 2 * cols + lax.axis_index("col")

    def exchange(x):
        return lax.all_to_all(x, ("row", "col"), 0, 0, axis_index_groups=groups, tiled=True)

    modes = probe_modes.transpose(2, 0, 1, 3).reshape(PS, MODES, 2 * PS)
    mine = lax.dynamic_index_in_dim(modes, core * ROWS + place, 0, keepdims=False)
    pieces, modes = extend(object_field, modes)
    ext = jnp.concatenate(pieces, axis=2)
    for iteration in range(ITERS):
        final = iteration == ITERS - 1
        if iteration == 0:
            probe_r, probe_i, tables = first_probes(
                jnp.zeros_like(half), counts, modes, coef, tables
            )
        else:
            probe_r, probe_i = mix_probes(half * ROWS, counts, near, coef)
            probe_r, probe_i = mix_probes((1 - half) * ROWS, counts, far, coef, probe_r, probe_i)
        up, mid, down, cross_r, cross_i, powers, kept, given = waves(
            half, counts, offs, pieces, photons, probe_r, probe_i, coef, tables, MARGIN if final else PS
        )
        if final:
            sent = kept + lax.ppermute(given, "row", mates)
            got = exchange(sent)
            coef = new_coefficients(cross_r, cross_i, powers, modes, coef)
            got, coef = lax.optimization_barrier((got, coef))
            mine, copies = update_row(got, mine)
            near = exchange(copies)
        else:
            from_above = shifted(up, (-1, 0))
            from_below = shifted(down, (1, 0))
            sent = kept + lax.ppermute(given, "row", mates)
            got = exchange(sent)
            own, beside, to_right, to_left = sum_rows(up, down, from_above, from_below)
            from_left = shifted(to_right, (0, -1))
            from_right = shifted(to_left, (0, 1))
            mine, copies = update_row(got, mine)
            copies, cross_r = lax.optimization_barrier((copies, cross_r))
            coef = new_coefficients(cross_r, cross_i, powers, modes, coef)
            near = exchange(copies)
        far = lax.ppermute(near, "row", mates)
        modes = jnp.where(
            core == 0, jnp.concatenate([near, far]), jnp.concatenate([far, near])
        )
        if final:
            total = fold(up, mid, down)
            object_field = ext[:, 0, MARGIN:-MARGIN] + total[0:2] / (total[2:3] + 1.0)
        else:
            total = sum_columns(own, beside, from_left, from_right)
            step = total[0:2] / (total[2:3] + 1.0)
            ext = ext + jnp.where(inside_object()[None], step, 0.0)
            pieces = (ext,)
    probe_modes = modes.reshape(PS, MODES, 2, PS).transpose(1, 2, 0, 3)
    return (object_field, probe_modes, coef.T[None, None])


def solution(mesh):
    placed = (
        P(None, "row", "col"),
        P(),
        P("row", "col", None, None),
        P("row", "col", None, None),
        P("row", "col"),
        P("row", "col", None, None, None),
    )
    return jax.shard_map(
        shards,
        mesh=mesh,
        in_specs=placed,
        out_specs=(P(None, "row", "col"), P(), P("row", "col", None, None)),
        check_vma=False,
    )
```

```python
import math

import jax
import jax.numpy as jnp
import numpy as np
from jax import lax
from jax.experimental import pallas as pl
from jax.experimental.pallas import tpu as pltpu
from jax.sharding import PartitionSpec as P

PS = 128
MODES = 8
TILE = 128
PMAX = 32
ITERS = 2
EXT = TILE + PS
F32 = jnp.float32
BF16 = jnp.bfloat16
PAIRS = 4
LEAD = 33
ROWS = PS // 2
MARGIN = PS // 2


def split(x):
    hi = x.astype(BF16)
    lo = (x - hi.astype(F32)).astype(BF16)
    return hi, lo


def triple(x, axis):
    hi, lo = split(x)
    return jnp.concatenate([hi, lo, hi], axis=axis)


def dft_constants():
    ramp = np.arange(PS)
    angles = (ramp[:, None] * ramp[None, :] % PS) * (2.0 * math.pi / PS)
    cos = np.cos(angles) / math.sqrt(PS)
    sin = -np.sin(angles) / math.sqrt(PS)
    parts = []
    for table in (np.block([[cos, sin], [-sin, cos]]), np.block([[cos, -sin], [sin, cos]])):
        table = table.astype(np.float32)
        hi = table.astype(jnp.bfloat16)
        parts += [hi, (table - hi.astype(np.float32)).astype(jnp.bfloat16)]
    return np.stack(parts)


def dot(a, b):
    return jnp.dot(a, b, preferred_element_type=F32)


def live_only(coef, counts):
    slot = lax.broadcasted_iota(jnp.int32, coef.shape, 1)
    return jnp.where(slot < counts[0, 0], coef[...], 0.0)


def probe_kernel(base, counts, modes, coef, *refs):
    probe_r, probe_i = refs[-2:]
    left = triple(live_only(coef, counts).T, 1)

    def rows(y, _):
        m = modes[y]
        h = m.astype(BF16).astype(F32)
        right = jnp.concatenate([h, h, m - h], axis=0).astype(BF16)
        out = dot(left, right)
        start = (base[0] + y) * LEAD
        probe_r[pl.ds(start, PMAX), :] = out[:, :PS]
        probe_i[pl.ds(start, PMAX), :] = out[:, PS:]
        return 0

    lax.fori_loop(0, modes.shape[0], rows, 0, unroll=64)


def first_probe_kernel(base, counts, modes, coef, tables, probe_r, probe_i, kept, sem):
    copy = pltpu.make_async_copy(tables, kept, sem)
    copy.start()
    probe_kernel(base, counts, modes, coef, probe_r, probe_i)
    copy.wait()


def wave_kernel(half, counts, offs, *refs):
    (
        photons, probe_r, probe_i, coef, tables,
        up, mid, down, out_r, out_i, out_p, near, far,
        acc_rl, acc_rh, acc_il, acc_ih, acc_pl, acc_ph,
        patches, wave, field, cross_r, cross_i, power, sems, ext,
    ) = refs[-27:]
    pieces = refs[:-27]
    step = pl.program_id(0)
    lane = lax.broadcasted_iota(jnp.int32, (PS, PS), 1)
    if len(pieces) == 1:
        ext = pieces[0]
    sums = ((acc_rl, acc_rh), (acc_il, acc_ih), (acc_pl, acc_ph))

    @pl.when(step == 0)
    def _():
        if len(pieces) == 3:
            row = 0
            for piece in pieces:
                ext[:, :, row : row + piece.shape[2]] = piece[...]
                row += piece.shape[2]
        for low, high in sums:
            low[...] = jnp.zeros_like(low)
            high[...] = jnp.zeros_like(high)

    def own_lanes(left):
        return (lane < left + MARGIN) & (lane >= left - MARGIN)

    def regroup(x):
        top = jnp.concatenate([x[:PS, :PS], x[PS:, :PS]], axis=1)
        low = jnp.concatenate([x[:PS, PS:], x[PS:, PS:]], axis=1)
        return jnp.concatenate([top, low], axis=0)

    def take(j, q):
        p = 2 * PAIRS * step + 2 * j + q
        return (
            probe_r[pl.ds(p, PS, stride=LEAD), :],
            probe_i[pl.ds(p, PS, stride=LEAD), :],
            patches[2 * j + q, 0],
            patches[2 * j + q, 1],
        )

    def cut(j, q):
        p = 2 * PAIRS * step + 2 * j + q
        top = offs[0, p]
        left = offs[1, p]
        turn = (PS + MARGIN - left) & (PS - 1)
        inside = own_lanes(left)
        total = None
        for c in range(2):
            patch = jnp.where(
                inside, ext[c, 0, pl.ds(top, PS), :], ext[c, 1, pl.ds(top, PS), :]
            )
            patch = pltpu.roll(patch, turn, 1)
            patches[2 * j + q, c] = patch
            total = patch * patch if total is None else total + patch * patch
        power[pl.ds(p, PS, stride=LEAD), :] = total

    def start(j):
        for q in range(2):
            cut(j, q)
            pr, pi, obj_r, obj_i = take(j, q)
            rows = slice(q * PS, (q + 1) * PS)
            wave[j, rows, :PS] = pr * obj_r - pi * obj_i
            wave[j, rows, PS:] = pr * obj_i + pi * obj_r

    def correct(j, there):
        count = jnp.concatenate([photons[2 * j], photons[2 * j + 1]], axis=1).astype(F32)
        far_r = there[:PS]
        far_i = there[PS:]
        power_there = jnp.maximum(far_r * far_r + far_i * far_i, 0.25)
        scale = count * lax.rsqrt(jnp.maximum(count * power_there, 0.0625)) * 0.03125
        return jnp.concatenate([far_r * scale, far_i * scale], axis=0)

    def finish(j):
        for q in range(2):
            p = 2 * PAIRS * step + 2 * j + q
            top = offs[0, p]
            left = offs[1, p]
            turn = (left + MARGIN) & (PS - 1)
            inside = own_lanes(left)
            rows = slice(q * PS, (q + 1) * PS)
            diff_r = field[j, rows, :PS]
            diff_i = field[j, rows, PS:]
            pr, pi, obj_r, obj_i = take(j, q)
            cross_r[pl.ds(p, PS, stride=LEAD), :] = obj_r * diff_r + obj_i * diff_i
            cross_i[pl.ds(p, PS, stride=LEAD), :] = obj_r * diff_i - obj_i * diff_r
            pieces = (
                pr * diff_r + pi * diff_i,
                pr * diff_i - pi * diff_r,
                pr * pr + pi * pi,
            )
            for (low, high), piece in zip(sums, pieces):
                turned = pltpu.roll(piece, turn, 1)
                near = jnp.where(inside, turned, 0.0)
                low[pl.ds(top, PS), :] += near
                high[pl.ds(top, PS), :] += turned - near

    def table(i, axis):
        hi = tables[2 * i]
        return jnp.concatenate([hi, hi, tables[2 * i + 1]], axis=axis)

    pairs = range(PAIRS)
    for j in pairs:
        start(j)
    size = 2 * PS
    x = []
    for j in range(0, PAIRS, 2):
        out = dot(triple(wave[j : j + 2].reshape(2 * size, size), 1), table(0, 0))
        x += [out[:size], out[size:]]
    x = [dot(table(1, 1), triple(regroup(x[j]), 0)) for j in pairs]
    x = [correct(j, x[j]) for j in pairs]
    x = [dot(table(0, 1), triple(x[j], 0)) for j in pairs]
    for j in range(0, PAIRS, 2):
        both = jnp.concatenate([regroup(x[j]), regroup(x[j + 1])], axis=0)
        out = dot(triple(both, 1), table(1, 0))
        field[j] = out[:size] - wave[j]
        field[j + 1] = out[size:] - wave[j + 1]
    for j in pairs:
        finish(j)

    @pl.when(step == PMAX // (2 * PAIRS) - 1)
    def _():
        width = up.shape[1]
        moves = [(cross_r, out_r), (cross_i, out_i), (power, out_p)]
        for i, piece in enumerate((acc_rl, acc_il, acc_pl, acc_rh, acc_ih, acc_ph)):
            moves.append((piece.at[:width], down.at[i]))
            moves.append((piece.at[EXT - width:], up.at[i]))
            if width < PS:
                moves.append((piece.at[width : EXT - width], mid.at[i]))
        copies = [
            pltpu.make_async_copy(source, target, sems.at[i])
            for i, (source, target) in enumerate(moves)
        ]
        for copy in copies:
            copy.start()

        def stacked(x):
            hi, lo = split(x)
            zero = jnp.zeros_like(hi)
            return jnp.concatenate(
                [jnp.concatenate([hi, hi], axis=1), jnp.concatenate([lo, zero], axis=1)], axis=0
            )

        used = live_only(coef, counts)
        left = stacked(used)
        left_square = stacked(used * used)
        for target, base in ((near, half[0] * ROWS), (far, (1 - half[0]) * ROWS)):

            def rows(y, _):
                begin = (base + y) * LEAD
                pair = jnp.concatenate(
                    [cross_r[pl.ds(begin, PMAX), :], cross_i[pl.ds(begin, PMAX), :]], axis=1
                )
                h, l = split(pair)
                out = dot(left, jnp.concatenate([h, l], axis=0))
                target[y, :, : 2 * PS] = out[:MODES] + out[MODES:]
                h, l = split(power[pl.ds(begin, PMAX), :])
                out = dot(left_square, jnp.concatenate([h, l], axis=0))
                target[y, :, 2 * PS:] = out[:MODES] + out[MODES:]
                return 0

            lax.fori_loop(0, ROWS, rows, 0, unroll=16)
        for copy in copies:
            copy.wait()


CHUNK = 64


def coef_kernel(cross_r, cross_i, powers, modes, coef, out, num, den):
    step = pl.program_id(0)

    @pl.when(step == 0)
    def _():
        num[...] = jnp.zeros_like(num)
        den[...] = jnp.zeros_like(den)

    dims = (((1,), (1,)), ((), ()))

    def wide_dot(a, b):
        return lax.dot_general(a, b, dims, preferred_element_type=F32)

    top = jnp.zeros((PMAX, MODES), F32)
    low = jnp.zeros((PMAX, MODES), F32)
    for y in range(CHUNK):
        rows = slice(y * LEAD, y * LEAD + PMAX)
        cross = jnp.concatenate([cross_r[rows, :], cross_i[rows, :]], axis=1)
        m = modes[y]
        power = m[:, :PS] * m[:, :PS] + m[:, PS:] * m[:, PS:]
        h, l = split(m)
        top += wide_dot(triple(cross, 1), jnp.concatenate([h, h, l], axis=1))
        h, l = split(power)
        low += wide_dot(triple(powers[rows, :], 1), jnp.concatenate([h, h, l], axis=1))
    num[...] += top
    den[...] += low

    @pl.when(step == PS // CHUNK - 1)
    def _():
        out[...] = coef[...] + (num[...] / (den[...] + 1.0)).T


def update_kernel(got, mine, new, copies):
    total = jnp.sum(got[...], axis=0)
    power = total[:, 2 * PS:] + 1.0
    row = mine[...] + total[:, : 2 * PS] / jnp.concatenate([power, power], axis=1)
    new[...] = row
    copies[...] = jnp.broadcast_to(row[None], copies.shape)


def beside_kernel(block, right, left, both, first, last):
    lane = lax.broadcasted_iota(jnp.int32, (PS, PS), 1)
    for c in range(2):
        beside = jnp.where(lane < MARGIN, right[c], left[c])
        for i, plane in ((0, block[c]), (1, beside)):
            both[c, i] = plane
            first[c, i] = plane[:MARGIN]
            last[c, i] = plane[MARGIN:]


def rows_kernel(up, down, from_above, from_below, full, to_right, to_left):
    lane = lax.broadcasted_iota(jnp.int32, (PS, PS), 1)
    for c in range(3):
        for rows, own, other in ((slice(0, PS), down, from_above), (slice(PS, EXT), up, from_below)):
            centre = own[c] + other[c]
            beside = own[3 + c] + other[3 + c]
            full[c, rows] = centre
            full[3 + c, rows] = beside
            to_right[c, rows] = jnp.where(lane < MARGIN, beside, centre)
            to_left[c, rows] = jnp.where(lane < MARGIN, centre, beside)


SMEM = pl.BlockSpec(memory_space=pltpu.SMEM)
VMEM = pl.BlockSpec(memory_space=pltpu.VMEM)


def mix_probes(base, counts, modes, coef, *before):
    grid = jax.ShapeDtypeStruct((PS * LEAD, PS), F32)
    return pl.pallas_call(
        probe_kernel,
        out_shape=(grid, grid),
        in_specs=[SMEM, SMEM, VMEM, VMEM, *[VMEM] * len(before)],
        out_specs=(VMEM, VMEM),
        input_output_aliases={4: 0, 5: 1} if before else {},
        compiler_params=pltpu.CompilerParams(vmem_limit_bytes=2 << 20),
        name="probes",
    )(base, counts, modes, coef, *before)


def first_probes(base, counts, modes, coef, tables):
    grid = jax.ShapeDtypeStruct((PS * LEAD, PS), F32)
    return pl.pallas_call(
        first_probe_kernel,
        out_shape=(grid, grid, jax.ShapeDtypeStruct(tables.shape, tables.dtype)),
        in_specs=[SMEM, SMEM, VMEM, VMEM, pl.BlockSpec(memory_space=pltpu.HBM)],
        out_specs=(VMEM, VMEM, VMEM),
        scratch_shapes=[pltpu.SemaphoreType.DMA],
        compiler_params=pltpu.CompilerParams(vmem_limit_bytes=2 << 20),
        name="probes",
    )(base, counts, modes, coef, tables)


def sum_rows(up, down, from_above, from_below):
    side = jax.ShapeDtypeStruct((3, EXT, PS), F32)
    return pl.pallas_call(
        rows_kernel,
        out_shape=(jax.ShapeDtypeStruct((6, EXT, PS), F32), side, side),
        in_specs=[VMEM] * 4,
        out_specs=(VMEM,) * 3,
        compiler_params=pltpu.CompilerParams(vmem_limit_bytes=2 << 20),
        name="rows",
    )(up, down, from_above, from_below)


def waves(half, counts, offs, pieces, photons, probe_r, probe_i, coef, tables, width):
    edge = pltpu.HBM((6, width, PS), F32)
    inner = pltpu.HBM((6, max(EXT - 2 * width, 8), PS), F32)
    grid = pltpu.HBM((PS * LEAD, PS), F32)
    rows = jax.ShapeDtypeStruct((ROWS, MODES, 3 * PS), F32)
    square = pltpu.VMEM((PAIRS, 2 * PS, 2 * PS), F32)
    return pl.pallas_call(
        wave_kernel,
        grid=(PMAX // (2 * PAIRS),),
        out_shape=(edge, inner, edge, *[grid] * 3, rows, rows),
        in_specs=[
            SMEM,
            SMEM,
            SMEM,
            *[VMEM] * len(pieces),
            pl.BlockSpec((2 * PAIRS, PS, PS), lambda i: (i, 0, 0)),
            VMEM,
            VMEM,
            VMEM,
            VMEM,
        ],
        out_specs=(*[pl.BlockSpec(memory_space=pltpu.HBM)] * 6, VMEM, VMEM),
        scratch_shapes=[
            *[pltpu.VMEM((EXT, PS), F32)] * 6,
            pltpu.VMEM((2 * PAIRS, 2, PS, PS), F32),
            square,
            square,
            *[pltpu.VMEM((PS * LEAD, PS), F32)] * 3,
            pltpu.SemaphoreType.DMA((21,)),
            pltpu.VMEM((2, 2, EXT, PS), F32),
        ],
        compiler_params=pltpu.CompilerParams(
            dimension_semantics=("arbitrary",), vmem_limit_bytes=24 << 20
        ),
        name="waves",
    )(half, counts, offs, *pieces, photons, probe_r, probe_i, coef, tables)


def new_coefficients(cross_r, cross_i, powers, modes, coef):
    rows = pl.BlockSpec((CHUNK * LEAD, PS), lambda i: (i, 0))
    whole = pl.BlockSpec((MODES, PMAX), lambda i: (0, 0))
    return pl.pallas_call(
        coef_kernel,
        grid=(PS // CHUNK,),
        out_shape=jax.ShapeDtypeStruct((MODES, PMAX), F32),
        in_specs=[
            rows,
            rows,
            rows,
            pl.BlockSpec((CHUNK, MODES, 2 * PS), lambda i: (i, 0, 0)),
            whole,
        ],
        out_specs=whole,
        scratch_shapes=[pltpu.VMEM((PMAX, MODES), F32)] * 2,
        compiler_params=pltpu.CompilerParams(
            dimension_semantics=("arbitrary",), vmem_limit_bytes=56 << 20
        ),
        name="coefs",
    )(cross_r, cross_i, powers, modes, coef)


def update_row(got, mine):
    return pl.pallas_call(
        update_kernel,
        out_shape=(
            jax.ShapeDtypeStruct((MODES, 2 * PS), F32),
            jax.ShapeDtypeStruct((ROWS, MODES, 2 * PS), F32),
        ),
        in_specs=[VMEM, VMEM],
        out_specs=(VMEM, VMEM),
        compiler_params=pltpu.CompilerParams(vmem_limit_bytes=2 << 20),
        name="update",
    )(got, mine)


def shifted(x, move):
    rows, cols = lax.axis_size("row"), lax.axis_size("col")
    pairs = []
    for a in range(rows):
        for b in range(cols):
            c, d = a + move[0], b + move[1]
            if 0 <= c < rows and 0 <= d < cols:
                pairs.append((c * cols + d, a * cols + b))
    return lax.ppermute(x, ("row", "col"), pairs)


def by_side(low, high):
    lane = lax.broadcasted_iota(jnp.int32, low.shape, low.ndim - 1)
    return jnp.where(lane < MARGIN, low, high)


def extend(block, modes):
    right, left, modes = lax.optimization_barrier(
        (shifted(block, (0, 1)), shifted(block, (0, -1)), modes)
    )
    strip = jax.ShapeDtypeStruct((2, 2, MARGIN, PS), F32)
    both, first, last = pl.pallas_call(
        beside_kernel,
        out_shape=(jax.ShapeDtypeStruct((2, 2, PS, PS), F32), strip, strip),
        in_specs=[VMEM] * 3,
        out_specs=(VMEM,) * 3,
        compiler_params=pltpu.CompilerParams(vmem_limit_bytes=2 << 20),
        name="beside",
    )(block, right, left)
    return (shifted(last, (-1, 0)), both, shifted(first, (1, 0))), modes


def sum_columns(full, from_left, from_right):
    own = full[:3] + by_side(from_left, from_right)
    beside = full[3:] + by_side(from_right, from_left)
    return jnp.stack([own, beside], axis=1)


def inside_object():
    a, b = lax.axis_index("row"), lax.axis_index("col")
    place = a * TILE - MARGIN + lax.iota(jnp.int32, EXT)
    rows = (place >= 0) & (place < lax.axis_size("row") * TILE)
    lane = lax.iota(jnp.int32, PS)
    beside = ((lane < MARGIN) & (b < lax.axis_size("col") - 1)) | ((lane >= MARGIN) & (b > 0))
    cols = jnp.stack([jnp.ones_like(beside), beside])
    return rows[None, :, None] & cols[:, None, :]


def fold(up, mid, down):
    edges = jnp.concatenate([shifted(up, (-1, 0)), shifted(down, (1, 0))], axis=1)
    mid = mid + edges
    beside = mid[3:]
    return mid[:3] + by_side(shifted(beside, (0, -1)), shifted(beside, (0, 1)))


def shards(object_field, probe_modes, coefficients, offsets, counts, measured):
    tables = jnp.asarray(dft_constants())
    offs = offsets[0, 0].T
    photons = measured[0, 0]
    coef = coefficients[0, 0].T
    rows, cols = lax.axis_size("row"), lax.axis_size("col")
    core = lax.axis_index("row") % 2
    half = core.reshape(1)
    groups = [[a * cols + b for a in range(k, rows, 2) for b in range(cols)] for k in range(2)]
    mates = [(a, a ^ 1) for a in range(rows)]
    place = lax.axis_index("row") // 2 * cols + lax.axis_index("col")

    def exchange(x):
        return lax.all_to_all(x, ("row", "col"), 0, 0, axis_index_groups=groups, tiled=True)

    modes = probe_modes.transpose(2, 0, 1, 3).reshape(PS, MODES, 2 * PS)
    mine = lax.dynamic_index_in_dim(modes, core * ROWS + place, 0, keepdims=False)
    pieces, modes = extend(object_field, modes)
    ext = jnp.concatenate(pieces, axis=2)
    for iteration in range(ITERS):
        final = iteration == ITERS - 1
        if iteration == 0:
            probe_r, probe_i, tables = first_probes(
                jnp.zeros_like(half), counts, modes, coef, tables
            )
        else:
            probe_r, probe_i = mix_probes(half * ROWS, counts, near, coef)
            probe_r, probe_i = mix_probes((1 - half) * ROWS, counts, far, coef, probe_r, probe_i)
        up, mid, down, cross_r, cross_i, powers, kept, given = waves(
            half, counts, offs, pieces, photons, probe_r, probe_i, coef, tables, MARGIN if final else PS
        )
        if final:
            sent = kept + lax.ppermute(given, "row", mates)
            got = exchange(sent)
            coef = new_coefficients(cross_r, cross_i, powers, modes, coef)
            got, coef = lax.optimization_barrier((got, coef))
            mine, copies = update_row(got, mine)
            near = exchange(copies)
        else:
            from_above = shifted(up, (-1, 0))
            from_below = shifted(down, (1, 0))
            sent = kept + lax.ppermute(given, "row", mates)
            got = exchange(sent)
            full, to_right, to_left = sum_rows(up, down, from_above, from_below)
            from_left = shifted(to_right, (0, -1))
            from_right = shifted(to_left, (0, 1))
            mine, copies = update_row(got, mine)
            copies, cross_r = lax.optimization_barrier((copies, cross_r))
            coef = new_coefficients(cross_r, cross_i, powers, modes, coef)
            near = exchange(copies)
        far = lax.ppermute(near, "row", mates)
        modes = jnp.where(
            core == 0, jnp.concatenate([near, far]), jnp.concatenate([far, near])
        )
        if final:
            total = fold(up, mid, down)
            object_field = ext[:, 0, MARGIN:-MARGIN] + total[0:2] / (total[2:3] + 1.0)
        else:
            total = sum_columns(full, from_left, from_right)
            step = total[0:2] / (total[2:3] + 1.0)
            ext = ext + jnp.where(inside_object()[None], step, 0.0)
            pieces = (ext,)
    probe_modes = modes.reshape(PS, MODES, 2, PS).transpose(1, 2, 0, 3)
    return (object_field, probe_modes, coef.T[None, None])


def solution(mesh):
    placed = (
        P(None, "row", "col"),
        P(),
        P("row", "col", None, None),
        P("row", "col", None, None),
        P("row", "col"),
        P("row", "col", None, None, None),
    )
    return jax.shard_map(
        shards,
        mesh=mesh,
        in_specs=placed,
        out_specs=(P(None, "row", "col"), P(), P("row", "col", None, None)),
        check_vma=False,
    )
```
